128 devices in a mesh: px: 8 (over x, core), py: 16 (over z, y).
Axes of the slice: x: 4, y: 4, z: 4, core: 2. Of those that a mesh axis runs over, the one named last changes fastest.
Arguments:
- fields: float32 [4, 35, 589824], P(None, None, ('px', 'py')), may hold values from -6 to 6
- residue: float32 [4, 35, 589824], P(None, None, ('px', 'py')), may hold values from -4 to 4
- geometry: float32 [9, 589824], P(None, ('px', 'py')), may hold values from -4 to 4
- normals: float32 [3, 4, 589824], P(None, None, ('px', 'py')), as said below
- face_scale: float32 [4, 589824], P(None, ('px', 'py')), may hold values from 0.5 to 4
- neighbours: int32 [4, 589824], P(None, ('px', 'py')), may hold values from -1 to 19199, as said below
- send_faces: int32 [8, 12288], P(None, ('px', 'py')), may hold values from 0 to 14591, as said below
- live_counts: int32 [128], P(('px', 'py')), may hold values from 768 to 4608, as said below
- sample_ids: int32 [25600], P(('px', 'py')), may hold values from 0 to 25599, each once
- sample_elems: int32 [25600], P(('px', 'py')), may hold values from 0 to 4607, as said below
- sample_coords: float32 [3, 25600], P(None, ('px', 'py')), as said below
Outputs:
- fields_next: float32 [4, 35, 589824], P(None, None, ('px', 'py'))
- residue_next: float32 [4, 35, 589824], P(None, None, ('px', 'py'))
- coefficients: float32 [25, 512], P(None, ('px', 'py'))
The draws below stay inside these ranges and needn't reach their ends.
Inputs may be any that keep to these rules, and one draw needn't show every extreme that they name: `live_counts`: one partition holds exactly 4608 live slots, each other one between 768 and 2304. `neighbours`: codes of live slots name live face blocks. Slot d * 96 + j, for d below 8, has exactly one face coded 4 * 4608 + d * 96 + j, or coded -1 where that neighbour lies off the grid; no other face has a code at or above 18432. Matched faces list their nodes in the same order. send_faces[d, P * 96 + j] is the face block of partition P's slot d * 96 + j that faces neighbour d. `sample_elems`: each names a live slot of the partition holding the sample slot. `sample_coords`: the point lies inside the reference tetrahedron. `normals`: unit vectors.
All inputs are finite; a program needn't handle non-finite values.
Results may differ from the reference program's by a relative error of at most 0.0003.
Values sent between devices are 32-bit elements; how exact they have to be, the bound alone decides.
No kernel may reach another device: no remote copies, remote signals or barrier semaphores. Data moves between devices by JAX's collectives and lax.ppermute only.
A program may use at most 128 MiB of HBM per device.

```python
import math
import jax
import jax.numpy as jnp
import numpy as np
from jax import lax

ELEM_CAP = 4608
BOUND_FACES = 96
NODES = 35
QPTS = 50
ELEMENTS = 589824
RECEIVERS = 512
SAMP_DEV = 200
SAMPLES = 25600
N_PX = 8
N_PY = 16


def partition_counts(key):
    devices = N_PX * N_PY
    stream = jax.random.fold_in(key, 11)
    others = jax.random.randint(stream, (devices,), ELEM_CAP // 6, ELEM_CAP // 2 + 1)
    heavy = jax.random.randint(jax.random.fold_in(stream, 1), (), 0, devices)
    return jnp.where(jnp.arange(devices) == heavy, ELEM_CAP, others).astype(jnp.int32)


def remote_faces(key):
    devices = N_PX * N_PY
    return jax.random.randint(jax.random.fold_in(key, 12), (devices, 8 * BOUND_FACES), 0, 4).astype(jnp.int32)


def draw_live_counts(key, part):
    return partition_counts(key)


def draw_neighbours(key, part):
    devices = N_PX * N_PY
    total = ELEM_CAP * devices
    counts = partition_counts(key)
    faces = remote_faces(key)
    column = jnp.arange(total, dtype=jnp.int32)
    device = column // ELEM_CAP
    slot_id = column % ELEM_CAP
    live_here = counts[device]
    pick_face = jax.random.randint(jax.random.fold_in(key, 21), (4, total), 0, 4)
    pick_elem = jax.random.randint(jax.random.fold_in(key, 22), (4, total), 0, 1 << 30) % live_here[None, :]
    local_code = pick_face * ELEM_CAP + pick_elem
    is_wall = jax.random.randint(jax.random.fold_in(key, 23), (4, total), 0, 8) == 0
    code = jnp.where(is_wall, -1, local_code)
    reach = 8 * BOUND_FACES
    kept = jnp.minimum(slot_id, reach - 1)
    chosen = faces[device, kept]
    heading = kept // BOUND_FACES
    flat_dir = heading + (heading >= 4).astype(jnp.int32)
    row_pos = device // N_PY + flat_dir // 3 - 1
    col_pos = device % N_PY + flat_dir % 3 - 1
    inside = (row_pos >= 0) & (row_pos < N_PX) & (col_pos >= 0) & (col_pos < N_PY)
    remote_code = jnp.where(inside, 4 * ELEM_CAP + kept, -1)
    is_remote = (slot_id < reach)[None, :] & (jnp.arange(4)[:, None] == chosen[None, :])
    return jnp.where(is_remote, remote_code[None, :], code).astype(jnp.int32)


def draw_send_faces(key, part):
    devices = N_PX * N_PY
    faces = remote_faces(key)
    element = jnp.arange(8 * BOUND_FACES, dtype=jnp.int32)
    blocks = (faces * ELEM_CAP + element[None, :]).reshape(devices, 8, BOUND_FACES)
    return jnp.transpose(blocks, (1, 0, 2)).reshape(8, devices * BOUND_FACES).astype(jnp.int32)


def draw_sample_elems(key, part):
    devices = N_PX * N_PY
    counts = partition_counts(key)
    holder = jnp.arange(SAMP_DEV * devices, dtype=jnp.int32) // SAMP_DEV
    raw = jax.random.randint(jax.random.fold_in(key, 31), (SAMP_DEV * devices,), 0, 1 << 30)
    return (raw % counts[holder]).astype(jnp.int32)


def draw_sample_coords(key, part):
    devices = N_PX * N_PY
    weights = jax.random.uniform(jax.random.fold_in(key, 41), (4, SAMP_DEV * devices), jnp.float32, 0.02, 1.0)
    bary = weights / jnp.sum(weights, axis=0, keepdims=True)
    return bary[1:4].astype(jnp.float32)


def draw_normals(key, part):
    devices = N_PX * N_PY
    height = jax.random.uniform(jax.random.fold_in(key, 51), (4, ELEM_CAP * devices), jnp.float32, -1.0, 1.0)
    turn = jax.random.uniform(jax.random.fold_in(key, 52), (4, ELEM_CAP * devices), jnp.float32, -3.14159265, 3.14159265)
    radial = jnp.sqrt(jnp.maximum(1.0 - height * height, 0.0))
    return jnp.stack([radial * jnp.cos(turn), radial * jnp.sin(turn), height]).astype(jnp.float32)


def levels(key, dims, cuts, least, largest):
    loudness, own = 1.0, jax.random.fold_in(key, 6)
    for axis_at, shards_of in cuts:
        heights = jnp.exp(jax.random.uniform(jax.random.fold_in(own, axis_at), (shards_of,), jnp.float32, least / len(cuts), largest / len(cuts)))
        loudness = loudness * jnp.repeat(heights, dims[axis_at] // shards_of).reshape([-1 if axis == axis_at else 1 for axis in range(len(dims))])
    return loudness


def scatter_about(own_key, dims, spread, limit, pieces=(), kind=jnp.bfloat16):
    values = spread * jax.random.normal(own_key, dims, jnp.float32)
    if pieces:
        values = values * levels(own_key, dims, pieces, -0.22, 0.18)
    return jnp.clip(values, -limit, limit).astype(kind)


def setup_inputs(seed: int = 0) -> dict:
    key_of = jax.random.split(jax.random.key(seed), 12)
    return {
        "fields": scatter_about(key_of[0], (4, NODES, ELEMENTS), 1.0, 6.0, ((2, 128),), jnp.float32),
        "residue": scatter_about(key_of[1], (4, NODES, ELEMENTS), 0.5, 4.0, ((2, 128),), jnp.float32),
        "geometry": scatter_about(key_of[2], (9, ELEMENTS), 1.0, 4.0, ((1, 128),), jnp.float32),
        "normals": draw_normals(jax.random.fold_in(key_of[11], 71), 0),
        "face_scale": jnp.clip(jnp.exp(math.log(4.0) - 2.0794415 * jax.random.uniform(key_of[4], (4, ELEMENTS), jnp.float32) ** levels(key_of[4], (4, ELEMENTS), ((1, 128),), -0.2, 0.2)), 0.5, 4.0),
        "neighbours": draw_neighbours(jax.random.fold_in(key_of[11], 71), 0),
        "send_faces": draw_send_faces(jax.random.fold_in(key_of[11], 71), 0),
        "live_counts": draw_live_counts(jax.random.fold_in(key_of[11], 71), 0),
        "sample_ids": jax.random.permutation(key_of[8], SAMPLES).astype(jnp.int32),
        "sample_elems": draw_sample_elems(jax.random.fold_in(key_of[11], 71), 0),
        "sample_coords": draw_sample_coords(jax.random.fold_in(key_of[11], 71), 0),
    }


highest = lax.Precision.HIGHEST
section_decay = -567301805773.0 / 1357537059087.0
section_gain = 5161836677717.0 / 13612068292357.0
time_step = 0.01

def exponent_table():
    listing = []
    for degree in range(5):
        for third in range(degree + 1):
            for second in range(degree + 1 - third):
                listing.append((degree - second - third, second, third))
    return np.array(listing)

def factorials(values):
    lookup = np.array([float(math.factorial(level)) for level in range(24)])
    return lookup[values]

def eliminate(matrix, right_hand):
    order_size = matrix.shape[0]
    work = np.concatenate([matrix, right_hand], axis=1).astype(float)
    for pivot_col in range(order_size):
        best = max(range(pivot_col, order_size), key=lambda row_id: abs(work[row_id, pivot_col]))
        work[[pivot_col, best]] = work[[best, pivot_col]]
        work[pivot_col] = work[pivot_col] / work[pivot_col, pivot_col]
        for row_id in range(order_size):
            if row_id != pivot_col:
                work[row_id] = work[row_id] - work[row_id, pivot_col] * work[pivot_col]
    return work[:, order_size:]

def element_tables():
    powers = exponent_table()
    points = powers / 4.0
    vander = np.prod(points[:, None, :] ** powers[None, :, :], axis=2)
    inverse = eliminate(vander, np.eye(35))
    derivs = []
    for axis_id in range(3):
        lowered = np.maximum(powers - (np.arange(3) == axis_id)[None, :], 0)
        slope_table = powers[None, :, axis_id] * np.prod(points[:, None, :] ** lowered[None, :, :], axis=2)
        derivs.append(slope_table @ inverse)
    summed = powers[:, None, :] + powers[None, :, :]
    exp_r = summed[..., 0]
    exp_s = summed[..., 1]
    exp_t = summed[..., 2]
    volume = factorials(exp_r) * factorials(exp_s) * factorials(exp_t) / factorials(exp_r + exp_s + exp_t + 3)
    mass_matrix = inverse.T @ volume @ inverse
    face_grams = [np.where(exp_t == 0, factorials(exp_r) * factorials(exp_s) / factorials(exp_r + exp_s + 2), 0.0), np.where(exp_s == 0, factorials(exp_r) * factorials(exp_t) / factorials(exp_r + exp_t + 2), 0.0), factorials(exp_r) * factorials(exp_s) * factorials(exp_t) / factorials(exp_r + exp_s + exp_t + 2), np.where(exp_r == 0, factorials(exp_s) * factorials(exp_t) / factorials(exp_s + exp_t + 2), 0.0)]
    listed = [tuple((int(entry) for entry in powers[node_id])) for node_id in range(35)]
    face_nodes = np.array([[node_id for node_id in range(35) if listed[node_id][2] == 0], [node_id for node_id in range(35) if listed[node_id][1] == 0], [node_id for node_id in range(35) if sum(listed[node_id]) == 4], [node_id for node_id in range(35) if listed[node_id][0] == 0]])
    surface = np.zeros((35, 60))
    for face_id in range(4):
        face_mass = inverse.T @ face_grams[face_id] @ inverse
        for node_id in range(15):
            surface[:, 4 * node_id + face_id] = face_mass[:, face_nodes[face_id, node_id]]
    lifting = eliminate(mass_matrix, surface)
    return (np.stack(derivs), lifting, face_nodes, inverse, powers)

def associated(degree, order, cosine, sine):
    current = cosine * 0.0 + 1.0
    for step_id in range(1, order + 1):
        current = -(2 * step_id - 1) * sine * current
    if degree == order:
        return current
    following = cosine * (2 * order + 1) * current
    for level in range(order + 2, degree + 1):
        current, following = (following, ((2 * level - 1) * cosine * following - (level + order - 1) * current) / (level - order))
    return following

def harmonic_table():
    inner_node = math.sqrt(5.0 - 2.0 * math.sqrt(10.0 / 7.0)) / 3.0
    outer_node = math.sqrt(5.0 + 2.0 * math.sqrt(10.0 / 7.0)) / 3.0
    inner_weight = (322.0 + 13.0 * math.sqrt(70.0)) / 900.0
    outer_weight = (322.0 - 13.0 * math.sqrt(70.0)) / 900.0
    cosines = np.array([-outer_node, -inner_node, 0.0, inner_node, outer_node])
    weights = np.array([outer_weight, inner_weight, 128.0 / 225.0, inner_weight, outer_weight])
    azimuth = 2.0 * np.pi * (np.arange(10) + 0.5) / 10.0
    polar = np.repeat(cosines, 10)
    circle = np.tile(azimuth, 5)
    point_weight = np.repeat(weights, 10) * 2.0 * np.pi / 10.0
    sine = np.sqrt(1.0 - polar ** 2)
    table_rows = []
    for degree in range(5):
        for order in range(-degree, degree + 1):
            absolute = abs(order)
            legendre = associated(degree, absolute, polar, sine)
            factor = math.sqrt((2 * degree + 1) / (4.0 * math.pi) * math.factorial(degree - absolute) / math.factorial(degree + absolute))
            if order > 0:
                angular = math.sqrt(2.0) * np.cos(order * circle)
            elif order < 0:
                angular = math.sqrt(2.0) * np.sin(absolute * circle)
            else:
                angular = circle * 0.0 + 1.0
            table_rows.append(factor * legendre * angular * point_weight)
    return np.array(table_rows)

def sample_basis(inverse, powers, coords):
    ladders = [jnp.stack([coords[axis_id] ** level for level in range(5)]) for axis_id in range(3)]
    monomial = ladders[0][powers[:, 0]] * ladders[1][powers[:, 1]] * ladders[2][powers[:, 2]]
    return jnp.dot(jnp.asarray(inverse.T, jnp.float32), monomial, precision=highest, preferred_element_type=jnp.float32)

def section_update(derivs, lifting, fields, residue, geometry, normals, face_scale, inner_trace, outer_trace, wall_mask, live_mask):
    slot_count = fields.shape[2]
    width = 4 * slot_count
    inner_vals = inner_trace.reshape(4, 15, width)
    outer_vals = outer_trace.reshape(4, 15, width)
    facing = normals.reshape(3, 1, width)
    blocked = wall_mask.reshape(1, width)
    jump_p = jnp.where(blocked, 0.0, inner_vals[0] - outer_vals[0])
    along_in = lax.optimization_barrier(jnp.sum(facing * inner_vals[1:], axis=0))
    along_jump = lax.optimization_barrier(jnp.sum(facing * (inner_vals[1:] - outer_vals[1:]), axis=0))
    jump_n = jnp.where(blocked, 2.0 * along_in, along_jump)
    scaling = face_scale.reshape(1, width)
    flux_p = 0.5 * (jump_n - jump_p) * scaling
    flux_u = 0.5 * facing * ((jump_p - jump_n) * scaling)[None]
    flux = jnp.concatenate([flux_p[None], flux_u], axis=0).reshape(4, 60, slot_count)
    lifted = jnp.einsum('in,fns->fis', lifting, flux, precision=highest)
    slopes = jnp.einsum('dij,fjs->dfis', derivs, fields, precision=highest)

    def gradient(field_id, axis_id):
        return geometry[axis_id][None] * slopes[0, field_id] + geometry[3 + axis_id][None] * slopes[1, field_id] + geometry[6 + axis_id][None] * slopes[2, field_id]
    divergence = gradient(1, 0) + gradient(2, 1) + gradient(3, 2)
    rates = jnp.stack([lifted[0] - divergence] + [lifted[1 + axis_id] - gradient(0, axis_id) for axis_id in range(3)])
    residue_next = section_decay * residue + time_step * rates
    fields_next = fields + section_gain * residue_next
    keep = live_mask[None, None, :]
    return (jnp.where(keep, fields_next, 0.0), jnp.where(keep, residue_next, 0.0))

def reference(fields, residue, geometry, normals, face_scale, neighbours, send_faces, live_counts, sample_ids, sample_elems, sample_coords):
    derivs_np, lifting_np, face_nodes, inverse, powers = element_tables()
    derivs = jnp.asarray(derivs_np, jnp.float32)
    lifting = jnp.asarray(lifting_np, jnp.float32)
    devices = N_PX * N_PY
    slot_count = ELEM_CAP
    total = slot_count * devices
    table = jnp.stack([fields[:, face_nodes[face_id], :].reshape(60, devices, slot_count) for face_id in range(4)], axis=2).reshape(60, devices * 4 * slot_count)
    column = jnp.arange(total, dtype=jnp.int32)
    device = column // slot_count
    element = column % slot_count
    face_rows = jnp.arange(4, dtype=jnp.int32)[:, None]
    own_block = device[None] * (4 * slot_count) + face_rows * slot_count + element[None]
    wall_mask = neighbours < 0
    shifted = neighbours - 4 * slot_count
    heading = jnp.clip(shifted // BOUND_FACES, 0, 7)
    position = shifted % BOUND_FACES
    flat_dir = heading + (heading >= 4).astype(jnp.int32)
    other = (device[None] // N_PY + flat_dir // 3 - 1) * N_PY + (device[None] % N_PY + flat_dir % 3 - 1)
    other = jnp.clip(other, 0, devices - 1)
    reverse = 7 - heading
    sent = send_faces[reverse, other * BOUND_FACES + position]
    target = jnp.where(neighbours >= 4 * slot_count, other * (4 * slot_count) + sent, device[None] * (4 * slot_count) + neighbours)
    target = jnp.where(wall_mask, own_block, target)

    def one_device(index):
        start = index * slot_count
        part_fields = lax.dynamic_slice_in_dim(fields, start, slot_count, 2)
        part_residue = lax.dynamic_slice_in_dim(residue, start, slot_count, 2)
        part_geometry = lax.dynamic_slice_in_dim(geometry, start, slot_count, 1)
        part_normals = lax.dynamic_slice_in_dim(normals, start, slot_count, 2)
        part_scale = lax.dynamic_slice_in_dim(face_scale, start, slot_count, 1)
        part_target = lax.dynamic_slice_in_dim(target, start, slot_count, 1)
        part_walls = lax.dynamic_slice_in_dim(wall_mask, start, slot_count, 1)
        inner_trace = jnp.concatenate([part_fields[:, face_nodes[face_id], :].reshape(60, slot_count) for face_id in range(4)], axis=1)
        outer_trace = jnp.take(table, part_target.reshape(-1), axis=1)
        live_mask = jnp.arange(slot_count, dtype=jnp.int32) < live_counts[index]
        return section_update(derivs, lifting, part_fields, part_residue, part_geometry, part_normals, part_scale, inner_trace, outer_trace, part_walls.reshape(-1), live_mask)
    results = lax.map(one_device, jnp.arange(devices, dtype=jnp.int32))
    fields_next = jnp.moveaxis(results[0], 0, 2).reshape(4, 35, total)
    residue_next = jnp.moveaxis(results[1], 0, 2).reshape(4, 35, total)
    pressure = fields_next[0]
    holder = jnp.arange(SAMPLES, dtype=jnp.int32) // SAMP_DEV
    gathered = jnp.take(pressure, holder * slot_count + sample_elems, axis=1)
    basis = sample_basis(inverse, powers, sample_coords)
    values = lax.optimization_barrier(jnp.sum(basis * gathered, axis=0))
    ordered = jnp.zeros((SAMPLES,), jnp.float32).at[sample_ids].set(values)
    harmonic = jnp.asarray(harmonic_table(), jnp.float32)
    coefficients = jnp.dot(harmonic, ordered.reshape(RECEIVERS, QPTS).T, precision=highest, preferred_element_type=jnp.float32)
    return (fields_next, residue_next, coefficients)
```

```python
import functools
import math

import jax
import jax.numpy as jnp
import numpy as np
from jax import lax
from jax.experimental import pallas as pl
from jax.experimental.pallas import tpu as pltpu
from jax.sharding import PartitionSpec as P

QPTS = 50
NODES = 35
PAD = 40
FACE_ROWS = 16
LANES = 128


highest = lax.Precision.HIGHEST
section_decay = -567301805773.0 / 1357537059087.0
section_gain = 5161836677717.0 / 13612068292357.0
time_step = 0.01
f32 = jnp.float32
bf16 = jnp.bfloat16


def exponent_table():
    listing = []
    for degree in range(5):
        for third in range(degree + 1):
            for second in range(degree + 1 - third):
                listing.append((degree - second - third, second, third))
    return np.array(listing)


def factorials(values):
    lookup = np.array([float(math.factorial(level)) for level in range(24)])
    return lookup[values]


def eliminate(matrix, right_hand):
    order_size = matrix.shape[0]
    work = np.concatenate([matrix, right_hand], axis=1).astype(float)
    for pivot_col in range(order_size):
        best = max(range(pivot_col, order_size), key=lambda row_id: abs(work[row_id, pivot_col]))
        work[[pivot_col, best]] = work[[best, pivot_col]]
        work[pivot_col] = work[pivot_col] / work[pivot_col, pivot_col]
        for row_id in range(order_size):
            if row_id != pivot_col:
                work[row_id] = work[row_id] - work[row_id, pivot_col] * work[pivot_col]
    return work[:, order_size:]


def element_tables():
    powers = exponent_table()
    points = powers / 4.0
    vander = np.prod(points[:, None, :] ** powers[None, :, :], axis=2)
    inverse = eliminate(vander, np.eye(35))
    derivs = []
    for axis_id in range(3):
        lowered = np.maximum(powers - (np.arange(3) == axis_id)[None, :], 0)
        slope_table = powers[None, :, axis_id] * np.prod(
            points[:, None, :] ** lowered[None, :, :], axis=2
        )
        derivs.append(slope_table @ inverse)
    summed = powers[:, None, :] + powers[None, :, :]
    exp_r = summed[..., 0]
    exp_s = summed[..., 1]
    exp_t = summed[..., 2]
    volume = (
        factorials(exp_r)
        * factorials(exp_s)
        * factorials(exp_t)
        / factorials(exp_r + exp_s + exp_t + 3)
    )
    mass_matrix = inverse.T @ volume @ inverse
    face_grams = [
        np.where(
            exp_t == 0, factorials(exp_r) * factorials(exp_s) / factorials(exp_r + exp_s + 2), 0.0
        ),
        np.where(
            exp_s == 0, factorials(exp_r) * factorials(exp_t) / factorials(exp_r + exp_t + 2), 0.0
        ),
        factorials(exp_r)
        * factorials(exp_s)
        * factorials(exp_t)
        / factorials(exp_r + exp_s + exp_t + 2),
        np.where(
            exp_r == 0, factorials(exp_s) * factorials(exp_t) / factorials(exp_s + exp_t + 2), 0.0
        ),
    ]
    listed = [tuple((int(entry) for entry in powers[node_id])) for node_id in range(35)]
    face_nodes = np.array(
        [
            [node_id for node_id in range(35) if listed[node_id][2] == 0],
            [node_id for node_id in range(35) if listed[node_id][1] == 0],
            [node_id for node_id in range(35) if sum(listed[node_id]) == 4],
            [node_id for node_id in range(35) if listed[node_id][0] == 0],
        ]
    )
    surface = np.zeros((35, 60))
    for face_id in range(4):
        face_mass = inverse.T @ face_grams[face_id] @ inverse
        for node_id in range(15):
            surface[:, 4 * node_id + face_id] = face_mass[:, face_nodes[face_id, node_id]]
    lifting = eliminate(mass_matrix, surface)
    return (np.stack(derivs), lifting, face_nodes, inverse, powers)


def associated(degree, order, cosine, sine):
    current = cosine * 0.0 + 1.0
    for step_id in range(1, order + 1):
        current = -(2 * step_id - 1) * sine * current
    if degree == order:
        return current
    following = cosine * (2 * order + 1) * current
    for level in range(order + 2, degree + 1):
        current, following = (
            following,
            ((2 * level - 1) * cosine * following - (level + order - 1) * current)
            / (level - order),
        )
    return following


def harmonic_table():
    inner_node = math.sqrt(5.0 - 2.0 * math.sqrt(10.0 / 7.0)) / 3.0
    outer_node = math.sqrt(5.0 + 2.0 * math.sqrt(10.0 / 7.0)) / 3.0
    inner_weight = (322.0 + 13.0 * math.sqrt(70.0)) / 900.0
    outer_weight = (322.0 - 13.0 * math.sqrt(70.0)) / 900.0
    cosines = np.array([-outer_node, -inner_node, 0.0, inner_node, outer_node])
    weights = np.array([outer_weight, inner_weight, 128.0 / 225.0, inner_weight, outer_weight])
    azimuth = 2.0 * np.pi * (np.arange(10) + 0.5) / 10.0
    polar = np.repeat(cosines, 10)
    circle = np.tile(azimuth, 5)
    point_weight = np.repeat(weights, 10) * 2.0 * np.pi / 10.0
    sine = np.sqrt(1.0 - polar**2)
    table_rows = []
    for degree in range(5):
        for order in range(-degree, degree + 1):
            absolute = abs(order)
            legendre = associated(degree, absolute, polar, sine)
            factor = math.sqrt(
                (2 * degree + 1)
                / (4.0 * math.pi)
                * math.factorial(degree - absolute)
                / math.factorial(degree + absolute)
            )
            if order > 0:
                angular = math.sqrt(2.0) * np.cos(order * circle)
            elif order < 0:
                angular = math.sqrt(2.0) * np.sin(absolute * circle)
            else:
                angular = circle * 0.0 + 1.0
            table_rows.append(factor * legendre * angular * point_weight)
    return np.array(table_rows)


def constant_tables():
    derivs, lifting, face_nodes, inverse, powers = element_tables()
    table_select = np.zeros((4 * PAD, 4 * LANES), np.float32)
    trace_select = np.zeros((4 * 4 * FACE_ROWS, 4 * PAD), np.float32)
    for face in range(4):
        for field in range(4):
            for place in range(15):
                source = PAD * field + face_nodes[face, place]
                column = FACE_ROWS * field + place
                table_select[source, LANES * face + column] = 1.0
                table_select[source, LANES * face + 64 + column] = 1.0
                trace_select[64 * face + column, source] = 1.0
    whole = np.round(3.0 * derivs)
    into_p = np.zeros((PAD, 128), np.float32)
    from_p = np.zeros((3 * PAD, 48), np.float32)
    for axis_id in range(3):
        into_p[:NODES, PAD * axis_id : PAD * axis_id + NODES] = whole[axis_id]
        from_p[PAD * axis_id : PAD * axis_id + NODES, :NODES] = whole[axis_id]
    lift = np.zeros((PAD, 64), np.float32)
    for face in range(4):
        for place in range(15):
            lift[:NODES, FACE_ROWS * face + place] = lifting[:, 4 * place + face]
    lift_hi = lift.astype(jnp.bfloat16)
    lift_lo = (lift - lift_hi.astype(np.float32)).astype(jnp.bfloat16)
    return {
        "table_select": jnp.asarray(table_select, bf16),
        "trace_select": jnp.asarray(trace_select, bf16),
        "into_p": jnp.asarray(np.concatenate([into_p, into_p], axis=1), bf16),
        "from_p": jnp.asarray(np.concatenate([from_p, from_p], axis=1), bf16),
        "lift": jnp.asarray(np.concatenate([lift_hi, lift_hi, lift_lo], axis=1)),
        "inverse": jnp.asarray(np.pad(inverse.T, ((0, 5), (0, 5))), f32),
        "powers": powers,
    }


def halves(values):
    high = values.astype(bf16)
    return high, (values - high.astype(f32)).astype(bf16)


def thirds(values):
    high = values.astype(bf16)
    rest = values - high.astype(f32)
    middle = rest.astype(bf16)
    return high, middle, (rest - middle.astype(f32)).astype(bf16)


def product(left, right, dims=((1,), (0,))):
    return lax.dot_general(left, right, (dims, ((), ())), preferred_element_type=f32)


def stack_fields(fields_ref, stacked):
    for field in range(4):
        stacked[PAD * field : PAD * field + NODES, :] = fields_ref[field]
    return halves(stacked[...])


def pack_kernel(slot_faces, fields_ref, codes_ref, select_ref, up_ref, down_ref, left_ref, right_ref, stacked):
    stacked[...] = jnp.zeros_like(stacked)
    high, low = stack_fields(fields_ref, stacked)
    traces = product(select_ref[...], high) + product(select_ref[...], low)
    chosen = jnp.zeros((64, traces.shape[1]), f32)
    for face in range(4):
        remote = codes_ref[face : face + 1, :] >= slot_faces
        chosen = jnp.where(remote, traces[64 * face : 64 * face + 64, :], chosen)
    width = left_ref.shape[1]
    pieces = [chosen[:, width * heading : width * heading + width] for heading in range(8)]
    for place in range(3):
        up_ref[place] = pieces[place]
        down_ref[place] = pieces[5 + place]
    left_ref[...] = pieces[3]
    right_ref[...] = pieces[4]


def table_kernel(fields_ref, select_ref, table_ref, stacked):
    @pl.when(pl.program_id(0) == 0)
    def _():
        stacked[...] = jnp.zeros_like(stacked)

    high, low = stack_fields(fields_ref, stacked)
    for half in range(2):
        select = select_ref[:, 256 * half : 256 * half + 256]
        rows = product(high, select, ((0,), (0,))) + product(low, select, ((0,), (0,)))
        table_ref[2 * half] = rows[:, :LANES]
        table_ref[2 * half + 1] = rows[:, LANES:]


def gather_kernel(slot_count, codes_ref, table_ref, normals_ref, outer_ref, *rows_refs):
    width = outer_ref.shape[1]
    first = pl.program_id(0) * width
    left_half = lax.broadcasted_iota(jnp.int32, (1, LANES), 1) < 64
    for tile in range(width // LANES):
        for half in range(2):
            rows_ref = rows_refs[half]
            base = half * slot_count + first + tile * LANES
            for row in range(LANES):
                code = codes_ref[base + row]
                one = table_ref[pl.ds(code & 0xFFFF, 1), :]
                two = table_ref[pl.ds(lax.shift_right_logical(code, 16), 1), :]
                rows_ref[row : row + 1, :] = jnp.where(left_half, one, two)
            turned = rows_ref[...].T
            lanes = slice(tile * LANES, tile * LANES + LANES)
            for side in range(2):
                face = 2 * half + side
                part = turned[64 * side : 64 * side + 64, :]
                total = -part[0:16]
                for axis_id in range(3):
                    facing = normals_ref[axis_id, face : face + 1, lanes]
                    total = total + facing * part[16 + 16 * axis_id : 32 + 16 * axis_id]
                outer_ref[FACE_ROWS * face : FACE_ROWS * face + FACE_ROWS, lanes] = total


def pressure_kernel(
    slot_faces,
    powers,
    group,
    live_ref,
    fields_ref,
    residue_ref,
    geometry_ref,
    normals_ref,
    scale_ref,
    codes_ref,
    outer_ref,
    right_ref,
    left_ref,
    below_ref,
    above_ref,
    elems_ref,
    ids_ref,
    coords_ref,
    select_ref,
    into_ref,
    lift_ref,
    inverse_ref,
    next_ref,
    rate_ref,
    flux_ref,
    spread_ref,
    stacked,
    combined,
    remote,
    outside,
    sampled,
    pressure,
    monomials,
):
    step = pl.program_id(0)
    width = fields_ref.shape[2]

    @pl.when(step == 0)
    def _():
        stacked[...] = jnp.zeros_like(stacked)
        combined[...] = jnp.zeros_like(combined)
        pressure[...] = jnp.zeros_like(pressure)
        sampled[...] = jnp.zeros_like(sampled)
        monomials[...] = jnp.zeros_like(monomials)

    outside[...] = outer_ref[...]

    @pl.when(step == 0)
    def _():
        count = right_ref.shape[2]
        sources = [
            left_ref[2],
            above_ref[1],
            right_ref[2],
            left_ref[0],
            right_ref[0],
            left_ref[1],
            below_ref[1],
            right_ref[1],
        ]
        for heading in range(8):
            remote[:, count * heading : count * heading + count] = sources[heading]
        for face in range(4):
            rows = slice(FACE_ROWS * face, FACE_ROWS * face + FACE_ROWS)
            total = -remote[0:16, :]
            for axis_id in range(3):
                facing = normals_ref[axis_id, face : face + 1, :]
                total = total + facing * remote[16 + 16 * axis_id : 32 + 16 * axis_id, :]
            is_remote = codes_ref[face : face + 1, :] >= slot_faces
            outside[rows, :] = jnp.where(is_remote, total, outside[rows, :])

    high, low = stack_fields(fields_ref, stacked)
    traces = product(select_ref[...], high) + product(select_ref[...], low)
    fluxes = []
    for face in range(4):
        inner_p = traces[64 * face : 64 * face + 16]
        along = jnp.zeros_like(inner_p)
        for axis_id in range(3):
            facing = normals_ref[axis_id, face : face + 1, :]
            start = 64 * face + 16 + 16 * axis_id
            along = along + facing * traces[start : start + 16]
        wall = codes_ref[face : face + 1, :] < 0
        beyond = outside[FACE_ROWS * face : FACE_ROWS * face + FACE_ROWS, :]
        beyond = jnp.where(wall, -along - inner_p, beyond)
        flux = (0.5 * scale_ref[face : face + 1, :]) * (along - inner_p - beyond)
        flux_ref[FACE_ROWS * face : FACE_ROWS * face + FACE_ROWS, :] = flux
    flux_hi, flux_lo = halves(flux_ref[...])
    lifted = product(lift_ref[...], jnp.concatenate([flux_hi, flux_lo, flux_hi], axis=0))
    for axis_id in range(3):
        total = geometry_ref[3 * axis_id : 3 * axis_id + 1, :] * fields_ref[1]
        for direction in range(1, 3):
            at = 3 * axis_id + direction
            total = total + geometry_ref[at : at + 1, :] * fields_ref[1 + direction]
        combined[PAD * axis_id : PAD * axis_id + NODES, :] = total
    high, low = halves(combined[...])
    divergence = product(into_ref[...], jnp.concatenate([high, low], axis=0))
    rate = (lifted - divergence * (1.0 / 3.0))[:NODES]
    keep = lax.broadcasted_iota(jnp.int32, (1, width), 1) + step * width < live_ref[0]
    residue_next = section_decay * residue_ref[0] + time_step * rate
    fields_next = fields_ref[0] + section_gain * residue_next
    fields_next = jnp.where(keep, fields_next, 0.0)
    next_ref[...] = fields_next
    rate_ref[...] = jnp.where(keep, residue_next, 0.0)

    pressure[0:NODES, :] = fields_next
    parts = jnp.concatenate(thirds(pressure[...]), axis=0)
    slots = lax.broadcasted_iota(jnp.int32, (width, elems_ref.shape[1]), 0) + step * width
    picks = jnp.where(slots == elems_ref[...], 1.0, 0.0).astype(bf16)
    sampled[...] += product(parts, picks)

    @pl.when(step == pl.num_programs(0) - 1)
    def _():
        ladders = []
        for axis_id in range(3):
            base = coords_ref[axis_id : axis_id + 1, :]
            square = base * base
            ladders.append([jnp.ones_like(base), base, square, square * base, square * square])
        for node in range(NODES):
            exps = [int(entry) for entry in powers[node]]
            monomials[node : node + 1, :] = (
                ladders[0][exps[0]] * ladders[1][exps[1]] * ladders[2][exps[2]]
            )
        basis = jnp.dot(
            inverse_ref[...], monomials[...], precision=highest, preferred_element_type=f32
        )
        gathered = sampled[0:PAD, :] + sampled[48 : 48 + PAD, :] + sampled[96 : 96 + PAD, :]
        values = jnp.sum(basis * gathered, axis=0, keepdims=True)
        ids = ids_ref[...]
        owner = lax.shift_right_logical(ids * 5243, 20)
        place = ids - group * owner
        devices = spread_ref.shape[0]
        owners = lax.broadcasted_iota(jnp.int32, (devices, ids.shape[1]), 0)
        held = jnp.where(owners == owner, values, 0.0)
        places = lax.broadcasted_iota(jnp.int32, (spread_ref.shape[1], ids.shape[1]), 0)
        chosen = jnp.where(places == place, 1.0, 0.0).astype(bf16)
        spread = jnp.zeros(spread_ref.shape, f32)
        for part in thirds(held):
            spread = spread + product(part, chosen, ((1,), (1,)))
        spread_ref[...] = spread


def velocity_kernel(
    live_ref,
    fields_ref,
    residue_x_ref,
    residue_y_ref,
    residue_z_ref,
    geometry_ref,
    normals_ref,
    flux_ref,
    done_p_ref,
    done_r_ref,
    from_ref,
    lift_ref,
    fields_out,
    residue_out,
    pressure,
):
    step = pl.program_id(0)
    width = fields_ref.shape[2]

    @pl.when(step == 0)
    def _():
        pressure[...] = jnp.zeros_like(pressure)

    pressure[0:NODES, :] = fields_ref[0]
    high, low = halves(pressure[...])
    slopes = product(from_ref[...], jnp.concatenate([high, low], axis=0))
    keep = lax.broadcasted_iota(jnp.int32, (1, width), 1) + step * width < live_ref[0]
    fields_out[0] = done_p_ref[...]
    residue_out[0] = done_r_ref[...]
    for direction, residue_ref in enumerate((residue_x_ref, residue_y_ref, residue_z_ref)):
        pieces = []
        for face in range(4):
            facing = normals_ref[direction, face : face + 1, :]
            pieces.append(facing * flux_ref[FACE_ROWS * face : FACE_ROWS * face + FACE_ROWS, :])
        flux_hi, flux_lo = halves(jnp.concatenate(pieces, axis=0))
        lifted = product(lift_ref[...], jnp.concatenate([flux_hi, flux_lo, flux_hi], axis=0))
        rate = lifted
        for axis_id in range(3):
            at = 3 * axis_id + direction
            rate = rate + (geometry_ref[at : at + 1, :] * (1.0 / 3.0)) * (
                slopes[PAD * axis_id : PAD * axis_id + PAD]
            )
        residue_next = section_decay * residue_ref[0] - time_step * rate[:NODES]
        fields_next = fields_ref[1 + direction] + section_gain * residue_next
        fields_out[1 + direction] = jnp.where(keep, fields_next, 0.0)
        residue_out[1 + direction] = jnp.where(keep, residue_next, 0.0)


def harmonic_kernel(received_ref, table_ref, groups_ref, out_ref):
    mine = jnp.sum(received_ref[...], axis=0, keepdims=True)
    weighted = table_ref[...] * mine
    out_ref[...] = jnp.dot(
        weighted, groups_ref[...], precision=highest, preferred_element_type=f32
    )


def fixed(shape):
    return pl.BlockSpec(shape, lambda *_: (0,) * len(shape))


def local(
    fields,
    residue,
    geometry,
    normals,
    face_scale,
    neighbours,
    send_faces,
    live_counts,
    sample_ids,
    sample_elems,
    sample_coords,
):
    const = constant_tables()
    slot_count = fields.shape[2]
    slot_faces = 4 * slot_count
    bound_count = send_faces.shape[1]
    reach = 8 * bound_count
    width = reach
    steps = slot_count // width
    samples = sample_ids.shape[0]
    devices = lax.axis_size(("px", "py"))
    limit = pltpu.CompilerParams(vmem_limit_bytes=48 << 20)
    shape = jax.ShapeDtypeStruct

    up, down, left, right = pl.pallas_call(
        functools.partial(pack_kernel, slot_faces),
        grid=(1,),
        in_specs=[
            pl.BlockSpec((4, NODES, reach), lambda t: (0, 0, 0)),
            pl.BlockSpec((4, reach), lambda t: (0, 0)),
            fixed((256, 4 * PAD)),
        ],
        out_specs=[
            fixed((3, 64, bound_count)),
            fixed((3, 64, bound_count)),
            fixed((64, bound_count)),
            fixed((64, bound_count)),
        ],
        out_shape=[
            shape((3, 64, bound_count), f32),
            shape((3, 64, bound_count), f32),
            shape((64, bound_count), f32),
            shape((64, bound_count), f32),
        ],
        scratch_shapes=[pltpu.VMEM((4 * PAD, reach), f32)],
        compiler_params=limit,
        name="pack",
    )(fields, neighbours, const["trace_select"])

    def steps_along(axis):
        count = lax.axis_size(axis)
        forward = [(i, i + 1) for i in range(count - 1)]
        return forward, [(target, source) for source, target in forward]

    forward, backward = steps_along("px")
    below = lax.ppermute(up, "px", backward)
    above = lax.ppermute(down, "px", forward)

    table = pl.pallas_call(
        table_kernel,
        grid=(steps,),
        in_specs=[
            pl.BlockSpec((4, NODES, width), lambda t: (0, 0, t)),
            fixed((4 * PAD, 4 * LANES)),
        ],
        out_specs=pl.BlockSpec((4, width, LANES), lambda t: (0, t, 0)),
        out_shape=shape((4, slot_count, LANES), f32),
        scratch_shapes=[pltpu.VMEM((4 * PAD, width), f32)],
        compiler_params=limit,
        name="table",
    )(fields, const["table_select"]).reshape(slot_faces, LANES)

    forward, backward = steps_along("py")
    to_left = jnp.concatenate([left[None], below[0:1], above[0:1]])
    to_right = jnp.concatenate([right[None], below[2:3], above[2:3]])
    from_right = lax.ppermute(to_left, "py", backward)
    from_left = lax.ppermute(to_right, "py", forward)

    inside = (neighbours >= 0) & (neighbours < slot_faces)
    codes = jnp.where(inside, neighbours, 0)
    codes = (codes[0::2] + (codes[1::2] << 16)).reshape(-1)
    gather_width = 512
    outer = pl.pallas_call(
        functools.partial(gather_kernel, slot_count),
        grid_spec=pltpu.PrefetchScalarGridSpec(
            num_scalar_prefetch=1,
            grid=(slot_count // gather_width,),
            in_specs=[
                pl.BlockSpec(memory_space=pltpu.VMEM),
                pl.BlockSpec((3, 4, gather_width), lambda t, _: (0, 0, t)),
            ],
            out_specs=pl.BlockSpec((64, gather_width), lambda t, _: (0, t)),
            scratch_shapes=[pltpu.VMEM((LANES, LANES), f32)] * 2,
        ),
        out_shape=shape((64, slot_count), f32),
        compiler_params=limit,
        name="gather",
    )(codes, table, normals)

    next_p, next_r, flux, spread = pl.pallas_call(
        functools.partial(pressure_kernel, slot_faces, const["powers"], samples),
        grid_spec=pltpu.PrefetchScalarGridSpec(
            num_scalar_prefetch=1,
            grid=(steps,),
            in_specs=[
                pl.BlockSpec((4, NODES, width), lambda t, _: (0, 0, t)),
                pl.BlockSpec((1, NODES, width), lambda t, _: (0, 0, t)),
                pl.BlockSpec((9, width), lambda t, _: (0, t)),
                pl.BlockSpec((3, 4, width), lambda t, _: (0, 0, t)),
                pl.BlockSpec((4, width), lambda t, _: (0, t)),
                pl.BlockSpec((4, width), lambda t, _: (0, t)),
                pl.BlockSpec((64, width), lambda t, _: (0, t)),
                fixed((3, 64, bound_count)),
                fixed((3, 64, bound_count)),
                fixed((3, 64, bound_count)),
                fixed((3, 64, bound_count)),
                fixed((1, samples)),
                fixed((1, samples)),
                fixed((3, samples)),
                fixed((256, 4 * PAD)),
                fixed((PAD, 256)),
                fixed((PAD, 192)),
                fixed((PAD, PAD)),
            ],
            out_specs=[
                pl.BlockSpec((NODES, width), lambda t, _: (0, t)),
                pl.BlockSpec((NODES, width), lambda t, _: (0, t)),
                pl.BlockSpec((64, width), lambda t, _: (0, t)),
                fixed((devices, samples)),
            ],
            scratch_shapes=[
                pltpu.VMEM((4 * PAD, width), f32),
                pltpu.VMEM((128, width), f32),
                pltpu.VMEM((64, width), f32),
                pltpu.VMEM((64, width), f32),
                pltpu.VMEM((144, samples), f32),
                pltpu.VMEM((48, width), f32),
                pltpu.VMEM((PAD, samples), f32),
            ],
        ),
        out_shape=[
            shape((NODES, slot_count), f32),
            shape((NODES, slot_count), f32),
            shape((64, slot_count), f32),
            shape((devices, samples), f32),
        ],
        compiler_params=limit,
        name="pressure",
    )(
        live_counts,
        fields,
        residue,
        geometry,
        normals,
        face_scale,
        neighbours,
        outer,
        from_right,
        from_left,
        below,
        above,
        sample_elems.reshape(1, samples),
        sample_ids.reshape(1, samples),
        sample_coords,
        const["trace_select"],
        const["into_p"],
        const["lift"],
        const["inverse"],
    )
    received = lax.all_to_all(spread, ("px", "py"), 0, 0, tiled=True)

    def plane(index):
        return pl.BlockSpec((1, NODES, width), lambda t, _: (index, 0, t))

    fields_next, residue_next = pl.pallas_call(
        velocity_kernel,
        grid_spec=pltpu.PrefetchScalarGridSpec(
            num_scalar_prefetch=1,
            grid=(steps,),
            in_specs=[
                pl.BlockSpec((4, NODES, width), lambda t, _: (0, 0, t)),
                plane(1),
                plane(2),
                plane(3),
                pl.BlockSpec((9, width), lambda t, _: (0, t)),
                pl.BlockSpec((3, 4, width), lambda t, _: (0, 0, t)),
                pl.BlockSpec((64, width), lambda t, _: (0, t)),
                pl.BlockSpec((NODES, width), lambda t, _: (0, t)),
                pl.BlockSpec((NODES, width), lambda t, _: (0, t)),
                fixed((3 * PAD, 96)),
                fixed((PAD, 192)),
            ],
            out_specs=[
                pl.BlockSpec((4, NODES, width), lambda t, _: (0, 0, t)),
                pl.BlockSpec((4, NODES, width), lambda t, _: (0, 0, t)),
            ],
            scratch_shapes=[pltpu.VMEM((48, width), f32)],
        ),
        out_shape=[shape(fields.shape, f32), shape(residue.shape, f32)],
        compiler_params=limit,
        name="velocity",
    )(
        live_counts,
        fields,
        residue,
        residue,
        residue,
        geometry,
        normals,
        flux,
        next_p,
        next_r,
        const["from_p"],
        const["lift"],
    )

    receivers = samples // QPTS
    harmonic = np.tile(harmonic_table(), (1, receivers)).astype(np.float32)
    groups = (np.arange(samples)[:, None] // QPTS == np.arange(receivers)[None]).astype(np.float32)
    coefficients = pl.pallas_call(
        harmonic_kernel,
        out_shape=shape((harmonic.shape[0], receivers), f32),
        name="harmonic",
    )(received, jnp.asarray(harmonic), jnp.asarray(groups))
    return (fields_next, residue_next, coefficients)


def solution(mesh):
    placed = (
        P(None, None, ("px", "py")),
        P(None, None, ("px", "py")),
        P(None, ("px", "py")),
        P(None, None, ("px", "py")),
        P(None, ("px", "py")),
        P(None, ("px", "py")),
        P(None, ("px", "py")),
        P(("px", "py")),
        P(("px", "py")),
        P(("px", "py")),
        P(None, ("px", "py")),
    )
    return jax.shard_map(
        local,
        mesh=mesh,
        in_specs=placed,
        out_specs=(P(None, None, ("px", "py")), P(None, None, ("px", "py")), P(None, ("px", "py"))),
        check_vma=False,
    )
```

```python
import functools
import math

import jax
import jax.numpy as jnp
import numpy as np
from jax import lax
from jax.experimental import pallas as pl
from jax.experimental.pallas import tpu as pltpu
from jax.sharding import PartitionSpec as P

QPTS = 50
NODES = 35
PAD = 40
FACE_ROWS = 16
ROWS = 144
LANES = 128


highest = lax.Precision.HIGHEST
section_decay = -567301805773.0 / 1357537059087.0
section_gain = 5161836677717.0 / 13612068292357.0
time_step = 0.01
f32 = jnp.float32
bf16 = jnp.bfloat16


def exponent_table():
    listing = []
    for degree in range(5):
        for third in range(degree + 1):
            for second in range(degree + 1 - third):
                listing.append((degree - second - third, second, third))
    return np.array(listing)


def factorials(values):
    lookup = np.array([float(math.factorial(level)) for level in range(24)])
    return lookup[values]


def eliminate(matrix, right_hand):
    order_size = matrix.shape[0]
    work = np.concatenate([matrix, right_hand], axis=1).astype(float)
    for pivot_col in range(order_size):
        best = max(range(pivot_col, order_size), key=lambda row_id: abs(work[row_id, pivot_col]))
        work[[pivot_col, best]] = work[[best, pivot_col]]
        work[pivot_col] = work[pivot_col] / work[pivot_col, pivot_col]
        for row_id in range(order_size):
            if row_id != pivot_col:
                work[row_id] = work[row_id] - work[row_id, pivot_col] * work[pivot_col]
    return work[:, order_size:]


def element_tables():
    powers = exponent_table()
    points = powers / 4.0
    vander = np.prod(points[:, None, :] ** powers[None, :, :], axis=2)
    inverse = eliminate(vander, np.eye(35))
    derivs = []
    for axis_id in range(3):
        lowered = np.maximum(powers - (np.arange(3) == axis_id)[None, :], 0)
        slope_table = powers[None, :, axis_id] * np.prod(
            points[:, None, :] ** lowered[None, :, :], axis=2
        )
        derivs.append(slope_table @ inverse)
    summed = powers[:, None, :] + powers[None, :, :]
    exp_r = summed[..., 0]
    exp_s = summed[..., 1]
    exp_t = summed[..., 2]
    volume = (
        factorials(exp_r)
        * factorials(exp_s)
        * factorials(exp_t)
        / factorials(exp_r + exp_s + exp_t + 3)
    )
    mass_matrix = inverse.T @ volume @ inverse
    face_grams = [
        np.where(
            exp_t == 0, factorials(exp_r) * factorials(exp_s) / factorials(exp_r + exp_s + 2), 0.0
        ),
        np.where(
            exp_s == 0, factorials(exp_r) * factorials(exp_t) / factorials(exp_r + exp_t + 2), 0.0
        ),
        factorials(exp_r)
        * factorials(exp_s)
        * factorials(exp_t)
        / factorials(exp_r + exp_s + exp_t + 2),
        np.where(
            exp_r == 0, factorials(exp_s) * factorials(exp_t) / factorials(exp_s + exp_t + 2), 0.0
        ),
    ]
    listed = [tuple((int(entry) for entry in powers[node_id])) for node_id in range(35)]
    face_nodes = np.array(
        [
            [node_id for node_id in range(35) if listed[node_id][2] == 0],
            [node_id for node_id in range(35) if listed[node_id][1] == 0],
            [node_id for node_id in range(35) if sum(listed[node_id]) == 4],
            [node_id for node_id in range(35) if listed[node_id][0] == 0],
        ]
    )
    surface = np.zeros((35, 60))
    for face_id in range(4):
        face_mass = inverse.T @ face_grams[face_id] @ inverse
        for node_id in range(15):
            surface[:, 4 * node_id + face_id] = face_mass[:, face_nodes[face_id, node_id]]
    lifting = eliminate(mass_matrix, surface)
    return (np.stack(derivs), lifting, face_nodes, inverse, powers)


def associated(degree, order, cosine, sine):
    current = cosine * 0.0 + 1.0
    for step_id in range(1, order + 1):
        current = -(2 * step_id - 1) * sine * current
    if degree == order:
        return current
    following = cosine * (2 * order + 1) * current
    for level in range(order + 2, degree + 1):
        current, following = (
            following,
            ((2 * level - 1) * cosine * following - (level + order - 1) * current)
            / (level - order),
        )
    return following


def harmonic_table():
    inner_node = math.sqrt(5.0 - 2.0 * math.sqrt(10.0 / 7.0)) / 3.0
    outer_node = math.sqrt(5.0 + 2.0 * math.sqrt(10.0 / 7.0)) / 3.0
    inner_weight = (322.0 + 13.0 * math.sqrt(70.0)) / 900.0
    outer_weight = (322.0 - 13.0 * math.sqrt(70.0)) / 900.0
    cosines = np.array([-outer_node, -inner_node, 0.0, inner_node, outer_node])
    weights = np.array([outer_weight, inner_weight, 128.0 / 225.0, inner_weight, outer_weight])
    azimuth = 2.0 * np.pi * (np.arange(10) + 0.5) / 10.0
    polar = np.repeat(cosines, 10)
    circle = np.tile(azimuth, 5)
    point_weight = np.repeat(weights, 10) * 2.0 * np.pi / 10.0
    sine = np.sqrt(1.0 - polar**2)
    table_rows = []
    for degree in range(5):
        for order in range(-degree, degree + 1):
            absolute = abs(order)
            legendre = associated(degree, absolute, polar, sine)
            factor = math.sqrt(
                (2 * degree + 1)
                / (4.0 * math.pi)
                * math.factorial(degree - absolute)
                / math.factorial(degree + absolute)
            )
            if order > 0:
                angular = math.sqrt(2.0) * np.cos(order * circle)
            elif order < 0:
                angular = math.sqrt(2.0) * np.sin(absolute * circle)
            else:
                angular = circle * 0.0 + 1.0
            table_rows.append(factor * legendre * angular * point_weight)
    return np.array(table_rows)


def constant_tables():
    derivs, lifting, face_nodes, inverse, powers = element_tables()
    table_select = np.zeros((ROWS, 4 * LANES), np.float32)
    trace_select = np.zeros((4 * 4 * FACE_ROWS, ROWS), np.float32)
    for face in range(4):
        for field in range(4):
            for place in range(15):
                source = 4 * face_nodes[face, place] + field
                column = FACE_ROWS * field + place
                table_select[source, LANES * face + column] = 1.0
                table_select[source, LANES * face + 64 + column] = 1.0
                trace_select[64 * face + column, source] = 1.0
    whole = np.round(3.0 * derivs)
    into_p = np.zeros((ROWS, 128), np.float32)
    from_p = np.zeros((3 * ROWS, 48), np.float32)
    lift = np.zeros((ROWS, 256), np.float32)
    for node in range(NODES):
        for axis_id in range(3):
            into_p[4 * node, PAD * axis_id : PAD * axis_id + NODES] = -whole[axis_id, node]
            for field in range(1, 4):
                from_p[ROWS * axis_id + 4 * node + field, :NODES] = whole[axis_id, node]
        for face in range(4):
            for place in range(15):
                entry = lifting[node, 4 * place + face]
                column = FACE_ROWS * face + place
                lift[4 * node, column] = entry
                for field in range(1, 4):
                    lift[4 * node + field, 64 * field + column] = -entry
    lift_hi = lift.astype(jnp.bfloat16)
    lift_lo = (lift - lift_hi.astype(np.float32)).astype(jnp.bfloat16)
    return {
        "table_select": jnp.asarray(table_select, bf16),
        "trace_select": jnp.asarray(trace_select, bf16),
        "into_p": jnp.asarray(np.concatenate([into_p, into_p], axis=1), bf16),
        "from_p": jnp.asarray(np.concatenate([from_p, from_p], axis=1), bf16),
        "lift": jnp.asarray(np.concatenate([lift_hi, lift_lo], axis=0)),
        "inverse": jnp.asarray(np.pad(inverse.T, ((0, 5), (0, 5))), f32),
        "powers": powers,
    }


def halves(values):
    high = values.astype(bf16)
    return high, (values - high.astype(f32)).astype(bf16)


def thirds(values):
    high = values.astype(bf16)
    rest = values - high.astype(f32)
    middle = rest.astype(bf16)
    return high, middle, (rest - middle.astype(f32)).astype(bf16)


def product(left, right, dims=((1,), (0,))):
    return lax.dot_general(left, right, (dims, ((), ())), preferred_element_type=f32)


def stack_nodes(fields_ref, stacked):
    tiles = range(stacked.shape[0])
    for tile in tiles:
        for node in range(NODES):
            stacked[tile, 4 * node : 4 * node + 4, :] = fields_ref[
                node, :, LANES * tile : LANES * tile + LANES
            ]
    return halves(jnp.concatenate([stacked[tile] for tile in tiles], axis=1))


def one_field(stacked, field):
    tiles = range(stacked.shape[0])
    rows = pl.ds(field, NODES, stride=4)
    return jnp.concatenate([stacked[tile, rows, :] for tile in tiles], axis=1)


def pack_kernel(slot_faces, fields_ref, codes_ref, select_ref, up_ref, down_ref, left_ref, right_ref, stacked):
    stacked[...] = jnp.zeros_like(stacked)
    high, low = stack_nodes(fields_ref, stacked)
    traces = product(select_ref[...], high) + product(select_ref[...], low)
    chosen = jnp.zeros((64, traces.shape[1]), f32)
    for face in range(4):
        remote = codes_ref[face : face + 1, :] >= slot_faces
        chosen = jnp.where(remote, traces[64 * face : 64 * face + 64, :], chosen)
    width = left_ref.shape[1]
    pieces = [chosen[:, width * heading : width * heading + width] for heading in range(8)]
    for place in range(3):
        up_ref[place] = pieces[place]
        down_ref[place] = pieces[5 + place]
    left_ref[...] = pieces[3]
    right_ref[...] = pieces[4]


def table_kernel(slot_faces, fields_ref, codes_ref, select_ref, table_ref, packed_ref, stacked):
    @pl.when(pl.program_id(0) == 0)
    def _():
        stacked[...] = jnp.zeros_like(stacked)

    high, low = stack_nodes(fields_ref, stacked)
    for half in range(2):
        select = select_ref[:, 256 * half : 256 * half + 256]
        rows = product(high, select, ((0,), (0,))) + product(low, select, ((0,), (0,)))
        table_ref[2 * half] = rows[:, :LANES]
        table_ref[2 * half + 1] = rows[:, LANES:]
        codes = codes_ref[2 * half : 2 * half + 2, :]
        codes = jnp.where((codes >= 0) & (codes < slot_faces), codes, 0)
        packed_ref[half : half + 1, :] = codes[0:1] + (codes[1:2] << 16)


def gather_rows(slot_count, first, codes_ref, table_ref, normals_ref, outer_ref, rows_refs):
    width = outer_ref.shape[1]
    left_half = lax.broadcasted_iota(jnp.int32, (1, LANES), 1) < 64
    for tile in range(width // LANES):
        for half in range(2):
            rows_ref = rows_refs[half]
            base = half * slot_count + first + tile * LANES
            for row in range(LANES):
                code = codes_ref[base + row]
                one = table_ref[pl.ds(code & 0xFFFF, 1), :]
                two = table_ref[pl.ds(lax.shift_right_logical(code, 16), 1), :]
                rows_ref[row : row + 1, :] = jnp.where(left_half, one, two)
            turned = rows_ref[...].T
            lanes = slice(tile * LANES, tile * LANES + LANES)
            for side in range(2):
                face = 2 * half + side
                part = turned[64 * side : 64 * side + 64, :]
                total = -part[0:16]
                for axis_id in range(3):
                    facing = normals_ref[axis_id, face : face + 1, lanes]
                    total = total + facing * part[16 + 16 * axis_id : 32 + 16 * axis_id]
                outer_ref[FACE_ROWS * face : FACE_ROWS * face + FACE_ROWS, lanes] = total


def outer_flux(traces, normals_ref, scale_ref, codes_ref, outer_ref):
    fluxes = []
    for face in range(4):
        inner_p = traces[64 * face : 64 * face + 16]
        along = jnp.zeros_like(inner_p)
        for axis_id in range(3):
            facing = normals_ref[axis_id, face : face + 1, :]
            start = 64 * face + 16 + 16 * axis_id
            along = along + facing * traces[start : start + 16]
        wall = codes_ref[face : face + 1, :] < 0
        beyond = outer_ref[FACE_ROWS * face : FACE_ROWS * face + FACE_ROWS, :]
        beyond = jnp.where(wall, -along - inner_p, beyond)
        fluxes.append((0.5 * scale_ref[face : face + 1, :]) * (along - inner_p - beyond))
    columns = list(fluxes)
    for axis_id in range(3):
        for face in range(4):
            columns.append(normals_ref[axis_id, face : face + 1, :] * fluxes[face])
    return jnp.concatenate(columns, axis=0)


def section_kernel(
    slot_count,
    powers,
    group,
    packed_ref,
    live_ref,
    table_ref,
    next_normals_ref,
    fields_ref,
    residue_ref,
    geometry_ref,
    normals_ref,
    scale_ref,
    codes_ref,
    right_ref,
    left_ref,
    below_ref,
    above_ref,
    elems_ref,
    ids_ref,
    coords_ref,
    select_ref,
    into_ref,
    from_ref,
    lift_ref,
    inverse_ref,
    fields_out,
    residue_out,
    spread_ref,
    stacked,
    combined,
    slow,
    rates,
    remote,
    outer,
    sampled,
    pressure,
    monomials,
    *rows_refs,
):
    step = pl.program_id(0)
    last = pl.num_programs(0) - 1
    width = fields_ref.shape[2]
    slot_faces = 4 * slot_count

    def gather():
        first = step * width
        gather_rows(slot_count, first, packed_ref, table_ref, next_normals_ref, outer, rows_refs)

    def update(beside):
        first = (step - 1) * width
        high, low = stack_nodes(fields_ref, stacked)
        traces = product(select_ref[...], high) + product(select_ref[...], low)
        flux = outer_flux(traces, normals_ref, scale_ref, codes_ref, outer)
        beside()
        flux_hi, flux_lo = halves(flux)
        lifted = product(lift_ref[...], flux_hi)
        total = lifted[:ROWS] + lifted[ROWS:] + product(lift_ref[0:ROWS, :], flux_lo)
        geometry = geometry_ref[...] * (1.0 / 3.0)
        for axis_id in range(3):
            weighted = jnp.zeros((NODES, width), f32)
            for direction in range(3):
                at = 3 * axis_id + direction
                velocity = one_field(stacked, 1 + direction)
                weighted = weighted + geometry[at : at + 1, :] * velocity
            combined[PAD * axis_id : PAD * axis_id + NODES, :] = weighted
        total = total + product(into_ref[...], jnp.concatenate(halves(combined[...]), axis=0))
        slow[0:NODES, :] = one_field(stacked, 0)
        slopes = product(from_ref[...], jnp.concatenate(halves(slow[...]), axis=0))
        place = lax.broadcasted_iota(jnp.int32, (8, width), 0) & 3
        for axis_id in range(3):
            pattern = jnp.zeros((8, width), f32)
            for direction in range(3):
                at = 3 * axis_id + direction
                pattern = jnp.where(place == direction + 1, geometry[at : at + 1, :], pattern)
            slope = slopes[ROWS * axis_id : ROWS * axis_id + ROWS].reshape(ROWS // 8, 8, width)
            total = total - (slope * pattern[None]).reshape(ROWS, width)
        rates[...] = total
        keep = lax.broadcasted_iota(jnp.int32, (1, width), 1) + first < live_ref[0]
        for node in range(NODES):
            rate = rates[4 * node : 4 * node + 4, :]
            residue_next = section_decay * residue_ref[node] + time_step * rate
            fields_next = fields_ref[node] + section_gain * residue_next
            fields_next = jnp.where(keep, fields_next, 0.0)
            fields_out[node] = fields_next
            residue_out[node] = jnp.where(keep, residue_next, 0.0)
            pressure[node : node + 1, :] = fields_next[0:1]
        parts = jnp.concatenate(thirds(pressure[...]), axis=0)
        slots = lax.broadcasted_iota(jnp.int32, (width, elems_ref.shape[1]), 0) + first
        picks = jnp.where(slots == elems_ref[...], 1.0, 0.0).astype(bf16)
        sampled[...] += product(parts, picks)

    @pl.when(step == 0)
    def _():
        stacked[...] = jnp.zeros_like(stacked)
        combined[...] = jnp.zeros_like(combined)
        slow[...] = jnp.zeros_like(slow)
        pressure[...] = jnp.zeros_like(pressure)
        sampled[...] = jnp.zeros_like(sampled)
        monomials[...] = jnp.zeros_like(monomials)
        remote[...] = jnp.zeros_like(remote)
        count = right_ref.shape[2]
        sources = [
            left_ref[2],
            above_ref[1],
            right_ref[2],
            left_ref[0],
            right_ref[0],
            left_ref[1],
            below_ref[1],
            right_ref[1],
        ]
        for heading in range(8):
            remote[:, count * heading : count * heading + count] = sources[heading]
        gather()

    @pl.when((step > 0) & ((step - 1) * width < 8 * right_ref.shape[2]))
    def _():
        lanes = pl.ds(pl.multiple_of((step - 1) * width, width), width)
        for face in range(4):
            rows = slice(FACE_ROWS * face, FACE_ROWS * face + FACE_ROWS)
            total = -remote[0:16, lanes]
            for axis_id in range(3):
                facing = normals_ref[axis_id, face : face + 1, :]
                total = total + facing * remote[16 + 16 * axis_id : 32 + 16 * axis_id, lanes]
            is_remote = codes_ref[face : face + 1, :] >= slot_faces
            outer[rows, :] = jnp.where(is_remote, total, outer[rows, :])

    @pl.when((step > 0) & (step < last))
    def _():
        update(gather)

    @pl.when(step == last)
    def _():
        update(lambda: None)
        ladders = []
        for axis_id in range(3):
            base = coords_ref[axis_id : axis_id + 1, :]
            square = base * base
            ladders.append([jnp.ones_like(base), base, square, square * base, square * square])
        for node in range(NODES):
            exps = [int(entry) for entry in powers[node]]
            monomials[node : node + 1, :] = (
                ladders[0][exps[0]] * ladders[1][exps[1]] * ladders[2][exps[2]]
            )
        basis = jnp.dot(
            inverse_ref[...], monomials[...], precision=highest, preferred_element_type=f32
        )
        gathered = sampled[0:PAD, :] + sampled[48 : 48 + PAD, :] + sampled[96 : 96 + PAD, :]
        values = jnp.sum(basis * gathered, axis=0, keepdims=True)
        ids = ids_ref[...]
        owner = lax.shift_right_logical(ids * 5243, 20)
        place = ids - group * owner
        owners = lax.broadcasted_iota(jnp.int32, (spread_ref.shape[0], ids.shape[1]), 0)
        held = jnp.where(owners == owner, values, 0.0)
        places = lax.broadcasted_iota(jnp.int32, (spread_ref.shape[2], ids.shape[1]), 0)
        chosen = jnp.where(places == place, 1.0, 0.0).astype(bf16)
        spread = jnp.zeros((spread_ref.shape[0], spread_ref.shape[2]), f32)
        for part in thirds(held):
            spread = spread + product(part, chosen, ((1,), (1,)))
        spread_ref[:, 0, :] = spread


def harmonic_kernel(received_ref, table_ref, groups_ref, out_ref):
    mine = jnp.sum(received_ref[...], axis=0)
    weighted = groups_ref[...] * mine
    out_ref[...] = lax.dot_general(
        weighted,
        table_ref[...],
        (((1,), (1,)), ((), ())),
        precision=highest,
        preferred_element_type=f32,
    )


def fixed(shape):
    return pl.BlockSpec(shape, lambda *_: (0,) * len(shape))


def local(
    fields,
    residue,
    geometry,
    normals,
    face_scale,
    neighbours,
    send_faces,
    live_counts,
    sample_ids,
    sample_elems,
    sample_coords,
):
    const = constant_tables()
    fields = jnp.transpose(fields, (1, 0, 2))
    residue = jnp.transpose(residue, (1, 0, 2))
    slot_count = fields.shape[2]
    slot_faces = 4 * slot_count
    bound_count = send_faces.shape[1]
    reach = 8 * bound_count
    samples = sample_ids.shape[0]
    devices = lax.axis_size(("px", "py"))
    shape = jax.ShapeDtypeStruct

    up, down, left, right = pl.pallas_call(
        functools.partial(pack_kernel, slot_faces),
        grid=(1,),
        in_specs=[
            pl.BlockSpec((NODES, 4, reach), lambda t: (0, 0, 0)),
            pl.BlockSpec((4, reach), lambda t: (0, 0)),
            fixed((256, ROWS)),
        ],
        out_specs=[
            fixed((3, 64, bound_count)),
            fixed((3, 64, bound_count)),
            fixed((64, bound_count)),
            fixed((64, bound_count)),
        ],
        out_shape=[
            shape((3, 64, bound_count), f32),
            shape((3, 64, bound_count), f32),
            shape((64, bound_count), f32),
            shape((64, bound_count), f32),
        ],
        scratch_shapes=[pltpu.VMEM((reach // LANES, ROWS, LANES), f32)],
        compiler_params=pltpu.CompilerParams(vmem_limit_bytes=16 << 20),
        name="pack",
    )(fields, neighbours, const["trace_select"])

    def steps_along(axis):
        count = lax.axis_size(axis)
        forward = [(i, i + 1) for i in range(count - 1)]
        return forward, [(target, source) for source, target in forward]

    forward, backward = steps_along("px")
    below = lax.ppermute(up, "px", backward)
    above = lax.ppermute(down, "px", forward)

    width = 768
    table, packed = pl.pallas_call(
        functools.partial(table_kernel, slot_faces),
        grid=(slot_count // width,),
        in_specs=[
            pl.BlockSpec((NODES, 4, width), lambda t: (0, 0, t)),
            pl.BlockSpec((4, width), lambda t: (0, t)),
            fixed((ROWS, 4 * LANES)),
        ],
        out_specs=[
            pl.BlockSpec((4, width, LANES), lambda t: (0, t, 0)),
            pl.BlockSpec((2, width), lambda t: (0, t)),
        ],
        out_shape=[
            shape((4, slot_count, LANES), f32),
            shape((2, slot_count), jnp.int32),
        ],
        scratch_shapes=[pltpu.VMEM((width // LANES, ROWS, LANES), f32)],
        compiler_params=pltpu.CompilerParams(vmem_limit_bytes=24 << 20),
        name="table",
    )(fields, neighbours, const["table_select"])
    table = table.reshape(slot_faces, LANES)

    forward, backward = steps_along("py")
    to_left = jnp.concatenate([left[None], below[0:1], above[0:1]])
    to_right = jnp.concatenate([right[None], below[2:3], above[2:3]])
    from_right = lax.ppermute(to_left, "py", backward)
    from_left = lax.ppermute(to_right, "py", forward)

    width = 512
    steps = slot_count // width

    def behind(rank):
        return lambda t, *_: (0,) * rank + (jnp.maximum(t - 1, 0),)

    def ahead(rank):
        return lambda t, *_: (0,) * rank + (jnp.minimum(t, steps - 1),)

    fields_next, residue_next, spread = pl.pallas_call(
        functools.partial(section_kernel, slot_count, const["powers"], samples),
        grid_spec=pltpu.PrefetchScalarGridSpec(
            num_scalar_prefetch=2,
            grid=(steps + 1,),
            in_specs=[
                pl.BlockSpec(memory_space=pltpu.VMEM),
                pl.BlockSpec((3, 4, width), ahead(2)),
                pl.BlockSpec((NODES, 4, width), behind(2)),
                pl.BlockSpec((NODES, 4, width), behind(2)),
                pl.BlockSpec((9, width), behind(1)),
                pl.BlockSpec((3, 4, width), behind(2)),
                pl.BlockSpec((4, width), behind(1)),
                pl.BlockSpec((4, width), behind(1)),
                fixed((3, 64, bound_count)),
                fixed((3, 64, bound_count)),
                fixed((3, 64, bound_count)),
                fixed((3, 64, bound_count)),
                fixed((1, samples)),
                fixed((1, samples)),
                fixed((3, samples)),
                fixed((256, ROWS)),
                fixed((ROWS, 256)),
                fixed((3 * ROWS, 96)),
                fixed((2 * ROWS, 256)),
                fixed((PAD, PAD)),
            ],
            out_specs=[
                pl.BlockSpec((NODES, 4, width), behind(2)),
                pl.BlockSpec((NODES, 4, width), behind(2)),
                fixed((devices, 1, samples)),
            ],
            scratch_shapes=[
                pltpu.VMEM((width // LANES, ROWS, LANES), f32),
                pltpu.VMEM((128, width), f32),
                pltpu.VMEM((48, width), f32),
                pltpu.VMEM((ROWS, width), f32),
                pltpu.VMEM((64, pl.cdiv(reach, width) * width), f32),
                pltpu.VMEM((64, width), f32),
                pltpu.VMEM((144, samples), f32),
                pltpu.VMEM((48, width), f32),
                pltpu.VMEM((PAD, samples), f32),
                pltpu.VMEM((LANES, LANES), f32),
                pltpu.VMEM((LANES, LANES), f32),
            ],
        ),
        out_shape=[
            shape(fields.shape, f32),
            shape(residue.shape, f32),
            shape((devices, 1, samples), f32),
        ],
        compiler_params=pltpu.CompilerParams(vmem_limit_bytes=32 << 20),
        name="section",
    )(
        packed.reshape(-1),
        live_counts,
        table,
        normals,
        fields,
        residue,
        geometry,
        normals,
        face_scale,
        neighbours,
        from_right,
        from_left,
        below,
        above,
        sample_elems.reshape(1, samples),
        sample_ids.reshape(1, samples),
        sample_coords,
        const["trace_select"],
        const["into_p"],
        const["from_p"],
        const["lift"],
        const["inverse"],
    )
    received = lax.all_to_all(spread, ("px", "py"), 0, 0, tiled=True)

    receivers = samples // QPTS
    harmonic = np.tile(harmonic_table(), (1, receivers)).astype(np.float32)
    groups = (np.arange(samples)[None] // QPTS == np.arange(receivers)[:, None]).astype(np.float32)
    coefficients = pl.pallas_call(
        harmonic_kernel,
        out_shape=shape((receivers, harmonic.shape[0]), f32),
        name="harmonic",
    )(received, jnp.asarray(harmonic), jnp.asarray(groups))
    return (
        jnp.transpose(fields_next, (1, 0, 2)),
        jnp.transpose(residue_next, (1, 0, 2)),
        coefficients.T,
    )


def solution(mesh):
    placed = (
        P(None, None, ("px", "py")),
        P(None, None, ("px", "py")),
        P(None, ("px", "py")),
        P(None, None, ("px", "py")),
        P(None, ("px", "py")),
        P(None, ("px", "py")),
        P(None, ("px", "py")),
        P(("px", "py")),
        P(("px", "py")),
        P(("px", "py")),
        P(None, ("px", "py")),
    )
    return jax.shard_map(
        local,
        mesh=mesh,
        in_specs=placed,
        out_specs=(P(None, None, ("px", "py")), P(None, None, ("px", "py")), P(None, ("px", "py"))),
        check_vma=False,
    )
```

```python
import functools
import math

import jax
import jax.numpy as jnp
import numpy as np
from jax import lax
from jax.experimental import pallas as pl
from jax.experimental.pallas import tpu as pltpu
from jax.sharding import PartitionSpec as P

QPTS = 50
NODES = 35
PAD = 40
FACE_ROWS = 16
ROWS = 144
LANES = 128


highest = lax.Precision.HIGHEST
section_decay = -567301805773.0 / 1357537059087.0
section_gain = 5161836677717.0 / 13612068292357.0
time_step = 0.01
f32 = jnp.float32
bf16 = jnp.bfloat16


def exponent_table():
    listing = []
    for degree in range(5):
        for third in range(degree + 1):
            for second in range(degree + 1 - third):
                listing.append((degree - second - third, second, third))
    return np.array(listing)


def factorials(values):
    lookup = np.array([float(math.factorial(level)) for level in range(24)])
    return lookup[values]


def eliminate(matrix, right_hand):
    order_size = matrix.shape[0]
    work = np.concatenate([matrix, right_hand], axis=1).astype(float)
    for pivot_col in range(order_size):
        best = max(range(pivot_col, order_size), key=lambda row_id: abs(work[row_id, pivot_col]))
        work[[pivot_col, best]] = work[[best, pivot_col]]
        work[pivot_col] = work[pivot_col] / work[pivot_col, pivot_col]
        for row_id in range(order_size):
            if row_id != pivot_col:
                work[row_id] = work[row_id] - work[row_id, pivot_col] * work[pivot_col]
    return work[:, order_size:]


def element_tables():
    powers = exponent_table()
    points = powers / 4.0
    vander = np.prod(points[:, None, :] ** powers[None, :, :], axis=2)
    inverse = eliminate(vander, np.eye(35))
    derivs = []
    for axis_id in range(3):
        lowered = np.maximum(powers - (np.arange(3) == axis_id)[None, :], 0)
        slope_table = powers[None, :, axis_id] * np.prod(
            points[:, None, :] ** lowered[None, :, :], axis=2
        )
        derivs.append(slope_table @ inverse)
    summed = powers[:, None, :] + powers[None, :, :]
    exp_r = summed[..., 0]
    exp_s = summed[..., 1]
    exp_t = summed[..., 2]
    volume = (
        factorials(exp_r)
        * factorials(exp_s)
        * factorials(exp_t)
        / factorials(exp_r + exp_s + exp_t + 3)
    )
    mass_matrix = inverse.T @ volume @ inverse
    face_grams = [
        np.where(
            exp_t == 0, factorials(exp_r) * factorials(exp_s) / factorials(exp_r + exp_s + 2), 0.0
        ),
        np.where(
            exp_s == 0, factorials(exp_r) * factorials(exp_t) / factorials(exp_r + exp_t + 2), 0.0
        ),
        factorials(exp_r)
        * factorials(exp_s)
        * factorials(exp_t)
        / factorials(exp_r + exp_s + exp_t + 2),
        np.where(
            exp_r == 0, factorials(exp_s) * factorials(exp_t) / factorials(exp_s + exp_t + 2), 0.0
        ),
    ]
    listed = [tuple((int(entry) for entry in powers[node_id])) for node_id in range(35)]
    face_nodes = np.array(
        [
            [node_id for node_id in range(35) if listed[node_id][2] == 0],
            [node_id for node_id in range(35) if listed[node_id][1] == 0],
            [node_id for node_id in range(35) if sum(listed[node_id]) == 4],
            [node_id for node_id in range(35) if listed[node_id][0] == 0],
        ]
    )
    surface = np.zeros((35, 60))
    for face_id in range(4):
        face_mass = inverse.T @ face_grams[face_id] @ inverse
        for node_id in range(15):
            surface[:, 4 * node_id + face_id] = face_mass[:, face_nodes[face_id, node_id]]
    lifting = eliminate(mass_matrix, surface)
    return (np.stack(derivs), lifting, face_nodes, inverse, powers)


def associated(degree, order, cosine, sine):
    current = cosine * 0.0 + 1.0
    for step_id in range(1, order + 1):
        current = -(2 * step_id - 1) * sine * current
    if degree == order:
        return current
    following = cosine * (2 * order + 1) * current
    for level in range(order + 2, degree + 1):
        current, following = (
            following,
            ((2 * level - 1) * cosine * following - (level + order - 1) * current)
            / (level - order),
        )
    return following


def harmonic_table():
    inner_node = math.sqrt(5.0 - 2.0 * math.sqrt(10.0 / 7.0)) / 3.0
    outer_node = math.sqrt(5.0 + 2.0 * math.sqrt(10.0 / 7.0)) / 3.0
    inner_weight = (322.0 + 13.0 * math.sqrt(70.0)) / 900.0
    outer_weight = (322.0 - 13.0 * math.sqrt(70.0)) / 900.0
    cosines = np.array([-outer_node, -inner_node, 0.0, inner_node, outer_node])
    weights = np.array([outer_weight, inner_weight, 128.0 / 225.0, inner_weight, outer_weight])
    azimuth = 2.0 * np.pi * (np.arange(10) + 0.5) / 10.0
    polar = np.repeat(cosines, 10)
    circle = np.tile(azimuth, 5)
    point_weight = np.repeat(weights, 10) * 2.0 * np.pi / 10.0
    sine = np.sqrt(1.0 - polar**2)
    table_rows = []
    for degree in range(5):
        for order in range(-degree, degree + 1):
            absolute = abs(order)
            legendre = associated(degree, absolute, polar, sine)
            factor = math.sqrt(
                (2 * degree + 1)
                / (4.0 * math.pi)
                * math.factorial(degree - absolute)
                / math.factorial(degree + absolute)
            )
            if order > 0:
                angular = math.sqrt(2.0) * np.cos(order * circle)
            elif order < 0:
                angular = math.sqrt(2.0) * np.sin(absolute * circle)
            else:
                angular = circle * 0.0 + 1.0
            table_rows.append(factor * legendre * angular * point_weight)
    return np.array(table_rows)


def constant_tables():
    derivs, lifting, face_nodes, inverse, powers = element_tables()
    table_select = np.zeros((ROWS, 4 * LANES), np.float32)
    trace_select = np.zeros((4 * 4 * FACE_ROWS, ROWS), np.float32)
    for face in range(4):
        for field in range(4):
            for place in range(15):
                source = 4 * face_nodes[face, place] + field
                column = FACE_ROWS * field + place
                table_select[source, LANES * face + column] = 1.0
                table_select[source, LANES * face + 64 + column] = 1.0
                trace_select[64 * face + column, source] = 1.0
    whole = np.round(3.0 * derivs)
    into_p = np.zeros((ROWS, 128), np.float32)
    from_p = np.zeros((3 * ROWS, 48), np.float32)
    lift = np.zeros((ROWS, 256), np.float32)
    for node in range(NODES):
        for axis_id in range(3):
            into_p[4 * node, PAD * axis_id : PAD * axis_id + NODES] = -whole[axis_id, node]
            for field in range(1, 4):
                from_p[ROWS * axis_id + 4 * node + field, :NODES] = whole[axis_id, node]
        for face in range(4):
            for place in range(15):
                entry = lifting[node, 4 * place + face]
                column = FACE_ROWS * face + place
                lift[4 * node, column] = entry
                for field in range(1, 4):
                    lift[4 * node + field, 64 * field + column] = -entry
    lift_hi = lift.astype(jnp.bfloat16)
    lift_lo = (lift - lift_hi.astype(np.float32)).astype(jnp.bfloat16)
    return {
        "table_select": jnp.asarray(table_select, bf16),
        "trace_select": jnp.asarray(trace_select, bf16),
        "into_p": jnp.asarray(np.concatenate([into_p, into_p], axis=1), bf16),
        "from_p": jnp.asarray(np.concatenate([from_p, from_p], axis=1), bf16),
        "lift": jnp.asarray(np.concatenate([lift_hi, lift_lo], axis=0)),
        "inverse": jnp.asarray(np.pad(inverse.T, ((0, 5), (0, 5))), f32),
        "powers": powers,
    }


def halves(values):
    high = values.astype(bf16)
    return high, (values - high.astype(f32)).astype(bf16)


def thirds(values):
    high = values.astype(bf16)
    rest = values - high.astype(f32)
    middle = rest.astype(bf16)
    return high, middle, (rest - middle.astype(f32)).astype(bf16)


def product(left, right, dims=((1,), (0,))):
    return lax.dot_general(left, right, (dims, ((), ())), preferred_element_type=f32)


def stack_nodes(fields_ref, stacked):
    tiles = range(stacked.shape[0])
    for tile in tiles:
        for node in range(NODES):
            stacked[tile, 4 * node : 4 * node + 4, :] = fields_ref[
                node, :, LANES * tile : LANES * tile + LANES
            ]
    return halves(jnp.concatenate([stacked[tile] for tile in tiles], axis=1))


def one_field(stacked, field):
    tiles = range(stacked.shape[0])
    rows = pl.ds(field, NODES, stride=4)
    return jnp.concatenate([stacked[tile, rows, :] for tile in tiles], axis=1)


def pack_kernel(
    slot_faces,
    fields_ref,
    codes_ref,
    select_ref,
    up_ref,
    down_ref,
    left_ref,
    right_ref,
    packed_ref,
    stacked,
):
    stacked[...] = jnp.zeros_like(stacked)
    high, low = stack_nodes(fields_ref, stacked)
    traces = product(select_ref[...], high) + product(select_ref[...], low)
    width = left_ref.shape[1]
    reach = 8 * width
    chosen = jnp.zeros((64, reach), f32)
    for face in range(4):
        remote = codes_ref[face : face + 1, 0:reach] >= slot_faces
        chosen = jnp.where(remote, traces[64 * face : 64 * face + 64, :], chosen)
    pieces = [chosen[:, width * heading : width * heading + width] for heading in range(8)]
    for place in range(3):
        up_ref[place] = pieces[place]
        down_ref[place] = pieces[5 + place]
    left_ref[...] = pieces[3]
    right_ref[...] = pieces[4]
    tiles = codes_ref.shape[1] // LANES
    for half in range(2):
        codes = codes_ref[2 * half : 2 * half + 2, :]
        codes = jnp.where((codes >= 0) & (codes < slot_faces), codes, 0)
        codes = codes[0:1] + (codes[1:2] << 16)
        for tile in range(tiles):
            row = half * tiles + tile
            packed_ref[row : row + 1, :] = codes[:, LANES * tile : LANES * tile + LANES]


def relay_kernel(left_ref, right_ref, below_ref, above_ref, to_left_ref, to_right_ref):
    to_left_ref[0] = left_ref[...]
    to_left_ref[1] = below_ref[0]
    to_left_ref[2] = above_ref[0]
    to_right_ref[0] = right_ref[...]
    to_right_ref[1] = below_ref[2]
    to_right_ref[2] = above_ref[2]


def build_rows(first, fields_ref, select_ref, table_ref, stacked):
    slot_count = table_ref.shape[0] // 4
    width = fields_ref.shape[2]
    high, low = stack_nodes(fields_ref, stacked)
    for half in range(2):
        select = select_ref[:, 256 * half : 256 * half + 256]
        rows = product(high, select, ((0,), (0,))) + product(low, select, ((0,), (0,)))
        for side in range(2):
            start = pl.multiple_of((2 * half + side) * slot_count + first, width)
            table_ref[pl.ds(start, width), :] = rows[:, LANES * side : LANES * side + LANES]


def gather_pieces(slot_count, first, codes_ref, table_ref, normals_ref, outer_ref, rows_refs):
    width = outer_ref.shape[1]
    left_half = lax.broadcasted_iota(jnp.int32, (1, LANES), 1) < 64

    def load(tile, half, rows):
        base = half * slot_count + first + tile * LANES
        for row in rows:
            code = codes_ref[base + row]
            one = table_ref[pl.ds(code & 0xFFFF, 1), :]
            two = table_ref[pl.ds(lax.shift_right_logical(code, 16), 1), :]
            rows_refs[half][row : row + 1, :] = jnp.where(left_half, one, two)

    def combine(tile, half):
        turned = rows_refs[half][...].T
        lanes = slice(tile * LANES, tile * LANES + LANES)
        for side in range(2):
            face = 2 * half + side
            part = turned[64 * side : 64 * side + 64, :]
            total = -part[0:16]
            for axis_id in range(3):
                facing = normals_ref[axis_id, face : face + 1, lanes]
                total = total + facing * part[16 + 16 * axis_id : 32 + 16 * axis_id]
            outer_ref[FACE_ROWS * face : FACE_ROWS * face + FACE_ROWS, lanes] = total

    for tile in range(width // LANES):
        for half in range(2):
            for part in range(2):
                yield functools.partial(load, tile, half, range(64 * part, 64 * part + 64))
            yield functools.partial(combine, tile, half)


def section_kernel(
    slot_count,
    powers,
    group,
    packed_ref,
    live_ref,
    next_normals_ref,
    fields_ref,
    residue_ref,
    geometry_ref,
    normals_ref,
    scale_ref,
    codes_ref,
    right_ref,
    left_ref,
    below_ref,
    above_ref,
    elems_ref,
    ids_ref,
    coords_ref,
    table_select_ref,
    select_ref,
    into_ref,
    from_ref,
    lift_ref,
    inverse_ref,
    fields_out,
    residue_out,
    spread_ref,
    table_ref,
    stacked,
    combined,
    slow,
    rates,
    remote,
    outer,
    beyond_ref,
    sampled,
    pressure,
    monomials,
    *rows_refs,
):
    width = fields_ref.shape[2]
    tiles = slot_count // width
    step = pl.program_id(0) - tiles
    slot_faces = 4 * slot_count
    half_width = 256

    def gather():
        first = step * width
        return gather_pieces(
            slot_count, first, packed_ref, table_ref, next_normals_ref, outer, rows_refs
        )

    def update_pieces():
        first = (step - 1) * width
        kept = {}

        def inside(at):
            return slice(half_width * at, half_width * at + half_width)

        def traces(at):
            lanes = inside(at)
            for tile in range(2 * at, 2 * at + 2):
                for node in range(NODES):
                    stacked[tile, 4 * node : 4 * node + 4, :] = fields_ref[
                        node, :, LANES * tile : LANES * tile + LANES
                    ]
            high, low = halves(jnp.concatenate([stacked[2 * at], stacked[2 * at + 1]], axis=1))
            inner = product(select_ref[...], high) + product(select_ref[...], low)
            fluxes = []
            for face in range(4):
                inner_p = inner[64 * face : 64 * face + 16]
                along = jnp.zeros_like(inner_p)
                for axis_id in range(3):
                    facing = normals_ref[axis_id, face : face + 1, lanes]
                    start = 64 * face + 16 + 16 * axis_id
                    along = along + facing * inner[start : start + 16]
                wall = codes_ref[face : face + 1, lanes] < 0
                beyond = beyond_ref[FACE_ROWS * face : FACE_ROWS * face + FACE_ROWS, lanes]
                beyond = jnp.where(wall, -along - inner_p, beyond)
                scale = 0.5 * scale_ref[face : face + 1, lanes]
                fluxes.append(scale * (along - inner_p - beyond))
            kept[at] = fluxes

        def lift(at):
            lanes = inside(at)
            fluxes = kept.pop(at)
            columns = list(fluxes)
            for axis_id in range(3):
                for face in range(4):
                    columns.append(normals_ref[axis_id, face : face + 1, lanes] * fluxes[face])
            flux_hi, flux_lo = halves(jnp.concatenate(columns, axis=0))
            lifted = product(lift_ref[...], flux_hi)
            total = lifted[:ROWS] + lifted[ROWS:] + product(lift_ref[0:ROWS, :], flux_lo)
            rates[:, lanes] = total

        def field_rows(at, field):
            rows = pl.ds(field, NODES, stride=4)
            return jnp.concatenate([stacked[tile, rows, :] for tile in (2 * at, 2 * at + 1)], axis=1)

        def into(at):
            lanes = inside(at)
            geometry = geometry_ref[:, lanes] * (1.0 / 3.0)
            for axis_id in range(3):
                weighted = jnp.zeros((NODES, half_width), f32)
                for direction in range(3):
                    row = 3 * axis_id + direction
                    weighted = weighted + geometry[row : row + 1, :] * field_rows(at, 1 + direction)
                combined[PAD * axis_id : PAD * axis_id + NODES, lanes] = weighted
            parts = jnp.concatenate(halves(combined[:, lanes]), axis=0)
            rates[:, lanes] += product(into_ref[...], parts)

        def slopes(at):
            lanes = inside(at)
            geometry = geometry_ref[:, lanes] * (1.0 / 3.0)
            slow[0:NODES, lanes] = field_rows(at, 0)
            parts = jnp.concatenate(halves(slow[:, lanes]), axis=0)
            place = lax.broadcasted_iota(jnp.int32, (8, half_width), 0) & 3
            total = rates[:, lanes]
            for axis_id in range(3):
                slope = product(from_ref[ROWS * axis_id : ROWS * axis_id + ROWS, :], parts)
                pattern = jnp.zeros((8, half_width), f32)
                for direction in range(3):
                    row = 3 * axis_id + direction
                    pattern = jnp.where(place == direction + 1, geometry[row : row + 1, :], pattern)
                slope = slope.reshape(ROWS // 8, 8, half_width) * pattern[None]
                total = total - slope.reshape(ROWS, half_width)
            rates[:, lanes] = total

        def advance(at):
            lanes = inside(at)
            slots = lax.broadcasted_iota(jnp.int32, (1, half_width), 1) + (first + half_width * at)
            keep = slots < live_ref[0]
            for node in range(NODES):
                rate = rates[4 * node : 4 * node + 4, lanes]
                residue_next = section_decay * residue_ref[node, :, lanes] + time_step * rate
                fields_next = fields_ref[node, :, lanes] + section_gain * residue_next
                fields_next = jnp.where(keep, fields_next, 0.0)
                fields_out[node, :, lanes] = fields_next
                residue_out[node, :, lanes] = jnp.where(keep, residue_next, 0.0)
                pressure[node : node + 1, lanes] = fields_next[0:1]

        def sample(at):
            lanes = inside(at)
            parts = jnp.concatenate(thirds(pressure[:, lanes]), axis=0)
            start = first + half_width * at
            slots = lax.broadcasted_iota(jnp.int32, (half_width, elems_ref.shape[1]), 0) + start
            picks = jnp.where(slots == elems_ref[...], 1.0, 0.0).astype(bf16)
            sampled[...] += product(parts, picks)

        for at in range(width // half_width):
            for piece in (traces, lift, into, slopes, advance, sample):
                yield functools.partial(piece, at)

    def interleave(gathers, updates):
        gathers, updates = list(gathers), list(updates)
        done = 0
        for at, piece in enumerate(gathers):
            piece()
            upto = (at + 1) * len(updates) // len(gathers)
            for other in updates[done:upto]:
                other()
            done = upto

    @pl.when(step == -tiles)
    def _():
        stacked[...] = jnp.zeros_like(stacked)
        combined[...] = jnp.zeros_like(combined)
        slow[...] = jnp.zeros_like(slow)
        pressure[...] = jnp.zeros_like(pressure)
        sampled[...] = jnp.zeros_like(sampled)
        monomials[...] = jnp.zeros_like(monomials)
        remote[...] = jnp.zeros_like(remote)
        count = right_ref.shape[2]
        sources = [
            left_ref[2],
            above_ref[1],
            right_ref[2],
            left_ref[0],
            right_ref[0],
            left_ref[1],
            below_ref[1],
            right_ref[1],
        ]
        for heading in range(8):
            remote[:, count * heading : count * heading + count] = sources[heading]

    @pl.when(step < 0)
    def _():
        build_rows((step + tiles) * width, fields_ref, table_select_ref, table_ref, stacked)

    @pl.when(step == 0)
    def _():
        for piece in gather():
            piece()

    @pl.when((step > 0) & ((step - 1) * width < 8 * right_ref.shape[2]))
    def _():
        lanes = pl.ds(pl.multiple_of((step - 1) * width, width), width)
        for face in range(4):
            rows = slice(FACE_ROWS * face, FACE_ROWS * face + FACE_ROWS)
            total = -remote[0:16, lanes]
            for axis_id in range(3):
                facing = normals_ref[axis_id, face : face + 1, :]
                total = total + facing * remote[16 + 16 * axis_id : 32 + 16 * axis_id, lanes]
            is_remote = codes_ref[face : face + 1, :] >= slot_faces
            outer[rows, :] = jnp.where(is_remote, total, outer[rows, :])

    @pl.when((step > 0) & (step < tiles))
    def _():
        beyond_ref[...] = outer[...]
        interleave(gather(), update_pieces())

    @pl.when(step == tiles)
    def _():
        beyond_ref[...] = outer[...]
        for piece in update_pieces():
            piece()
        ladders = []
        for axis_id in range(3):
            base = coords_ref[axis_id : axis_id + 1, :]
            square = base * base
            ladders.append([jnp.ones_like(base), base, square, square * base, square * square])
        for node in range(NODES):
            exps = [int(entry) for entry in powers[node]]
            monomials[node : node + 1, :] = (
                ladders[0][exps[0]] * ladders[1][exps[1]] * ladders[2][exps[2]]
            )
        basis = jnp.dot(
            inverse_ref[...], monomials[...], precision=highest, preferred_element_type=f32
        )
        gathered = sampled[0:PAD, :] + sampled[48 : 48 + PAD, :] + sampled[96 : 96 + PAD, :]
        values = jnp.sum(basis * gathered, axis=0, keepdims=True)
        ids = ids_ref[...]
        owner = lax.shift_right_logical(ids * 5243, 20)
        place = ids - group * owner
        owners = lax.broadcasted_iota(jnp.int32, (spread_ref.shape[0], ids.shape[1]), 0)
        held = jnp.where(owners == owner, values, 0.0)
        places = lax.broadcasted_iota(jnp.int32, (spread_ref.shape[2], ids.shape[1]), 0)
        chosen = jnp.where(places == place, 1.0, 0.0).astype(bf16)
        spread = jnp.zeros((spread_ref.shape[0], spread_ref.shape[2]), f32)
        for part in thirds(held):
            spread = spread + product(part, chosen, ((1,), (1,)))
        spread_ref[:, 0, :] = spread


def harmonic_kernel(received_ref, table_ref, groups_ref, out_ref):
    mine = jnp.sum(received_ref[...], axis=0)
    weighted = groups_ref[...] * mine
    out_ref[...] = lax.dot_general(
        weighted,
        table_ref[...],
        (((1,), (1,)), ((), ())),
        precision=highest,
        preferred_element_type=f32,
    )


def in_hbm(array):
    return pltpu.with_memory_space_constraint(array, pltpu.HBM)


def fixed(shape):
    return pl.BlockSpec(shape, lambda *_: (0,) * len(shape))


def local(
    fields,
    residue,
    geometry,
    normals,
    face_scale,
    neighbours,
    send_faces,
    live_counts,
    sample_ids,
    sample_elems,
    sample_coords,
):
    const = {
        name: in_hbm(table) if isinstance(table, jax.Array) else table
        for name, table in constant_tables().items()
    }
    fields = in_hbm(jnp.transpose(fields, (1, 0, 2)))
    residue = in_hbm(jnp.transpose(residue, (1, 0, 2)))
    geometry, normals, face_scale = in_hbm(geometry), in_hbm(normals), in_hbm(face_scale)
    neighbours, sample_coords = in_hbm(neighbours), in_hbm(sample_coords)
    slot_count = fields.shape[2]
    slot_faces = 4 * slot_count
    bound_count = send_faces.shape[1]
    reach = 8 * bound_count
    samples = sample_ids.shape[0]
    devices = lax.axis_size(("px", "py"))
    shape = jax.ShapeDtypeStruct

    width = 512
    tiles = slot_count // width
    piece = (3, 64, bound_count)

    up, down, left, right, packed = pl.pallas_call(
        functools.partial(pack_kernel, slot_faces),
        grid=(1,),
        in_specs=[
            pl.BlockSpec((NODES, 4, reach), lambda t: (0, 0, 0)),
            fixed((4, slot_count)),
            fixed((256, ROWS)),
        ],
        out_specs=[
            fixed(piece),
            fixed(piece),
            fixed(piece[1:]),
            fixed(piece[1:]),
            fixed((2 * slot_count // LANES, LANES)),
        ],
        out_shape=[
            shape(piece, f32),
            shape(piece, f32),
            shape(piece[1:], f32),
            shape(piece[1:], f32),
            shape((2 * slot_count // LANES, LANES), jnp.int32),
        ],
        scratch_shapes=[pltpu.VMEM((reach // LANES, ROWS, LANES), f32)],
        compiler_params=pltpu.CompilerParams(vmem_limit_bytes=16 << 20),
        name="pack",
    )(fields, neighbours, const["trace_select"])

    def steps_along(axis):
        count = lax.axis_size(axis)
        forward = [(i, i + 1) for i in range(count - 1)]
        return forward, [(target, source) for source, target in forward]

    forward, backward = steps_along("px")
    below = in_hbm(lax.ppermute(up, "px", backward))
    above = in_hbm(lax.ppermute(down, "px", forward))
    to_left, to_right = pl.pallas_call(
        relay_kernel,
        out_shape=[shape(piece, f32), shape(piece, f32)],
        name="relay",
    )(in_hbm(left), in_hbm(right), below, above)
    forward, backward = steps_along("py")
    from_right = in_hbm(lax.ppermute(to_left, "py", backward))
    from_left = in_hbm(lax.ppermute(to_right, "py", forward))

    def behind(rank):
        return lambda t, *_: (0,) * rank + (jnp.maximum(t - tiles - 1, 0),)

    def ahead(rank):
        return lambda t, *_: (0,) * rank + (jnp.clip(t - tiles, 0, tiles - 1),)

    def twice(t, *_):
        return (0, 0, jnp.where(t < tiles, t, jnp.maximum(t - tiles - 1, 0)))

    fields_next, residue_next, spread = pl.pallas_call(
        functools.partial(section_kernel, slot_count, const["powers"], samples),
        grid_spec=pltpu.PrefetchScalarGridSpec(
            num_scalar_prefetch=2,
            grid=(2 * tiles + 1,),
            in_specs=[
                pl.BlockSpec((3, 4, width), ahead(2)),
                pl.BlockSpec((NODES, 4, width), twice),
                pl.BlockSpec((NODES, 4, width), behind(2)),
                pl.BlockSpec((9, width), behind(1)),
                pl.BlockSpec((3, 4, width), behind(2)),
                pl.BlockSpec((4, width), behind(1)),
                pl.BlockSpec((4, width), behind(1)),
                fixed(piece),
                fixed(piece),
                fixed(piece),
                fixed(piece),
                fixed((1, samples)),
                fixed((1, samples)),
                fixed((3, samples)),
                fixed((ROWS, 4 * LANES)),
                fixed((256, ROWS)),
                fixed((ROWS, 256)),
                fixed((3 * ROWS, 96)),
                fixed((2 * ROWS, 256)),
                fixed((PAD, PAD)),
            ],
            out_specs=[
                pl.BlockSpec((NODES, 4, width), behind(2)),
                pl.BlockSpec((NODES, 4, width), behind(2)),
                fixed((devices, 1, samples)),
            ],
            scratch_shapes=[
                pltpu.VMEM((slot_faces, LANES), f32),
                pltpu.VMEM((width // LANES, ROWS, LANES), f32),
                pltpu.VMEM((128, width), f32),
                pltpu.VMEM((48, width), f32),
                pltpu.VMEM((ROWS, width), f32),
                pltpu.VMEM((64, pl.cdiv(reach, width) * width), f32),
                pltpu.VMEM((64, width), f32),
                pltpu.VMEM((64, width), f32),
                pltpu.VMEM((144, samples), f32),
                pltpu.VMEM((48, width), f32),
                pltpu.VMEM((PAD, samples), f32),
                pltpu.VMEM((LANES, LANES), f32),
                pltpu.VMEM((LANES, LANES), f32),
            ],
        ),
        out_shape=[
            shape(fields.shape, f32),
            shape(residue.shape, f32),
            shape((devices, 1, samples), f32),
        ],
        compiler_params=pltpu.CompilerParams(vmem_limit_bytes=48 << 20),
        name="section",
    )(
        packed.reshape(-1),
        live_counts,
        normals,
        fields,
        residue,
        geometry,
        normals,
        face_scale,
        neighbours,
        from_right,
        from_left,
        below,
        above,
        in_hbm(sample_elems.reshape(1, samples)),
        in_hbm(sample_ids.reshape(1, samples)),
        sample_coords,
        const["table_select"],
        const["trace_select"],
        const["into_p"],
        const["from_p"],
        const["lift"],
        const["inverse"],
    )
    received = lax.all_to_all(spread, ("px", "py"), 0, 0, tiled=True)

    receivers = samples // QPTS
    harmonic = np.tile(harmonic_table(), (1, receivers)).astype(np.float32)
    groups = (np.arange(samples)[None] // QPTS == np.arange(receivers)[:, None]).astype(np.float32)
    coefficients = pl.pallas_call(
        harmonic_kernel,
        out_shape=shape((receivers, harmonic.shape[0]), f32),
        name="harmonic",
    )(received, jnp.asarray(harmonic), jnp.asarray(groups))
    return (
        jnp.transpose(fields_next, (1, 0, 2)),
        jnp.transpose(residue_next, (1, 0, 2)),
        coefficients.T,
    )


def solution(mesh):
    placed = (
        P(None, None, ("px", "py")),
        P(None, None, ("px", "py")),
        P(None, ("px", "py")),
        P(None, None, ("px", "py")),
        P(None, ("px", "py")),
        P(None, ("px", "py")),
        P(None, ("px", "py")),
        P(("px", "py")),
        P(("px", "py")),
        P(("px", "py")),
        P(None, ("px", "py")),
    )
    return jax.shard_map(
        local,
        mesh=mesh,
        in_specs=placed,
        out_specs=(P(None, None, ("px", "py")), P(None, None, ("px", "py")), P(None, ("px", "py"))),
        check_vma=False,
    )
```

```python
import functools
import math

import jax
import jax.numpy as jnp
import numpy as np
from jax import lax
from jax.experimental import pallas as pl
from jax.experimental.pallas import tpu as pltpu
from jax.sharding import PartitionSpec as P

QPTS = 50
NODES = 35
PAD = 40
FACE_ROWS = 16
ROWS = 144
LANES = 128


highest = lax.Precision.HIGHEST
section_decay = -567301805773.0 / 1357537059087.0
section_gain = 5161836677717.0 / 13612068292357.0
time_step = 0.01
f32 = jnp.float32
bf16 = jnp.bfloat16


def exponent_table():
    listing = []
    for degree in range(5):
        for third in range(degree + 1):
            for second in range(degree + 1 - third):
                listing.append((degree - second - third, second, third))
    return np.array(listing)


def factorials(values):
    lookup = np.array([float(math.factorial(level)) for level in range(24)])
    return lookup[values]


def eliminate(matrix, right_hand):
    order_size = matrix.shape[0]
    work = np.concatenate([matrix, right_hand], axis=1).astype(float)
    for pivot_col in range(order_size):
        best = max(range(pivot_col, order_size), key=lambda row_id: abs(work[row_id, pivot_col]))
        work[[pivot_col, best]] = work[[best, pivot_col]]
        work[pivot_col] = work[pivot_col] / work[pivot_col, pivot_col]
        for row_id in range(order_size):
            if row_id != pivot_col:
                work[row_id] = work[row_id] - work[row_id, pivot_col] * work[pivot_col]
    return work[:, order_size:]


def element_tables():
    powers = exponent_table()
    points = powers / 4.0
    vander = np.prod(points[:, None, :] ** powers[None, :, :], axis=2)
    inverse = eliminate(vander, np.eye(35))
    derivs = []
    for axis_id in range(3):
        lowered = np.maximum(powers - (np.arange(3) == axis_id)[None, :], 0)
        slope_table = powers[None, :, axis_id] * np.prod(
            points[:, None, :] ** lowered[None, :, :], axis=2
        )
        derivs.append(slope_table @ inverse)
    summed = powers[:, None, :] + powers[None, :, :]
    exp_r = summed[..., 0]
    exp_s = summed[..., 1]
    exp_t = summed[..., 2]
    volume = (
        factorials(exp_r)
        * factorials(exp_s)
        * factorials(exp_t)
        / factorials(exp_r + exp_s + exp_t + 3)
    )
    mass_matrix = inverse.T @ volume @ inverse
    face_grams = [
        np.where(
            exp_t == 0, factorials(exp_r) * factorials(exp_s) / factorials(exp_r + exp_s + 2), 0.0
        ),
        np.where(
            exp_s == 0, factorials(exp_r) * factorials(exp_t) / factorials(exp_r + exp_t + 2), 0.0
        ),
        factorials(exp_r)
        * factorials(exp_s)
        * factorials(exp_t)
        / factorials(exp_r + exp_s + exp_t + 2),
        np.where(
            exp_r == 0, factorials(exp_s) * factorials(exp_t) / factorials(exp_s + exp_t + 2), 0.0
        ),
    ]
    listed = [tuple((int(entry) for entry in powers[node_id])) for node_id in range(35)]
    face_nodes = np.array(
        [
            [node_id for node_id in range(35) if listed[node_id][2] == 0],
            [node_id for node_id in range(35) if listed[node_id][1] == 0],
            [node_id for node_id in range(35) if sum(listed[node_id]) == 4],
            [node_id for node_id in range(35) if listed[node_id][0] == 0],
        ]
    )
    surface = np.zeros((35, 60))
    for face_id in range(4):
        face_mass = inverse.T @ face_grams[face_id] @ inverse
        for node_id in range(15):
            surface[:, 4 * node_id + face_id] = face_mass[:, face_nodes[face_id, node_id]]
    lifting = eliminate(mass_matrix, surface)
    return (np.stack(derivs), lifting, face_nodes, inverse, powers)


def associated(degree, order, cosine, sine):
    current = cosine * 0.0 + 1.0
    for step_id in range(1, order + 1):
        current = -(2 * step_id - 1) * sine * current
    if degree == order:
        return current
    following = cosine * (2 * order + 1) * current
    for level in range(order + 2, degree + 1):
        current, following = (
            following,
            ((2 * level - 1) * cosine * following - (level + order - 1) * current)
            / (level - order),
        )
    return following


def harmonic_table():
    inner_node = math.sqrt(5.0 - 2.0 * math.sqrt(10.0 / 7.0)) / 3.0
    outer_node = math.sqrt(5.0 + 2.0 * math.sqrt(10.0 / 7.0)) / 3.0
    inner_weight = (322.0 + 13.0 * math.sqrt(70.0)) / 900.0
    outer_weight = (322.0 - 13.0 * math.sqrt(70.0)) / 900.0
    cosines = np.array([-outer_node, -inner_node, 0.0, inner_node, outer_node])
    weights = np.array([outer_weight, inner_weight, 128.0 / 225.0, inner_weight, outer_weight])
    azimuth = 2.0 * np.pi * (np.arange(10) + 0.5) / 10.0
    polar = np.repeat(cosines, 10)
    circle = np.tile(azimuth, 5)
    point_weight = np.repeat(weights, 10) * 2.0 * np.pi / 10.0
    sine = np.sqrt(1.0 - polar**2)
    table_rows = []
    for degree in range(5):
        for order in range(-degree, degree + 1):
            absolute = abs(order)
            legendre = associated(degree, absolute, polar, sine)
            factor = math.sqrt(
                (2 * degree + 1)
                / (4.0 * math.pi)
                * math.factorial(degree - absolute)
                / math.factorial(degree + absolute)
            )
            if order > 0:
                angular = math.sqrt(2.0) * np.cos(order * circle)
            elif order < 0:
                angular = math.sqrt(2.0) * np.sin(absolute * circle)
            else:
                angular = circle * 0.0 + 1.0
            table_rows.append(factor * legendre * angular * point_weight)
    return np.array(table_rows)


def constant_tables():
    derivs, lifting, face_nodes, inverse, powers = element_tables()
    table_select = np.zeros((ROWS, 4 * LANES), np.float32)
    trace_select = np.zeros((4 * 4 * FACE_ROWS, ROWS), np.float32)
    for face in range(4):
        for field in range(4):
            for place in range(15):
                source = 4 * face_nodes[face, place] + field
                column = FACE_ROWS * field + place
                table_select[source, LANES * face + column] = 1.0
                table_select[source, LANES * face + 64 + column] = 1.0
                trace_select[64 * face + column, source] = 1.0
    whole = np.round(3.0 * derivs)
    into_p = np.zeros((ROWS, 128), np.float32)
    from_p = np.zeros((3 * ROWS, 48), np.float32)
    lift = np.zeros((ROWS, 256), np.float32)
    for node in range(NODES):
        for axis_id in range(3):
            into_p[4 * node, PAD * axis_id : PAD * axis_id + NODES] = -whole[axis_id, node]
            for field in range(1, 4):
                from_p[ROWS * axis_id + 4 * node + field, :NODES] = whole[axis_id, node]
        for face in range(4):
            for place in range(15):
                entry = lifting[node, 4 * place + face]
                column = FACE_ROWS * face + place
                lift[4 * node, column] = entry
                for field in range(1, 4):
                    lift[4 * node + field, 64 * field + column] = -entry
    lift_hi = lift.astype(jnp.bfloat16)
    lift_lo = (lift - lift_hi.astype(np.float32)).astype(jnp.bfloat16)
    return {
        "table_select": jnp.asarray(table_select, bf16),
        "trace_select": jnp.asarray(trace_select, bf16),
        "twice_select": jnp.asarray(np.concatenate([trace_select] * 2, axis=1), bf16),
        "from_p": jnp.asarray(np.concatenate([from_p, from_p], axis=1), bf16),
        "lift": jnp.asarray(
            np.concatenate(
                [lift_hi, lift_lo, lift_hi] + [into_p.astype(jnp.bfloat16)] * 2, axis=1
            )
        ),
        "inverse": jnp.asarray(np.pad(inverse.T, ((0, 5), (0, 5))), f32),
        "powers": powers,
    }


def halves(values):
    high = values.astype(bf16)
    return high, (values - high.astype(f32)).astype(bf16)


def thirds(values):
    high = values.astype(bf16)
    rest = values - high.astype(f32)
    middle = rest.astype(bf16)
    return high, middle, (rest - middle.astype(f32)).astype(bf16)


def product(left, right, dims=((1,), (0,))):
    return lax.dot_general(left, right, (dims, ((), ())), preferred_element_type=f32)


def stack_nodes(fields_ref, stacked):
    tiles = range(stacked.shape[0])
    for tile in tiles:
        for node in range(NODES):
            stacked[tile, 4 * node : 4 * node + 4, :] = fields_ref[
                node, :, LANES * tile : LANES * tile + LANES
            ]
    return halves(jnp.concatenate([stacked[tile] for tile in tiles], axis=1))


def one_field(stacked, field):
    tiles = range(stacked.shape[0])
    rows = pl.ds(field, NODES, stride=4)
    return jnp.concatenate([stacked[tile, rows, :] for tile in tiles], axis=1)


def pack_kernel(
    slot_faces,
    fields_ref,
    codes_ref,
    select_ref,
    up_ref,
    down_ref,
    left_ref,
    right_ref,
    faces_ref,
    stacked,
):
    stacked[...] = jnp.zeros_like(stacked)
    high, low = stack_nodes(fields_ref, stacked)
    traces = product(select_ref[...], high) + product(select_ref[...], low)
    reach = fields_ref.shape[2]
    count = reach // 8
    chosen = jnp.zeros((64, reach), f32)
    for face in range(4):
        remote = codes_ref[face : face + 1, 0:reach] >= slot_faces
        chosen = jnp.where(remote, traces[64 * face : 64 * face + 64, :], chosen)
    homes = [up_ref.at[0], up_ref.at[1], up_ref.at[2], left_ref, right_ref]
    homes += [down_ref.at[0], down_ref.at[1], down_ref.at[2]]
    for heading, home in enumerate(homes):
        part = chosen[:, count * heading : count * heading + count]
        home[:, 0:96] = part[0:48]
        for third in range(3):
            home[16 * third : 16 * third + 16, 96:128] = part[48:64, 32 * third : 32 * third + 32]
    tiles = codes_ref.shape[1] // LANES
    codes = codes_ref[...]
    codes = jnp.where((codes >= 0) & (codes < slot_faces), codes, 0)
    for face in range(4):
        for tile in range(tiles):
            row = face * tiles + tile
            faces_ref[row : row + 1, :] = codes[
                face : face + 1, LANES * tile : LANES * tile + LANES
            ]


def relay_kernel(left_ref, right_ref, below_ref, above_ref, to_left_ref, to_right_ref, middle_ref):
    to_left_ref[0] = left_ref[...]
    to_left_ref[1] = below_ref[0]
    to_left_ref[2] = above_ref[0]
    to_right_ref[0] = right_ref[...]
    to_right_ref[1] = below_ref[2]
    to_right_ref[2] = above_ref[2]
    middle_ref[0] = below_ref[1]
    middle_ref[1] = above_ref[1]


def build_rows(first, part, fields_ref, select_ref, table_ref, stacked):
    slot_count = table_ref.shape[0] // 4
    width = LANES * stacked.shape[0]
    high, low = stack_nodes(fields_ref.at[:, :, width * part : width * part + width], stacked)
    for half in range(2):
        select = select_ref[:, 256 * half : 256 * half + 256]
        rows = product(high, select, ((0,), (0,))) + product(low, select, ((0,), (0,)))
        for side in range(2):
            start = pl.multiple_of((2 * half + side) * slot_count + first + width * part, width)
            table_ref[pl.ds(start, width), :] = rows[:, LANES * side : LANES * side + LANES]


def gather_pieces(slot_count, first, faces_ref, table_ref, normals_ref, outer_ref, rows_refs):
    width = outer_ref.shape[1]
    left_half = lax.broadcasted_iota(jnp.int32, (1, LANES), 1) < 64

    def load(lists, tile, rows):
        for row in rows:
            for half in range(2):
                one = table_ref[pl.ds(lists[2 * half][row], 1), :]
                two = table_ref[pl.ds(lists[2 * half + 1][row], 1), :]
                rows_ref = rows_refs[2 * (tile % 2) + half]
                rows_ref[row : row + 1, :] = jnp.where(left_half, one, two)

    def combine(tile, half):
        turned = rows_refs[2 * (tile % 2) + half][...].T
        lanes = slice(tile * LANES, tile * LANES + LANES)
        for side in range(2):
            face = 2 * half + side
            part = turned[64 * side : 64 * side + 64, :]
            total = -part[0:16]
            for axis_id in range(3):
                facing = normals_ref[axis_id, face : face + 1, lanes]
                total = total + facing * part[16 + 16 * axis_id : 32 + 16 * axis_id]
            outer_ref[FACE_ROWS * face : FACE_ROWS * face + FACE_ROWS, lanes] = total

    for tile in range(width // LANES):
        base = first + tile * LANES
        lists = [faces_ref.at[pl.ds(base + face * slot_count, LANES)] for face in range(4)]
        for part in range(8):
            rows = range(16 * part, 16 * part + 16)
            yield functools.partial(load, lists, tile, rows)
            if tile > 0 and part < 2:
                yield functools.partial(combine, tile - 1, part)
    for half in range(2):
        yield functools.partial(combine, tile, half)


def section_kernel(
    slot_count,
    bound_count,
    powers,
    group,
    faces_ref,
    live_ref,
    next_normals_ref,
    bulk_ref,
    fields_ref,
    residue_ref,
    geometry_ref,
    normals_ref,
    scale_ref,
    codes_ref,
    right_ref,
    left_ref,
    middle_ref,
    elems_ref,
    ids_ref,
    coords_ref,
    table_select_ref,
    select_ref,
    from_ref,
    lift_ref,
    inverse_ref,
    fields_out,
    residue_out,
    spread_ref,
    table_ref,
    stacked,
    combined,
    slow,
    rates,
    remote,
    outer,
    beyond_ref,
    sampled,
    pressure,
    monomials,
    fields_split,
    slow_split,
    inner,
    sources,
    *rows_refs,
):
    width = fields_ref.shape[2]
    tiles = slot_count // width
    bulks = slot_count // bulk_ref.shape[2]
    step = pl.program_id(0) - bulks
    slot_faces = 4 * slot_count
    half_width = 256

    def gather():
        first = step * width
        return gather_pieces(
            slot_count, first, faces_ref, table_ref, next_normals_ref, outer, rows_refs
        )

    def update_pieces():
        first = (step - 1) * width

        def stack(at, low, high):
            for tile in range(2 * at, 2 * at + 2):
                for node in range(low, high):
                    stacked[tile, 4 * node : 4 * node + 4, :] = fields_ref[
                        node, :, LANES * tile : LANES * tile + LANES
                    ]

        def split(at):
            for side in range(2):
                lanes = slice(LANES * side, LANES * side + LANES)
                high, low = halves(stacked[2 * at + side])
                fields_split[at, 0:ROWS, lanes] = high
                fields_split[at, ROWS : 2 * ROWS, lanes] = low

        def inside(at):
            return slice(half_width * at, half_width * at + half_width)

        def field_rows(at, field):
            rows = pl.ds(field, NODES, stride=4)
            return jnp.concatenate([stacked[tile, rows, :] for tile in (2 * at, 2 * at + 1)], axis=1)

        def copy_slow(at):
            lanes = inside(at)
            slow[0:NODES, lanes] = field_rows(at, 0)
            slow_split[at, 0:48, :], slow_split[at, 48:96, :] = halves(slow[:, lanes])

        def weigh(at, axis_id):
            lanes = inside(at)
            weighted = jnp.zeros((NODES, half_width), f32)
            for direction in range(3):
                row = 3 * axis_id + direction
                factor = geometry_ref[row : row + 1, lanes] * (1.0 / 3.0)
                weighted = weighted + factor * field_rows(at, 1 + direction)
            combined[PAD * axis_id : PAD * axis_id + NODES, lanes] = weighted

        def split_weighted(at):
            high, low = halves(combined[:, inside(at)])
            sources[at, 768:896, :], sources[at, 896:1024, :] = high, low

        def traces(at):
            inner[at] = product(select_ref[...], fields_split[at])

        def slope(at, axis_id):
            lanes = inside(at)
            place = lax.broadcasted_iota(jnp.int32, (8, half_width), 0) & 3
            value = product(from_ref[ROWS * axis_id : ROWS * axis_id + ROWS, :], slow_split[at])
            pattern = jnp.zeros((8, half_width), f32)
            for direction in range(3):
                row = 3 * axis_id + direction
                factor = geometry_ref[row : row + 1, lanes] * (1.0 / 3.0)
                pattern = jnp.where(place == direction + 1, factor, pattern)
            value = value.reshape(ROWS // 8, 8, half_width) * pattern[None]
            value = value.reshape(ROWS, half_width)
            if axis_id == 0:
                rates[:, lanes] = value
            else:
                rates[:, lanes] += value

        def keep_split(at, start, value):
            high, low = halves(value)
            rows = value.shape[0]
            sources[at, start : start + rows, :] = high
            sources[at, 256 + start : 256 + start + rows, :] = high
            sources[at, 512 + start : 512 + start + rows, :] = low

        def jump(at, face):
            lanes = inside(at)
            inner_p = inner[at, 64 * face : 64 * face + 16, :]
            along = jnp.zeros_like(inner_p)
            for axis_id in range(3):
                facing = normals_ref[axis_id, face : face + 1, lanes]
                start = 64 * face + 16 + 16 * axis_id
                along = along + facing * inner[at, start : start + 16, :]
            wall = codes_ref[face : face + 1, lanes] < 0
            beyond = beyond_ref[FACE_ROWS * face : FACE_ROWS * face + FACE_ROWS, lanes]
            beyond = jnp.where(wall, -along - inner_p, beyond)
            scale = 0.5 * scale_ref[face : face + 1, lanes]
            value = scale * (along - inner_p - beyond)
            keep_split(at, FACE_ROWS * face, value)
            for axis_id in range(3):
                start = 64 + 64 * axis_id + FACE_ROWS * face
                keep_split(at, start, normals_ref[axis_id, face : face + 1, lanes] * value)

        def lift(at):
            lanes = inside(at)
            rates[:, lanes] = product(lift_ref[...], sources[at]) - rates[:, lanes]

        def advance(at, low, high):
            lanes = inside(at)
            slots = lax.broadcasted_iota(jnp.int32, (1, half_width), 1) + (first + half_width * at)
            keep = slots < live_ref[0]
            for node in range(low, high):
                rate = rates[4 * node : 4 * node + 4, lanes]
                residue_next = section_decay * residue_ref[node, :, lanes] + time_step * rate
                fields_next = fields_ref[node, :, lanes] + section_gain * residue_next
                fields_next = jnp.where(keep, fields_next, 0.0)
                fields_out[node, :, lanes] = fields_next
                residue_out[node, :, lanes] = jnp.where(keep, residue_next, 0.0)
                pressure[node : node + 1, lanes] = fields_next[0:1]

        def sample(at):
            lanes = inside(at)
            parts = jnp.concatenate(thirds(pressure[:, lanes]), axis=0)
            start = first + half_width * at
            slots = lax.broadcasted_iota(jnp.int32, (half_width, elems_ref.shape[1]), 0) + start
            picks = jnp.where(slots == elems_ref[...], 1.0, 0.0).astype(bf16)
            sampled[...] += product(parts, picks)

        call = functools.partial

        def stages(at):
            sevens = range(0, NODES, 7)
            return [
                [call(stack, at, low, low + 7) for low in sevens] + [call(split, at)],
                [call(copy_slow, at)]
                + [call(weigh, at, axis_id) for axis_id in range(3)]
                + [call(split_weighted, at), call(traces, at)],
                [call(slope, at, axis_id) for axis_id in range(3)],
                [call(jump, at, face) for face in range(4)],
                [call(lift, at)],
                [call(advance, at, low, low + 7) for low in sevens],
                [call(sample, at)],
            ]

        both = [stages(at) for at in range(width // half_width)]
        depth = len(both[0])
        return [
            [piece for lag, chain in enumerate(both) if 0 <= at - lag < depth for piece in chain[at - lag]]
            for at in range(depth + len(both) - 1)
        ]

    def interleave(gathers, groups):
        gathers = list(gathers)

        def run(at, updates):
            @pl.when(live_ref[0] > at)
            def _():
                low = at * len(gathers) // len(groups)
                loads = gathers[low : (at + 1) * len(gathers) // len(groups)]
                for place in range(max(len(loads), len(updates))):
                    for piece in loads[place : place + 1] + updates[place : place + 1]:
                        piece()

        for at, updates in enumerate(groups):
            run(at, updates)

    @pl.when(step == -bulks)
    def _():
        stacked[...] = jnp.zeros_like(stacked)
        combined[...] = jnp.zeros_like(combined)
        slow[...] = jnp.zeros_like(slow)
        pressure[...] = jnp.zeros_like(pressure)
        sampled[...] = jnp.zeros_like(sampled)
        monomials[...] = jnp.zeros_like(monomials)
        remote[...] = jnp.zeros_like(remote)
        arrivals = [
            left_ref[2],
            middle_ref[1],
            right_ref[2],
            left_ref[0],
            right_ref[0],
            left_ref[1],
            middle_ref[0],
            right_ref[1],
        ]
        for heading, source in enumerate(arrivals):
            start = bound_count * heading
            remote[0:48, start : start + 96] = source[:, 0:96]
            for third in range(3):
                place = start + 32 * third
                remote[48:64, place : place + 32] = source[16 * third : 16 * third + 16, 96:128]

    @pl.when(step < 0)
    def _():
        first = (step + bulks) * bulk_ref.shape[2]
        for part in range(bulk_ref.shape[2] // width):
            build_rows(first, part, bulk_ref, table_select_ref, table_ref, stacked)

    @pl.when(step == 0)
    def _():
        for piece in gather():
            piece()

    @pl.when((step > 0) & ((step - 1) * width < 8 * bound_count))
    def _():
        lanes = pl.ds(pl.multiple_of((step - 1) * width, width), width)
        for face in range(4):
            rows = slice(FACE_ROWS * face, FACE_ROWS * face + FACE_ROWS)
            total = -remote[0:16, lanes]
            for axis_id in range(3):
                facing = normals_ref[axis_id, face : face + 1, :]
                total = total + facing * remote[16 + 16 * axis_id : 32 + 16 * axis_id, lanes]
            is_remote = codes_ref[face : face + 1, :] >= slot_faces
            outer[rows, :] = jnp.where(is_remote, total, outer[rows, :])

    @pl.when((step > 0) & (step < tiles))
    def _():
        beyond_ref[...] = outer[...]
        interleave(gather(), update_pieces())

    @pl.when(step == tiles)
    def _():
        beyond_ref[...] = outer[...]
        for stage in update_pieces():
            for piece in stage:
                piece()
        ladders = []
        for axis_id in range(3):
            base = coords_ref[axis_id : axis_id + 1, :]
            square = base * base
            ladders.append([jnp.ones_like(base), base, square, square * base, square * square])
        for node in range(NODES):
            exps = [int(entry) for entry in powers[node]]
            monomials[node : node + 1, :] = (
                ladders[0][exps[0]] * ladders[1][exps[1]] * ladders[2][exps[2]]
            )
        basis = jnp.dot(
            inverse_ref[...], monomials[...], precision=highest, preferred_element_type=f32
        )
        gathered = sampled[0:PAD, :] + sampled[48 : 48 + PAD, :] + sampled[96 : 96 + PAD, :]
        values = jnp.sum(basis * gathered, axis=0, keepdims=True)
        ids = ids_ref[...]
        owner = lax.shift_right_logical(ids * 5243, 20)
        place = ids - group * owner
        owners = lax.broadcasted_iota(jnp.int32, (spread_ref.shape[0], ids.shape[1]), 0)
        held = jnp.where(owners == owner, values, 0.0)
        places = lax.broadcasted_iota(jnp.int32, (spread_ref.shape[2], ids.shape[1]), 0)
        chosen = jnp.where(places == place, 1.0, 0.0).astype(bf16)
        spread = jnp.zeros((spread_ref.shape[0], spread_ref.shape[2]), f32)
        for part in thirds(held):
            spread = spread + product(part, chosen, ((1,), (1,)))
        spread_ref[:, 0, :] = spread


def harmonic_kernel(received_ref, table_ref, groups_ref, out_ref):
    mine = jnp.sum(received_ref[...], axis=0)
    weighted = groups_ref[...] * mine
    out_ref[...] = lax.dot_general(
        weighted,
        table_ref[...],
        (((1,), (1,)), ((), ())),
        precision=highest,
        preferred_element_type=f32,
    )


def in_hbm(array):
    return pltpu.with_memory_space_constraint(array, pltpu.HBM)


def fixed(shape):
    return pl.BlockSpec(shape, lambda *_: (0,) * len(shape))


def local(
    fields,
    residue,
    geometry,
    normals,
    face_scale,
    neighbours,
    send_faces,
    live_counts,
    sample_ids,
    sample_elems,
    sample_coords,
):
    const = {
        name: in_hbm(table) if isinstance(table, jax.Array) else table
        for name, table in constant_tables().items()
    }
    fields = in_hbm(jnp.transpose(fields, (1, 0, 2)))
    residue = in_hbm(jnp.transpose(residue, (1, 0, 2)))
    geometry, normals, face_scale = in_hbm(geometry), in_hbm(normals), in_hbm(face_scale)
    neighbours, sample_coords = in_hbm(neighbours), in_hbm(sample_coords)
    slot_count = fields.shape[2]
    slot_faces = 4 * slot_count
    bound_count = send_faces.shape[1]
    reach = 8 * bound_count
    samples = sample_ids.shape[0]
    devices = lax.axis_size(("px", "py"))
    shape = jax.ShapeDtypeStruct

    width = 512
    tiles = slot_count // width
    piece = (3, 48, LANES)

    up, down, left, right, faces = pl.pallas_call(
        functools.partial(pack_kernel, slot_faces),
        grid=(1,),
        in_specs=[
            pl.BlockSpec((NODES, 4, reach), lambda t: (0, 0, 0)),
            fixed((4, slot_count)),
            fixed((256, ROWS)),
        ],
        out_specs=[
            fixed(piece),
            fixed(piece),
            fixed(piece[1:]),
            fixed(piece[1:]),
            fixed((slot_faces // LANES, LANES)),
        ],
        out_shape=[
            shape(piece, f32),
            shape(piece, f32),
            shape(piece[1:], f32),
            shape(piece[1:], f32),
            shape((slot_faces // LANES, LANES), jnp.int32),
        ],
        scratch_shapes=[pltpu.VMEM((reach // LANES, ROWS, LANES), f32)],
        compiler_params=pltpu.CompilerParams(vmem_limit_bytes=16 << 20),
        name="pack",
    )(fields, neighbours, const["trace_select"])

    def steps_along(axis):
        count = lax.axis_size(axis)
        forward = [(i, i + 1) for i in range(count - 1)]
        return forward, [(target, source) for source, target in forward]

    forward, backward = steps_along("px")
    below = lax.ppermute(up, "px", backward)
    above = lax.ppermute(down, "px", forward)
    to_left, to_right, middle = pl.pallas_call(
        relay_kernel,
        out_shape=[shape(piece, f32), shape(piece, f32), shape((2,) + piece[1:], f32)],
        name="relay",
    )(left, right, below, above)
    forward, backward = steps_along("py")
    from_right = lax.ppermute(to_left, "py", backward)
    from_left = lax.ppermute(to_right, "py", forward)

    bulk = 3 * width
    bulks = slot_count // bulk

    def behind(rank):
        return lambda t, *_: (0,) * rank + (jnp.maximum(t - bulks - 1, 0),)

    def ahead(rank):
        return lambda t, *_: (0,) * rank + (jnp.clip(t - bulks, 0, tiles - 1),)

    fields_next, residue_next, spread = pl.pallas_call(
        functools.partial(section_kernel, slot_count, bound_count, const["powers"], samples),
        grid_spec=pltpu.PrefetchScalarGridSpec(
            num_scalar_prefetch=2,
            grid=(bulks + tiles + 1,),
            in_specs=[
                pl.BlockSpec((3, 4, width), ahead(2)),
                pl.BlockSpec((NODES, 4, bulk), lambda t, *_: (0, 0, jnp.minimum(t, bulks - 1))),
                pl.BlockSpec((NODES, 4, width), behind(2)),
                pl.BlockSpec((NODES, 4, width), behind(2)),
                pl.BlockSpec((9, width), behind(1)),
                pl.BlockSpec((3, 4, width), behind(2)),
                pl.BlockSpec((4, width), behind(1)),
                pl.BlockSpec((4, width), behind(1)),
                fixed(piece),
                fixed(piece),
                fixed((2,) + piece[1:]),
                fixed((1, samples)),
                fixed((1, samples)),
                fixed((3, samples)),
                fixed((ROWS, 4 * LANES)),
                fixed((256, 2 * ROWS)),
                fixed((3 * ROWS, 96)),
                fixed((ROWS, 1024)),
                fixed((PAD, PAD)),
            ],
            out_specs=[
                pl.BlockSpec((NODES, 4, width), behind(2)),
                pl.BlockSpec((NODES, 4, width), behind(2)),
                fixed((devices, 1, samples)),
            ],
            scratch_shapes=[
                pltpu.VMEM((slot_faces, LANES), f32),
                pltpu.VMEM((width // LANES, ROWS, LANES), f32),
                pltpu.VMEM((128, width), f32),
                pltpu.VMEM((48, width), f32),
                pltpu.VMEM((ROWS, width), f32),
                pltpu.VMEM((64, pl.cdiv(reach, width) * width), f32),
                pltpu.VMEM((64, width), f32),
                pltpu.VMEM((64, width), f32),
                pltpu.VMEM((144, samples), f32),
                pltpu.VMEM((48, width), f32),
                pltpu.VMEM((PAD, samples), f32),
                pltpu.VMEM((width // 256, 2 * ROWS, 256), bf16),
                pltpu.VMEM((width // 256, 96, 256), bf16),
                pltpu.VMEM((width // 256, 256, 256), f32),
                pltpu.VMEM((width // 256, 1024, 256), bf16),
                *[pltpu.VMEM((LANES, LANES), f32)] * 4,
            ],
        ),
        out_shape=[
            shape(fields.shape, f32),
            shape(residue.shape, f32),
            shape((devices, 1, samples), f32),
        ],
        compiler_params=pltpu.CompilerParams(vmem_limit_bytes=48 << 20),
        name="section",
    )(
        faces.reshape(-1),
        live_counts,
        normals,
        fields,
        fields,
        residue,
        geometry,
        normals,
        face_scale,
        neighbours,
        from_right,
        from_left,
        middle,
        in_hbm(sample_elems.reshape(1, samples)),
        in_hbm(sample_ids.reshape(1, samples)),
        sample_coords,
        const["table_select"],
        const["twice_select"],
        const["from_p"],
        const["lift"],
        const["inverse"],
    )
    received = lax.all_to_all(spread, ("px", "py"), 0, 0, tiled=True)

    receivers = samples // QPTS
    harmonic = np.tile(harmonic_table(), (1, receivers)).astype(np.float32)
    groups = (np.arange(samples)[None] // QPTS == np.arange(receivers)[:, None]).astype(np.float32)
    coefficients = pl.pallas_call(
        harmonic_kernel,
        out_shape=shape((receivers, harmonic.shape[0]), f32),
        name="harmonic",
    )(received, jnp.asarray(harmonic), jnp.asarray(groups))
    return (
        jnp.transpose(fields_next, (1, 0, 2)),
        jnp.transpose(residue_next, (1, 0, 2)),
        coefficients.T,
    )


def solution(mesh):
    placed = (
        P(None, None, ("px", "py")),
        P(None, None, ("px", "py")),
        P(None, ("px", "py")),
        P(None, None, ("px", "py")),
        P(None, ("px", "py")),
        P(None, ("px", "py")),
        P(None, ("px", "py")),
        P(("px", "py")),
        P(("px", "py")),
        P(("px", "py")),
        P(None, ("px", "py")),
    )
    return jax.shard_map(
        local,
        mesh=mesh,
        in_specs=placed,
        out_specs=(P(None, None, ("px", "py")), P(None, None, ("px", "py")), P(None, ("px", "py"))),
        check_vma=False,
    )
```

```python
import functools
import math

import jax
import jax.numpy as jnp
import numpy as np
from jax import lax
from jax.experimental import pallas as pl
from jax.experimental.pallas import tpu as pltpu
from jax.sharding import PartitionSpec as P

QPTS = 50
NODES = 35
PAD = 40
FACE_ROWS = 16
ROWS = 144
LANES = 128


highest = lax.Precision.HIGHEST
section_decay = -567301805773.0 / 1357537059087.0
section_gain = 5161836677717.0 / 13612068292357.0
time_step = 0.01
f32 = jnp.float32
bf16 = jnp.bfloat16


def exponent_table():
    listing = []
    for degree in range(5):
        for third in range(degree + 1):
            for second in range(degree + 1 - third):
                listing.append((degree - second - third, second, third))
    return np.array(listing)


def factorials(values):
    lookup = np.array([float(math.factorial(level)) for level in range(24)])
    return lookup[values]


def eliminate(matrix, right_hand):
    order_size = matrix.shape[0]
    work = np.concatenate([matrix, right_hand], axis=1).astype(float)
    for pivot_col in range(order_size):
        best = max(range(pivot_col, order_size), key=lambda row_id: abs(work[row_id, pivot_col]))
        work[[pivot_col, best]] = work[[best, pivot_col]]
        work[pivot_col] = work[pivot_col] / work[pivot_col, pivot_col]
        for row_id in range(order_size):
            if row_id != pivot_col:
                work[row_id] = work[row_id] - work[row_id, pivot_col] * work[pivot_col]
    return work[:, order_size:]


def element_tables():
    powers = exponent_table()
    points = powers / 4.0
    vander = np.prod(points[:, None, :] ** powers[None, :, :], axis=2)
    inverse = eliminate(vander, np.eye(35))
    derivs = []
    for axis_id in range(3):
        lowered = np.maximum(powers - (np.arange(3) == axis_id)[None, :], 0)
        slope_table = powers[None, :, axis_id] * np.prod(
            points[:, None, :] ** lowered[None, :, :], axis=2
        )
        derivs.append(slope_table @ inverse)
    summed = powers[:, None, :] + powers[None, :, :]
    exp_r = summed[..., 0]
    exp_s = summed[..., 1]
    exp_t = summed[..., 2]
    volume = (
        factorials(exp_r)
        * factorials(exp_s)
        * factorials(exp_t)
        / factorials(exp_r + exp_s + exp_t + 3)
    )
    mass_matrix = inverse.T @ volume @ inverse
    face_grams = [
        np.where(
            exp_t == 0, factorials(exp_r) * factorials(exp_s) / factorials(exp_r + exp_s + 2), 0.0
        ),
        np.where(
            exp_s == 0, factorials(exp_r) * factorials(exp_t) / factorials(exp_r + exp_t + 2), 0.0
        ),
        factorials(exp_r)
        * factorials(exp_s)
        * factorials(exp_t)
        / factorials(exp_r + exp_s + exp_t + 2),
        np.where(
            exp_r == 0, factorials(exp_s) * factorials(exp_t) / factorials(exp_s + exp_t + 2), 0.0
        ),
    ]
    listed = [tuple((int(entry) for entry in powers[node_id])) for node_id in range(35)]
    face_nodes = np.array(
        [
            [node_id for node_id in range(35) if listed[node_id][2] == 0],
            [node_id for node_id in range(35) if listed[node_id][1] == 0],
            [node_id for node_id in range(35) if sum(listed[node_id]) == 4],
            [node_id for node_id in range(35) if listed[node_id][0] == 0],
        ]
    )
    surface = np.zeros((35, 60))
    for face_id in range(4):
        face_mass = inverse.T @ face_grams[face_id] @ inverse
        for node_id in range(15):
            surface[:, 4 * node_id + face_id] = face_mass[:, face_nodes[face_id, node_id]]
    lifting = eliminate(mass_matrix, surface)
    return (np.stack(derivs), lifting, face_nodes, inverse, powers)


def associated(degree, order, cosine, sine):
    current = cosine * 0.0 + 1.0
    for step_id in range(1, order + 1):
        current = -(2 * step_id - 1) * sine * current
    if degree == order:
        return current
    following = cosine * (2 * order + 1) * current
    for level in range(order + 2, degree + 1):
        current, following = (
            following,
            ((2 * level - 1) * cosine * following - (level + order - 1) * current)
            / (level - order),
        )
    return following


def harmonic_table():
    inner_node = math.sqrt(5.0 - 2.0 * math.sqrt(10.0 / 7.0)) / 3.0
    outer_node = math.sqrt(5.0 + 2.0 * math.sqrt(10.0 / 7.0)) / 3.0
    inner_weight = (322.0 + 13.0 * math.sqrt(70.0)) / 900.0
    outer_weight = (322.0 - 13.0 * math.sqrt(70.0)) / 900.0
    cosines = np.array([-outer_node, -inner_node, 0.0, inner_node, outer_node])
    weights = np.array([outer_weight, inner_weight, 128.0 / 225.0, inner_weight, outer_weight])
    azimuth = 2.0 * np.pi * (np.arange(10) + 0.5) / 10.0
    polar = np.repeat(cosines, 10)
    circle = np.tile(azimuth, 5)
    point_weight = np.repeat(weights, 10) * 2.0 * np.pi / 10.0
    sine = np.sqrt(1.0 - polar**2)
    table_rows = []
    for degree in range(5):
        for order in range(-degree, degree + 1):
            absolute = abs(order)
            legendre = associated(degree, absolute, polar, sine)
            factor = math.sqrt(
                (2 * degree + 1)
                / (4.0 * math.pi)
                * math.factorial(degree - absolute)
                / math.factorial(degree + absolute)
            )
            if order > 0:
                angular = math.sqrt(2.0) * np.cos(order * circle)
            elif order < 0:
                angular = math.sqrt(2.0) * np.sin(absolute * circle)
            else:
                angular = circle * 0.0 + 1.0
            table_rows.append(factor * legendre * angular * point_weight)
    return np.array(table_rows)


def constant_tables():
    derivs, lifting, face_nodes, inverse, powers = element_tables()
    table_select = np.zeros((ROWS, 4 * LANES), np.float32)
    trace_select = np.zeros((4 * 4 * FACE_ROWS, ROWS), np.float32)
    for face in range(4):
        for field in range(4):
            for place in range(15):
                source = 4 * face_nodes[face, place] + field
                column = FACE_ROWS * field + place
                table_select[source, LANES * face + column] = 1.0
                table_select[source, LANES * face + 64 + column] = 1.0
                trace_select[64 * face + column, source] = 1.0
    whole = np.round(3.0 * derivs)
    into_p = np.zeros((ROWS, 128), np.float32)
    from_p = np.zeros((3 * ROWS, 48), np.float32)
    lift = np.zeros((ROWS, 256), np.float32)
    for node in range(NODES):
        for axis_id in range(3):
            into_p[4 * node, PAD * axis_id : PAD * axis_id + NODES] = -whole[axis_id, node]
            for field in range(1, 4):
                from_p[ROWS * axis_id + 4 * node + field, :NODES] = whole[axis_id, node]
        for face in range(4):
            for place in range(15):
                entry = lifting[node, 4 * place + face]
                column = FACE_ROWS * face + place
                lift[4 * node, column] = entry
                for field in range(1, 4):
                    lift[4 * node + field, 64 * field + column] = -entry
    lift_hi = lift.astype(jnp.bfloat16)
    lift_lo = (lift - lift_hi.astype(np.float32)).astype(jnp.bfloat16)
    return {
        "table_select": jnp.asarray(table_select, bf16),
        "trace_select": jnp.asarray(trace_select, bf16),
        "twice_select": jnp.asarray(np.concatenate([trace_select] * 2, axis=1), bf16),
        "from_p": jnp.asarray(np.concatenate([from_p, from_p], axis=1), bf16),
        "lift": jnp.asarray(
            np.concatenate(
                [lift_hi, lift_lo, lift_hi] + [into_p.astype(jnp.bfloat16)] * 2, axis=1
            )
        ),
        "inverse": jnp.asarray(np.pad(inverse.T, ((0, 5), (0, 5))), f32),
        "powers": powers,
    }


def halves(values):
    high = values.astype(bf16)
    return high, (values - high.astype(f32)).astype(bf16)


def thirds(values):
    high = values.astype(bf16)
    rest = values - high.astype(f32)
    middle = rest.astype(bf16)
    return high, middle, (rest - middle.astype(f32)).astype(bf16)


def product(left, right, dims=((1,), (0,))):
    return lax.dot_general(left, right, (dims, ((), ())), preferred_element_type=f32)


def stack_nodes(fields_ref, stacked):
    tiles = range(stacked.shape[0])
    for tile in tiles:
        for node in range(NODES):
            stacked[tile, 4 * node : 4 * node + 4, :] = fields_ref[
                node, :, LANES * tile : LANES * tile + LANES
            ]
    return halves(jnp.concatenate([stacked[tile] for tile in tiles], axis=1))


def one_field(stacked, field):
    tiles = range(stacked.shape[0])
    rows = pl.ds(field, NODES, stride=4)
    return jnp.concatenate([stacked[tile, rows, :] for tile in tiles], axis=1)


def pack_kernel(
    slot_faces,
    fields_ref,
    codes_ref,
    select_ref,
    up_ref,
    down_ref,
    left_ref,
    right_ref,
    faces_ref,
    stacked,
):
    stacked[...] = jnp.zeros_like(stacked)
    high, low = stack_nodes(fields_ref, stacked)
    traces = product(select_ref[...], high) + product(select_ref[...], low)
    reach = fields_ref.shape[2]
    count = reach // 8
    chosen = jnp.zeros((64, reach), f32)
    for face in range(4):
        remote = codes_ref[face : face + 1, 0:reach] >= slot_faces
        chosen = jnp.where(remote, traces[64 * face : 64 * face + 64, :], chosen)
    homes = [up_ref.at[0], up_ref.at[1], up_ref.at[2], left_ref, right_ref]
    homes += [down_ref.at[0], down_ref.at[1], down_ref.at[2]]
    for heading, home in enumerate(homes):
        part = chosen[:, count * heading : count * heading + count]
        home[:, 0:96] = part[0:48]
        for third in range(3):
            home[16 * third : 16 * third + 16, 96:128] = part[48:64, 32 * third : 32 * third + 32]
    tiles = codes_ref.shape[1] // LANES
    codes = codes_ref[...]
    codes = jnp.where((codes >= 0) & (codes < slot_faces), codes, 0)
    for face in range(4):
        for tile in range(tiles):
            row = face * tiles + tile
            faces_ref[row : row + 1, :] = codes[
                face : face + 1, LANES * tile : LANES * tile + LANES
            ]


def relay_kernel(left_ref, right_ref, below_ref, above_ref, to_left_ref, to_right_ref):
    to_left_ref[0] = left_ref[...]
    to_left_ref[1] = below_ref[0]
    to_left_ref[2] = above_ref[0]
    to_right_ref[0] = right_ref[...]
    to_right_ref[1] = below_ref[2]
    to_right_ref[2] = above_ref[2]


def build_rows(first, part, fields_ref, select_ref, table_ref, stacked):
    slot_count = table_ref.shape[0] // 4
    width = LANES * stacked.shape[0]
    high, low = stack_nodes(fields_ref.at[:, :, width * part : width * part + width], stacked)
    for half in range(2):
        select = select_ref[:, 256 * half : 256 * half + 256]
        rows = product(high, select, ((0,), (0,))) + product(low, select, ((0,), (0,)))
        for side in range(2):
            start = pl.multiple_of((2 * half + side) * slot_count + first + width * part, width)
            table_ref[pl.ds(start, width), :] = rows[:, LANES * side : LANES * side + LANES]


def gather_pieces(slot_count, first, faces_ref, table_ref, normals_ref, outer_ref, rows_refs):
    width = outer_ref.shape[1]
    left_half = lax.broadcasted_iota(jnp.int32, (1, LANES), 1) < 64

    def load(lists, tile, rows):
        for row in rows:
            for half in range(2):
                one = table_ref[pl.ds(lists[2 * half][row], 1), :]
                two = table_ref[pl.ds(lists[2 * half + 1][row], 1), :]
                rows_ref = rows_refs[2 * (tile % 2) + half]
                rows_ref[row : row + 1, :] = jnp.where(left_half, one, two)

    def combine(tile, half):
        turned = rows_refs[2 * (tile % 2) + half][...].T
        lanes = slice(tile * LANES, tile * LANES + LANES)
        for side in range(2):
            face = 2 * half + side
            part = turned[64 * side : 64 * side + 64, :]
            total = -part[0:16]
            for axis_id in range(3):
                facing = normals_ref[axis_id, face : face + 1, lanes]
                total = total + facing * part[16 + 16 * axis_id : 32 + 16 * axis_id]
            outer_ref[FACE_ROWS * face : FACE_ROWS * face + FACE_ROWS, lanes] = total

    for tile in range(width // LANES):
        base = first + tile * LANES
        lists = [faces_ref.at[pl.ds(base + face * slot_count, LANES)] for face in range(4)]
        for part in range(8):
            rows = range(16 * part, 16 * part + 16)
            yield functools.partial(load, lists, tile, rows)
            if tile > 0 and part < 2:
                yield functools.partial(combine, tile - 1, part)
    for half in range(2):
        yield functools.partial(combine, tile, half)


def section_kernel(
    slot_count,
    reach,
    faces_ref,
    live_ref,
    next_normals_ref,
    bulk_ref,
    fields_ref,
    residue_ref,
    geometry_ref,
    normals_ref,
    scale_ref,
    codes_ref,
    elems_ref,
    table_select_ref,
    select_ref,
    from_ref,
    lift_ref,
    fields_out,
    residue_out,
    sampled,
    table_ref,
    stacked,
    combined,
    slow,
    rates,
    outer,
    beyond_ref,
    pressure,
    fields_split,
    slow_split,
    inner,
    sources,
    *rows_refs,
):
    width = fields_ref.shape[2]
    tiles = slot_count // width
    bulks = slot_count // bulk_ref.shape[2]
    step = pl.program_id(0) - bulks
    slot_faces = 4 * slot_count
    half_width = 256

    def gather():
        first = step * width
        return gather_pieces(
            slot_count, first, faces_ref, table_ref, next_normals_ref, outer, rows_refs
        )

    def update_pieces():
        first = (step - 1) * width

        def stack(at, low, high):
            for tile in range(2 * at, 2 * at + 2):
                for node in range(low, high):
                    stacked[tile, 4 * node : 4 * node + 4, :] = fields_ref[
                        node, :, LANES * tile : LANES * tile + LANES
                    ]

        def split(at):
            for side in range(2):
                lanes = slice(LANES * side, LANES * side + LANES)
                high, low = halves(stacked[2 * at + side])
                fields_split[at, 0:ROWS, lanes] = high
                fields_split[at, ROWS : 2 * ROWS, lanes] = low

        def inside(at):
            return slice(half_width * at, half_width * at + half_width)

        def field_rows(at, field):
            rows = pl.ds(field, NODES, stride=4)
            return jnp.concatenate([stacked[tile, rows, :] for tile in (2 * at, 2 * at + 1)], axis=1)

        def copy_slow(at):
            lanes = inside(at)
            slow[0:NODES, lanes] = field_rows(at, 0)
            slow_split[at, 0:48, :], slow_split[at, 48:96, :] = halves(slow[:, lanes])

        def weigh(at, axis_id):
            lanes = inside(at)
            weighted = jnp.zeros((NODES, half_width), f32)
            for direction in range(3):
                row = 3 * axis_id + direction
                factor = geometry_ref[row : row + 1, lanes] * (1.0 / 3.0)
                weighted = weighted + factor * field_rows(at, 1 + direction)
            combined[PAD * axis_id : PAD * axis_id + NODES, lanes] = weighted

        def split_weighted(at):
            high, low = halves(combined[:, inside(at)])
            sources[at, 768:896, :], sources[at, 896:1024, :] = high, low

        def traces(at):
            inner[at] = product(select_ref[...], fields_split[at])

        def slope(at, axis_id):
            lanes = inside(at)
            place = lax.broadcasted_iota(jnp.int32, (8, half_width), 0) & 3
            value = product(from_ref[ROWS * axis_id : ROWS * axis_id + ROWS, :], slow_split[at])
            pattern = jnp.zeros((8, half_width), f32)
            for direction in range(3):
                row = 3 * axis_id + direction
                factor = geometry_ref[row : row + 1, lanes] * (1.0 / 3.0)
                pattern = jnp.where(place == direction + 1, factor, pattern)
            value = value.reshape(ROWS // 8, 8, half_width) * pattern[None]
            value = value.reshape(ROWS, half_width)
            if axis_id == 0:
                rates[:, lanes] = value
            else:
                rates[:, lanes] += value

        def keep_split(at, start, value):
            high, low = halves(value)
            rows = value.shape[0]
            sources[at, start : start + rows, :] = high
            sources[at, 256 + start : 256 + start + rows, :] = high
            sources[at, 512 + start : 512 + start + rows, :] = low

        def jump(at, face):
            lanes = inside(at)
            inner_p = inner[at, 64 * face : 64 * face + 16, :]
            along = jnp.zeros_like(inner_p)
            for axis_id in range(3):
                facing = normals_ref[axis_id, face : face + 1, lanes]
                start = 64 * face + 16 + 16 * axis_id
                along = along + facing * inner[at, start : start + 16, :]
            wall = codes_ref[face : face + 1, lanes] < 0
            beyond = beyond_ref[FACE_ROWS * face : FACE_ROWS * face + FACE_ROWS, lanes]
            beyond = jnp.where(wall, -along - inner_p, beyond)
            beyond = jnp.where(codes_ref[face : face + 1, lanes] >= slot_faces, 0.0, beyond)
            scale = 0.5 * scale_ref[face : face + 1, lanes]
            value = scale * (along - inner_p - beyond)
            keep_split(at, FACE_ROWS * face, value)
            for axis_id in range(3):
                start = 64 + 64 * axis_id + FACE_ROWS * face
                keep_split(at, start, normals_ref[axis_id, face : face + 1, lanes] * value)

        def lift(at):
            lanes = inside(at)
            rates[:, lanes] = product(lift_ref[...], sources[at]) - rates[:, lanes]

        def advance(at, low, high):
            lanes = inside(at)
            slots = lax.broadcasted_iota(jnp.int32, (1, half_width), 1) + (first + half_width * at)
            keep = slots < live_ref[0]
            for node in range(low, high):
                rate = rates[4 * node : 4 * node + 4, lanes]
                residue_next = section_decay * residue_ref[node, :, lanes] + time_step * rate
                fields_next = fields_ref[node, :, lanes] + section_gain * residue_next
                fields_next = jnp.where(keep, fields_next, 0.0)
                fields_out[node, :, lanes] = fields_next
                residue_out[node, :, lanes] = jnp.where(keep, residue_next, 0.0)
                pressure[node : node + 1, lanes] = fields_next[0:1]

        def sample(at):
            lanes = inside(at)
            parts = jnp.concatenate(thirds(pressure[:, lanes]), axis=0)
            start = first + half_width * at
            slots = lax.broadcasted_iota(jnp.int32, (half_width, elems_ref.shape[1]), 0) + start
            elems = elems_ref[...]
            picks = (slots == elems) & (elems >= reach)
            sampled[...] += product(parts, jnp.where(picks, 1.0, 0.0).astype(bf16))

        call = functools.partial

        def stages(at):
            sevens = range(0, NODES, 7)
            return [
                [call(stack, at, low, low + 7) for low in sevens] + [call(split, at)],
                [call(copy_slow, at)]
                + [call(weigh, at, axis_id) for axis_id in range(3)]
                + [call(split_weighted, at), call(traces, at)],
                [call(slope, at, axis_id) for axis_id in range(3)],
                [call(jump, at, face) for face in range(4)],
                [call(lift, at)],
                [call(advance, at, low, low + 7) for low in sevens],
                [call(sample, at)],
            ]

        both = [stages(at) for at in range(width // half_width)]
        depth = len(both[0])
        return [
            [piece for lag, chain in enumerate(both) if 0 <= at - lag < depth for piece in chain[at - lag]]
            for at in range(depth + len(both) - 1)
        ]

    def interleave(gathers, groups):
        gathers = list(gathers)

        def run(at, updates):
            @pl.when(live_ref[0] > at)
            def _():
                low = at * len(gathers) // len(groups)
                loads = gathers[low : (at + 1) * len(gathers) // len(groups)]
                for place in range(max(len(loads), len(updates))):
                    for piece in loads[place : place + 1] + updates[place : place + 1]:
                        piece()

        for at, updates in enumerate(groups):
            run(at, updates)

    @pl.when(step == -bulks)
    def _():
        stacked[...] = jnp.zeros_like(stacked)
        combined[...] = jnp.zeros_like(combined)
        slow[...] = jnp.zeros_like(slow)
        pressure[...] = jnp.zeros_like(pressure)
        sampled[...] = jnp.zeros_like(sampled)

    @pl.when(step < 0)
    def _():
        first = (step + bulks) * bulk_ref.shape[2]
        for part in range(bulk_ref.shape[2] // width):
            build_rows(first, part, bulk_ref, table_select_ref, table_ref, stacked)

    @pl.when(step == 0)
    def _():
        for piece in gather():
            piece()

    @pl.when((step > 0) & (step < tiles))
    def _():
        beyond_ref[...] = outer[...]
        interleave(gather(), update_pieces())

    @pl.when(step == tiles)
    def _():
        beyond_ref[...] = outer[...]
        for stage in update_pieces():
            for piece in stage:
                piece()


def boundary_kernel(
    slot_faces,
    powers,
    group,
    fields_ref,
    residue_ref,
    normals_ref,
    scale_ref,
    codes_ref,
    right_ref,
    left_ref,
    below_ref,
    above_ref,
    elems_ref,
    ids_ref,
    coords_ref,
    partial_ref,
    lift_ref,
    inverse_ref,
    fields_out,
    residue_out,
    spread_ref,
    remote,
    sources,
    rates,
    pressure,
    monomials,
):
    reach = fields_ref.shape[2]
    bound_count = reach // 8
    pressure[...] = jnp.zeros_like(pressure)
    monomials[...] = jnp.zeros_like(monomials)
    arrivals = [
        left_ref[2],
        above_ref[1],
        right_ref[2],
        left_ref[0],
        right_ref[0],
        left_ref[1],
        below_ref[1],
        right_ref[1],
    ]
    for heading, source in enumerate(arrivals):
        start = bound_count * heading
        remote[0:48, start : start + 96] = source[:, 0:96]
        for third in range(3):
            place = start + 32 * third
            remote[48:64, place : place + 32] = source[16 * third : 16 * third + 16, 96:128]

    def keep_split(start, value):
        high, low = halves(value)
        sources[start : start + FACE_ROWS, :] = high
        sources[256 + start : 256 + start + FACE_ROWS, :] = high
        sources[512 + start : 512 + start + FACE_ROWS, :] = low

    for face in range(4):
        beyond = -remote[0:16, :]
        for axis_id in range(3):
            facing = normals_ref[axis_id, face : face + 1, :]
            beyond = beyond + facing * remote[16 + 16 * axis_id : 32 + 16 * axis_id, :]
        is_remote = codes_ref[face : face + 1, :] >= slot_faces
        flux = jnp.where(is_remote, -0.5 * scale_ref[face : face + 1, :] * beyond, 0.0)
        keep_split(FACE_ROWS * face, flux)
        for axis_id in range(3):
            facing = normals_ref[axis_id, face : face + 1, :]
            keep_split(64 + 64 * axis_id + FACE_ROWS * face, facing * flux)
    rates[...] = time_step * product(lift_ref[:, 0:768], sources[...])
    for node in range(NODES):
        rate = rates[4 * node : 4 * node + 4, :]
        residue_out[node] = residue_ref[node] + rate
        fields_next = fields_ref[node] + section_gain * rate
        fields_out[node] = fields_next
        pressure[node : node + 1, :] = fields_next[0:1]
    parts = jnp.concatenate(thirds(pressure[...]), axis=0)
    slots = lax.broadcasted_iota(jnp.int32, (reach, elems_ref.shape[1]), 0)
    picks = jnp.where(slots == elems_ref[...], 1.0, 0.0).astype(bf16)
    sampled = partial_ref[...] + product(parts, picks)
    ladders = []
    for axis_id in range(3):
        base = coords_ref[axis_id : axis_id + 1, :]
        square = base * base
        ladders.append([jnp.ones_like(base), base, square, square * base, square * square])
    for node in range(NODES):
        exps = [int(entry) for entry in powers[node]]
        monomials[node : node + 1, :] = (
            ladders[0][exps[0]] * ladders[1][exps[1]] * ladders[2][exps[2]]
        )
    basis = jnp.dot(
        inverse_ref[...], monomials[...], precision=highest, preferred_element_type=f32
    )
    gathered = sampled[0:PAD, :] + sampled[48 : 48 + PAD, :] + sampled[96 : 96 + PAD, :]
    values = jnp.sum(basis * gathered, axis=0, keepdims=True)
    ids = ids_ref[...]
    owner = lax.shift_right_logical(ids * 5243, 20)
    place = ids - group * owner
    owners = lax.broadcasted_iota(jnp.int32, (spread_ref.shape[0], ids.shape[1]), 0)
    held = jnp.where(owners == owner, values, 0.0)
    places = lax.broadcasted_iota(jnp.int32, (spread_ref.shape[2], ids.shape[1]), 0)
    chosen = jnp.where(places == place, 1.0, 0.0).astype(bf16)
    spread = jnp.zeros((spread_ref.shape[0], spread_ref.shape[2]), f32)
    for part in thirds(held):
        spread = spread + product(part, chosen, ((1,), (1,)))
    spread_ref[:, 0, :] = spread


def harmonic_kernel(received_ref, table_ref, groups_ref, out_ref):
    mine = jnp.sum(received_ref[...], axis=0)
    weighted = groups_ref[...] * mine
    out_ref[...] = lax.dot_general(
        weighted,
        table_ref[...],
        (((1,), (1,)), ((), ())),
        precision=highest,
        preferred_element_type=f32,
    )


def in_hbm(array):
    return pltpu.with_memory_space_constraint(array, pltpu.HBM)


def fixed(shape):
    return pl.BlockSpec(shape, lambda *_: (0,) * len(shape))


def local(
    fields,
    residue,
    geometry,
    normals,
    face_scale,
    neighbours,
    send_faces,
    live_counts,
    sample_ids,
    sample_elems,
    sample_coords,
):
    const = {
        name: in_hbm(table) if isinstance(table, jax.Array) else table
        for name, table in constant_tables().items()
    }
    fields = in_hbm(jnp.transpose(fields, (1, 0, 2)))
    residue = in_hbm(jnp.transpose(residue, (1, 0, 2)))
    geometry, normals, face_scale = in_hbm(geometry), in_hbm(normals), in_hbm(face_scale)
    neighbours, sample_coords = in_hbm(neighbours), in_hbm(sample_coords)
    slot_count = fields.shape[2]
    slot_faces = 4 * slot_count
    bound_count = send_faces.shape[1]
    reach = 8 * bound_count
    samples = sample_ids.shape[0]
    devices = lax.axis_size(("px", "py"))
    shape = jax.ShapeDtypeStruct

    elems = in_hbm(sample_elems.reshape(1, samples))
    width = 512
    tiles = slot_count // width
    piece = (3, 48, LANES)

    up, down, left, right, faces = pl.pallas_call(
        functools.partial(pack_kernel, slot_faces),
        grid=(1,),
        in_specs=[
            pl.BlockSpec((NODES, 4, reach), lambda t: (0, 0, 0)),
            fixed((4, slot_count)),
            fixed((256, ROWS)),
        ],
        out_specs=[
            fixed(piece),
            fixed(piece),
            fixed(piece[1:]),
            fixed(piece[1:]),
            fixed((slot_faces // LANES, LANES)),
        ],
        out_shape=[
            pltpu.HBM(piece, f32),
            pltpu.HBM(piece, f32),
            pltpu.HBM(piece[1:], f32),
            pltpu.HBM(piece[1:], f32),
            shape((slot_faces // LANES, LANES), jnp.int32),
        ],
        scratch_shapes=[pltpu.VMEM((reach // LANES, ROWS, LANES), f32)],
        compiler_params=pltpu.CompilerParams(vmem_limit_bytes=16 << 20),
        name="pack",
    )(fields, neighbours, const["trace_select"])

    def steps_along(axis):
        count = lax.axis_size(axis)
        forward = [(i, i + 1) for i in range(count - 1)]
        return forward, [(target, source) for source, target in forward]

    forward, backward = steps_along("px")
    below = lax.ppermute(up, "px", backward)
    above = lax.ppermute(down, "px", forward)
    to_left, to_right = pl.pallas_call(
        relay_kernel,
        out_shape=[pltpu.HBM(piece, f32), pltpu.HBM(piece, f32)],
        name="relay",
    )(left, right, below, above)
    forward, backward = steps_along("py")
    from_right = lax.ppermute(to_left, "py", backward)
    from_left = lax.ppermute(to_right, "py", forward)

    bulk = 3 * width
    bulks = slot_count // bulk

    def behind(rank):
        return lambda t, *_: (0,) * rank + (jnp.maximum(t - bulks - 1, 0),)

    def ahead(rank):
        return lambda t, *_: (0,) * rank + (jnp.clip(t - bulks, 0, tiles - 1),)

    fields_next, residue_next, partial = pl.pallas_call(
        functools.partial(section_kernel, slot_count, reach),
        grid_spec=pltpu.PrefetchScalarGridSpec(
            num_scalar_prefetch=2,
            grid=(bulks + tiles + 1,),
            in_specs=[
                pl.BlockSpec((3, 4, width), ahead(2)),
                pl.BlockSpec((NODES, 4, bulk), lambda t, *_: (0, 0, jnp.minimum(t, bulks - 1))),
                pl.BlockSpec((NODES, 4, width), behind(2)),
                pl.BlockSpec((NODES, 4, width), behind(2)),
                pl.BlockSpec((9, width), behind(1)),
                pl.BlockSpec((3, 4, width), behind(2)),
                pl.BlockSpec((4, width), behind(1)),
                pl.BlockSpec((4, width), behind(1)),
                fixed((1, samples)),
                fixed((ROWS, 4 * LANES)),
                fixed((256, 2 * ROWS)),
                fixed((3 * ROWS, 96)),
                fixed((ROWS, 1024)),
            ],
            out_specs=[
                pl.BlockSpec((NODES, 4, width), behind(2)),
                pl.BlockSpec((NODES, 4, width), behind(2)),
                fixed((144, samples)),
            ],
            scratch_shapes=[
                pltpu.VMEM((slot_faces, LANES), f32),
                pltpu.VMEM((width // LANES, ROWS, LANES), f32),
                pltpu.VMEM((128, width), f32),
                pltpu.VMEM((48, width), f32),
                pltpu.VMEM((ROWS, width), f32),
                pltpu.VMEM((64, width), f32),
                pltpu.VMEM((64, width), f32),
                pltpu.VMEM((48, width), f32),
                pltpu.VMEM((width // 256, 2 * ROWS, 256), bf16),
                pltpu.VMEM((width // 256, 96, 256), bf16),
                pltpu.VMEM((width // 256, 256, 256), f32),
                pltpu.VMEM((width // 256, 1024, 256), bf16),
                *[pltpu.VMEM((LANES, LANES), f32)] * 4,
            ],
        ),
        out_shape=[
            shape(fields.shape, f32),
            shape(residue.shape, f32),
            shape((144, samples), f32),
        ],
        compiler_params=pltpu.CompilerParams(vmem_limit_bytes=48 << 20),
        name="section",
    )(
        faces.reshape(-1),
        live_counts,
        normals,
        fields,
        fields,
        residue,
        geometry,
        normals,
        face_scale,
        neighbours,
        elems,
        const["table_select"],
        const["twice_select"],
        const["from_p"],
        const["lift"],
    )

    def head(rank):
        return lambda t: (0,) * rank

    fields_next, residue_next, spread = pl.pallas_call(
        functools.partial(boundary_kernel, slot_faces, const["powers"], samples),
        grid=(1,),
        in_specs=[
            pl.BlockSpec((NODES, 4, reach), head(3)),
            pl.BlockSpec((NODES, 4, reach), head(3)),
            pl.BlockSpec((3, 4, reach), head(3)),
            pl.BlockSpec((4, reach), head(2)),
            pl.BlockSpec((4, reach), head(2)),
            fixed(piece),
            fixed(piece),
            fixed(piece),
            fixed(piece),
            fixed((1, samples)),
            fixed((1, samples)),
            fixed((3, samples)),
            fixed((144, samples)),
            fixed((ROWS, 1024)),
            fixed((PAD, PAD)),
        ],
        out_specs=[
            pl.BlockSpec((NODES, 4, reach), head(3)),
            pl.BlockSpec((NODES, 4, reach), head(3)),
            fixed((devices, 1, samples)),
        ],
        out_shape=[
            shape(fields.shape, f32),
            shape(residue.shape, f32),
            shape((devices, 1, samples), f32),
        ],
        scratch_shapes=[
            pltpu.VMEM((64, reach), f32),
            pltpu.VMEM((768, reach), bf16),
            pltpu.VMEM((ROWS, reach), f32),
            pltpu.VMEM((48, reach), f32),
            pltpu.VMEM((PAD, samples), f32),
        ],
        input_output_aliases={0: 0, 1: 1},
        compiler_params=pltpu.CompilerParams(vmem_limit_bytes=24 << 20),
        name="boundary",
    )(
        in_hbm(fields_next),
        in_hbm(residue_next),
        normals,
        face_scale,
        neighbours,
        from_right,
        from_left,
        below,
        above,
        elems,
        in_hbm(sample_ids.reshape(1, samples)),
        sample_coords,
        partial,
        const["lift"],
        const["inverse"],
    )
    received = lax.all_to_all(spread, ("px", "py"), 0, 0, tiled=True)

    receivers = samples // QPTS
    harmonic = np.tile(harmonic_table(), (1, receivers)).astype(np.float32)
    groups = (np.arange(samples)[None] // QPTS == np.arange(receivers)[:, None]).astype(np.float32)
    coefficients = pl.pallas_call(
        harmonic_kernel,
        out_shape=shape((receivers, harmonic.shape[0]), f32),
        name="harmonic",
    )(received, jnp.asarray(harmonic), jnp.asarray(groups))
    return (
        jnp.transpose(fields_next, (1, 0, 2)),
        jnp.transpose(residue_next, (1, 0, 2)),
        coefficients.T,
    )


def solution(mesh):
    placed = (
        P(None, None, ("px", "py")),
        P(None, None, ("px", "py")),
        P(None, ("px", "py")),
        P(None, None, ("px", "py")),
        P(None, ("px", "py")),
        P(None, ("px", "py")),
        P(None, ("px", "py")),
        P(("px", "py")),
        P(("px", "py")),
        P(("px", "py")),
        P(None, ("px", "py")),
    )
    return jax.shard_map(
        local,
        mesh=mesh,
        in_specs=placed,
        out_specs=(P(None, None, ("px", "py")), P(None, None, ("px", "py")), P(None, ("px", "py"))),
        check_vma=False,
    )
```

```python
import functools
import math

import jax
import jax.numpy as jnp
import numpy as np
from jax import lax
from jax.experimental import pallas as pl
from jax.experimental.pallas import tpu as pltpu
from jax.sharding import PartitionSpec as P

QPTS = 50
NODES = 35
PAD = 40
FACE_ROWS = 16
ROWS = 144
LANES = 128
FACE_TILES = 4


highest = lax.Precision.HIGHEST
section_decay = -567301805773.0 / 1357537059087.0
section_gain = 5161836677717.0 / 13612068292357.0
time_step = 0.01
f32 = jnp.float32
bf16 = jnp.bfloat16


def exponent_table():
    listing = []
    for degree in range(5):
        for third in range(degree + 1):
            for second in range(degree + 1 - third):
                listing.append((degree - second - third, second, third))
    return np.array(listing)


def factorials(values):
    lookup = np.array([float(math.factorial(level)) for level in range(24)])
    return lookup[values]


def eliminate(matrix, right_hand):
    order_size = matrix.shape[0]
    work = np.concatenate([matrix, right_hand], axis=1).astype(float)
    for pivot_col in range(order_size):
        best = max(range(pivot_col, order_size), key=lambda row_id: abs(work[row_id, pivot_col]))
        work[[pivot_col, best]] = work[[best, pivot_col]]
        work[pivot_col] = work[pivot_col] / work[pivot_col, pivot_col]
        for row_id in range(order_size):
            if row_id != pivot_col:
                work[row_id] = work[row_id] - work[row_id, pivot_col] * work[pivot_col]
    return work[:, order_size:]


def element_tables():
    powers = exponent_table()
    points = powers / 4.0
    vander = np.prod(points[:, None, :] ** powers[None, :, :], axis=2)
    inverse = eliminate(vander, np.eye(35))
    derivs = []
    for axis_id in range(3):
        lowered = np.maximum(powers - (np.arange(3) == axis_id)[None, :], 0)
        slope_table = powers[None, :, axis_id] * np.prod(
            points[:, None, :] ** lowered[None, :, :], axis=2
        )
        derivs.append(slope_table @ inverse)
    summed = powers[:, None, :] + powers[None, :, :]
    exp_r = summed[..., 0]
    exp_s = summed[..., 1]
    exp_t = summed[..., 2]
    volume = (
        factorials(exp_r)
        * factorials(exp_s)
        * factorials(exp_t)
        / factorials(exp_r + exp_s + exp_t + 3)
    )
    mass_matrix = inverse.T @ volume @ inverse
    face_grams = [
        np.where(
            exp_t == 0, factorials(exp_r) * factorials(exp_s) / factorials(exp_r + exp_s + 2), 0.0
        ),
        np.where(
            exp_s == 0, factorials(exp_r) * factorials(exp_t) / factorials(exp_r + exp_t + 2), 0.0
        ),
        factorials(exp_r)
        * factorials(exp_s)
        * factorials(exp_t)
        / factorials(exp_r + exp_s + exp_t + 2),
        np.where(
            exp_r == 0, factorials(exp_s) * factorials(exp_t) / factorials(exp_s + exp_t + 2), 0.0
        ),
    ]
    listed = [tuple((int(entry) for entry in powers[node_id])) for node_id in range(35)]
    face_nodes = np.array(
        [
            [node_id for node_id in range(35) if listed[node_id][2] == 0],
            [node_id for node_id in range(35) if listed[node_id][1] == 0],
            [node_id for node_id in range(35) if sum(listed[node_id]) == 4],
            [node_id for node_id in range(35) if listed[node_id][0] == 0],
        ]
    )
    surface = np.zeros((35, 60))
    for face_id in range(4):
        face_mass = inverse.T @ face_grams[face_id] @ inverse
        for node_id in range(15):
            surface[:, 4 * node_id + face_id] = face_mass[:, face_nodes[face_id, node_id]]
    lifting = eliminate(mass_matrix, surface)
    return (np.stack(derivs), lifting, face_nodes, inverse, powers)


def associated(degree, order, cosine, sine):
    current = cosine * 0.0 + 1.0
    for step_id in range(1, order + 1):
        current = -(2 * step_id - 1) * sine * current
    if degree == order:
        return current
    following = cosine * (2 * order + 1) * current
    for level in range(order + 2, degree + 1):
        current, following = (
            following,
            ((2 * level - 1) * cosine * following - (level + order - 1) * current)
            / (level - order),
        )
    return following


def harmonic_table():
    inner_node = math.sqrt(5.0 - 2.0 * math.sqrt(10.0 / 7.0)) / 3.0
    outer_node = math.sqrt(5.0 + 2.0 * math.sqrt(10.0 / 7.0)) / 3.0
    inner_weight = (322.0 + 13.0 * math.sqrt(70.0)) / 900.0
    outer_weight = (322.0 - 13.0 * math.sqrt(70.0)) / 900.0
    cosines = np.array([-outer_node, -inner_node, 0.0, inner_node, outer_node])
    weights = np.array([outer_weight, inner_weight, 128.0 / 225.0, inner_weight, outer_weight])
    azimuth = 2.0 * np.pi * (np.arange(10) + 0.5) / 10.0
    polar = np.repeat(cosines, 10)
    circle = np.tile(azimuth, 5)
    point_weight = np.repeat(weights, 10) * 2.0 * np.pi / 10.0
    sine = np.sqrt(1.0 - polar**2)
    table_rows = []
    for degree in range(5):
        for order in range(-degree, degree + 1):
            absolute = abs(order)
            legendre = associated(degree, absolute, polar, sine)
            factor = math.sqrt(
                (2 * degree + 1)
                / (4.0 * math.pi)
                * math.factorial(degree - absolute)
                / math.factorial(degree + absolute)
            )
            if order > 0:
                angular = math.sqrt(2.0) * np.cos(order * circle)
            elif order < 0:
                angular = math.sqrt(2.0) * np.sin(absolute * circle)
            else:
                angular = circle * 0.0 + 1.0
            table_rows.append(factor * legendre * angular * point_weight)
    return np.array(table_rows)


def constant_tables():
    derivs, lifting, face_nodes, inverse, powers = element_tables()
    table_select = np.zeros((ROWS, 4 * LANES), np.float32)
    trace_select = np.zeros((4 * 4 * FACE_ROWS, ROWS), np.float32)
    for face in range(4):
        for field in range(4):
            for place in range(15):
                source = 4 * face_nodes[face, place] + field
                column = FACE_ROWS * field + place
                table_select[source, LANES * face + column] = 1.0
                table_select[source, LANES * face + 64 + column] = 1.0
                trace_select[64 * face + column, source] = 1.0
    whole = np.round(3.0 * derivs)
    into_p = np.zeros((ROWS, 128), np.float32)
    from_p = np.zeros((3 * ROWS, 48), np.float32)
    lift = np.zeros((ROWS, 256), np.float32)
    for node in range(NODES):
        for axis_id in range(3):
            into_p[4 * node, PAD * axis_id : PAD * axis_id + NODES] = -whole[axis_id, node]
            for field in range(1, 4):
                from_p[ROWS * axis_id + 4 * node + field, :NODES] = whole[axis_id, node]
        for face in range(4):
            for place in range(15):
                entry = lifting[node, 4 * place + face]
                column = FACE_ROWS * face + place
                lift[4 * node, column] = entry
                for field in range(1, 4):
                    lift[4 * node + field, 64 * field + column] = -entry
    lift_hi = lift.astype(jnp.bfloat16)
    lift_lo = (lift - lift_hi.astype(np.float32)).astype(jnp.bfloat16)
    return {
        "table_select": jnp.asarray(np.concatenate([table_select] * 2, axis=0), bf16),
        "trace_select": jnp.asarray(trace_select, bf16),
        "twice_select": jnp.asarray(np.concatenate([trace_select] * 2, axis=1), bf16),
        "from_p": jnp.asarray(np.concatenate([from_p, from_p], axis=1), bf16),
        "lift": jnp.asarray(
            np.concatenate(
                [lift_hi, lift_lo, lift_hi] + [into_p.astype(jnp.bfloat16)] * 2, axis=1
            )
        ),
        "inverse": jnp.asarray(np.pad(inverse.T, ((0, 5), (0, 5))), f32),
        "powers": powers,
    }


def halves(values):
    high = values.astype(bf16)
    return high, (values - high.astype(f32)).astype(bf16)


def thirds(values):
    high = values.astype(bf16)
    rest = values - high.astype(f32)
    middle = rest.astype(bf16)
    return high, middle, (rest - middle.astype(f32)).astype(bf16)


def product(left, right, dims=((1,), (0,))):
    return lax.dot_general(left, right, (dims, ((), ())), preferred_element_type=f32)


def stack_nodes(fields_ref, stacked):
    tiles = range(stacked.shape[0])
    for tile in tiles:
        for node in range(NODES):
            stacked[tile, 4 * node : 4 * node + 4, :] = fields_ref[
                node, :, LANES * tile : LANES * tile + LANES
            ]
    return halves(jnp.concatenate([stacked[tile] for tile in tiles], axis=1))


def one_field(stacked, field):
    tiles = range(stacked.shape[0])
    rows = pl.ds(field, NODES, stride=4)
    return jnp.concatenate([stacked[tile, rows, :] for tile in tiles], axis=1)


def pack_kernel(
    slot_faces,
    fields_ref,
    codes_ref,
    select_ref,
    up_ref,
    down_ref,
    left_ref,
    right_ref,
    faces_ref,
    stacked,
):
    stacked[...] = jnp.zeros_like(stacked)
    high, low = stack_nodes(fields_ref, stacked)
    traces = product(select_ref[...], high) + product(select_ref[...], low)
    reach = fields_ref.shape[2]
    count = reach // 8
    chosen = jnp.zeros((64, reach), f32)
    for face in range(4):
        remote = codes_ref[face : face + 1, 0:reach] >= slot_faces
        chosen = jnp.where(remote, traces[64 * face : 64 * face + 64, :], chosen)
    homes = [up_ref.at[0], up_ref.at[1], up_ref.at[2], left_ref, right_ref]
    homes += [down_ref.at[0], down_ref.at[1], down_ref.at[2]]
    for heading, home in enumerate(homes):
        part = chosen[:, count * heading : count * heading + count]
        home[:, 0:96] = part[0:48]
        for third in range(3):
            home[16 * third : 16 * third + 16, 96:128] = part[48:64, 32 * third : 32 * third + 32]
    tiles = codes_ref.shape[1] // LANES
    codes = codes_ref[...]
    codes = jnp.where((codes >= 0) & (codes < slot_faces), codes, 0)
    for face in range(4):
        for tile in range(tiles):
            row = 4 * FACE_TILES * (tile // FACE_TILES) + FACE_TILES * face + tile % FACE_TILES
            faces_ref[row : row + 1, :] = codes[
                face : face + 1, LANES * tile : LANES * tile + LANES
            ]


def relay_kernel(left_ref, right_ref, below_ref, above_ref, to_left_ref, to_right_ref):
    to_left_ref[0] = left_ref[...]
    to_left_ref[1] = below_ref[0]
    to_left_ref[2] = above_ref[0]
    to_right_ref[0] = right_ref[...]
    to_right_ref[1] = below_ref[2]
    to_right_ref[2] = above_ref[2]


def build_rows(first, part, fields_ref, select_ref, table_ref, stacked):
    slot_count = table_ref.shape[0] // 4
    width = LANES * stacked.shape[0]
    high, low = stack_nodes(fields_ref.at[:, :, width * part : width * part + width], stacked)
    both = jnp.concatenate([high, low], axis=0)
    for half in range(2):
        select = select_ref[:, 256 * half : 256 * half + 256]
        rows = product(both, select, ((0,), (0,)))
        for side in range(2):
            start = pl.multiple_of((2 * half + side) * slot_count + first + width * part, width)
            table_ref[pl.ds(start, width), :] = rows[:, LANES * side : LANES * side + LANES]


def gather_pieces(faces_ref, table_ref, normals_ref, outer_ref, rows_refs):
    width = outer_ref.shape[1]
    left_half = lax.broadcasted_iota(jnp.int32, (1, LANES), 1) < 64

    def load(tile, rows):
        for row in rows:
            at = tile * LANES + row
            for half in range(2):
                one = table_ref[pl.ds(faces_ref[2 * half * width + at], 1), :]
                two = table_ref[pl.ds(faces_ref[(2 * half + 1) * width + at], 1), :]
                rows_ref = rows_refs[2 * (tile % 2) + half]
                rows_ref[row : row + 1, :] = jnp.where(left_half, one, two)

    def combine(tile, half):
        turned = rows_refs[2 * (tile % 2) + half][...].T
        lanes = slice(tile * LANES, tile * LANES + LANES)
        for side in range(2):
            face = 2 * half + side
            part = turned[64 * side : 64 * side + 64, :]
            total = -part[0:16]
            for axis_id in range(3):
                facing = normals_ref[axis_id, face : face + 1, lanes]
                total = total + facing * part[16 + 16 * axis_id : 32 + 16 * axis_id]
            outer_ref[FACE_ROWS * face : FACE_ROWS * face + FACE_ROWS, lanes] = total

    for tile in range(width // LANES):
        for part in range(8):
            rows = range(16 * part, 16 * part + 16)
            yield functools.partial(load, tile, rows)
            if tile > 0 and part < 2:
                yield functools.partial(combine, tile - 1, part)
    for half in range(2):
        yield functools.partial(combine, tile, half)


def section_kernel(
    slot_count,
    reach,
    live_ref,
    faces_hbm,
    next_normals_ref,
    bulk_ref,
    fields_ref,
    residue_ref,
    geometry_ref,
    normals_ref,
    scale_ref,
    codes_ref,
    elems_ref,
    table_select_ref,
    select_ref,
    from_ref,
    lift_ref,
    fields_out,
    residue_out,
    sampled,
    table_ref,
    stacked,
    combined,
    slow,
    rates,
    outer,
    beyond_ref,
    pressure,
    fields_split,
    slow_split,
    inner,
    sources,
    even_faces,
    odd_faces,
    arrived,
    *rows_refs,
):
    faces_refs = (even_faces, odd_faces)
    width = fields_ref.shape[2]
    tiles = slot_count // width
    bulks = slot_count // bulk_ref.shape[2]
    step = pl.program_id(0) - bulks
    slot_faces = 4 * slot_count
    half_width = 256

    def codes_copy(tile, parity):
        source = faces_hbm.at[pl.ds(pl.multiple_of(tile * 4 * width, 4 * width), 4 * width)]
        return pltpu.make_async_copy(source, faces_refs[parity], arrived.at[parity])

    def gather(parity):
        return gather_pieces(
            faces_refs[parity], table_ref, next_normals_ref, outer, rows_refs
        )

    def take_codes(parity):
        codes_copy(step, parity).wait()

        @pl.when(step < tiles - 1)
        def _():
            codes_copy(step + 1, 1 - parity).start()

    def update_pieces():
        first = (step - 1) * width

        def stack(at, low, high):
            for tile in range(2 * at, 2 * at + 2):
                for node in range(low, high):
                    stacked[tile, 4 * node : 4 * node + 4, :] = fields_ref[
                        node, :, LANES * tile : LANES * tile + LANES
                    ]

        def split(at):
            for side in range(2):
                lanes = slice(LANES * side, LANES * side + LANES)
                high, low = halves(stacked[2 * at + side])
                fields_split[at, 0:ROWS, lanes] = high
                fields_split[at, ROWS : 2 * ROWS, lanes] = low

        def inside(at):
            return slice(half_width * at, half_width * at + half_width)

        def field_rows(at, field):
            rows = pl.ds(field, NODES, stride=4)
            return jnp.concatenate([stacked[tile, rows, :] for tile in (2 * at, 2 * at + 1)], axis=1)

        def copy_slow(at):
            lanes = inside(at)
            slow[0:NODES, lanes] = field_rows(at, 0)
            slow_split[at, 0:48, :], slow_split[at, 48:96, :] = halves(slow[:, lanes])

        def weigh(at, axis_id):
            lanes = inside(at)
            weighted = jnp.zeros((NODES, half_width), f32)
            for direction in range(3):
                row = 3 * axis_id + direction
                factor = geometry_ref[row : row + 1, lanes] * (1.0 / 3.0)
                weighted = weighted + factor * field_rows(at, 1 + direction)
            combined[PAD * axis_id : PAD * axis_id + NODES, lanes] = weighted

        def split_weighted(at):
            high, low = halves(combined[:, inside(at)])
            sources[at, 768:896, :], sources[at, 896:1024, :] = high, low

        def traces(at):
            inner[at] = product(select_ref[...], fields_split[at])

        def slope(at, axis_id):
            lanes = inside(at)
            place = lax.broadcasted_iota(jnp.int32, (8, half_width), 0) & 3
            value = product(from_ref[ROWS * axis_id : ROWS * axis_id + ROWS, :], slow_split[at])
            pattern = jnp.zeros((8, half_width), f32)
            for direction in range(3):
                row = 3 * axis_id + direction
                factor = geometry_ref[row : row + 1, lanes] * (1.0 / 3.0)
                pattern = jnp.where(place == direction + 1, factor, pattern)
            value = value.reshape(ROWS // 8, 8, half_width) * pattern[None]
            value = value.reshape(ROWS, half_width)
            if axis_id == 0:
                rates[:, lanes] = value
            else:
                rates[:, lanes] += value

        def keep_split(at, start, value):
            high, low = halves(value)
            rows = value.shape[0]
            sources[at, start : start + rows, :] = high
            sources[at, 256 + start : 256 + start + rows, :] = high
            sources[at, 512 + start : 512 + start + rows, :] = low

        def jump(at, face):
            lanes = inside(at)
            inner_p = inner[at, 64 * face : 64 * face + 16, :]
            along = jnp.zeros_like(inner_p)
            for axis_id in range(3):
                facing = normals_ref[axis_id, face : face + 1, lanes]
                start = 64 * face + 16 + 16 * axis_id
                along = along + facing * inner[at, start : start + 16, :]
            wall = codes_ref[face : face + 1, lanes] < 0
            beyond = beyond_ref[FACE_ROWS * face : FACE_ROWS * face + FACE_ROWS, lanes]
            beyond = jnp.where(wall, -along - inner_p, beyond)
            beyond = jnp.where(codes_ref[face : face + 1, lanes] >= slot_faces, 0.0, beyond)
            scale = 0.5 * scale_ref[face : face + 1, lanes]
            value = scale * (along - inner_p - beyond)
            keep_split(at, FACE_ROWS * face, value)
            for axis_id in range(3):
                start = 64 + 64 * axis_id + FACE_ROWS * face
                keep_split(at, start, normals_ref[axis_id, face : face + 1, lanes] * value)

        def lift(at):
            lanes = inside(at)
            rates[:, lanes] = product(lift_ref[...], sources[at]) - rates[:, lanes]

        def advance(at, low, high):
            lanes = inside(at)
            slots = lax.broadcasted_iota(jnp.int32, (1, half_width), 1) + (first + half_width * at)
            keep = slots < live_ref[0]
            for node in range(low, high):
                rate = rates[4 * node : 4 * node + 4, lanes]
                residue_next = section_decay * residue_ref[node, :, lanes] + time_step * rate
                fields_next = fields_ref[node, :, lanes] + section_gain * residue_next
                fields_next = jnp.where(keep, fields_next, 0.0)
                fields_out[node, :, lanes] = fields_next
                residue_out[node, :, lanes] = jnp.where(keep, residue_next, 0.0)
                pressure[node : node + 1, lanes] = fields_next[0:1]

        def sample(at):
            lanes = inside(at)
            parts = jnp.concatenate(thirds(pressure[:, lanes]), axis=0)
            start = first + half_width * at
            slots = lax.broadcasted_iota(jnp.int32, (half_width, elems_ref.shape[1]), 0) + start
            elems = elems_ref[...]
            picks = (slots == elems) & (elems >= reach)
            sampled[...] += product(parts, jnp.where(picks, 1.0, 0.0).astype(bf16))

        call = functools.partial

        def stages(at):
            sevens = range(0, NODES, 7)
            return [
                [call(stack, at, low, low + 7) for low in sevens] + [call(split, at)],
                [call(copy_slow, at)]
                + [call(weigh, at, axis_id) for axis_id in range(3)]
                + [call(split_weighted, at), call(traces, at)],
                [call(slope, at, axis_id) for axis_id in range(3)],
                [call(jump, at, face) for face in range(4)],
                [call(lift, at)],
                [call(advance, at, low, low + 7) for low in sevens],
                [call(sample, at)],
            ]

        both = [stages(at) for at in range(width // half_width)]
        depth = len(both[0])
        return [
            [piece for lag, chain in enumerate(both) if 0 <= at - lag < depth for piece in chain[at - lag]]
            for at in range(depth + len(both) - 1)
        ]

    def interleave(gathers, groups):
        gathers = list(gathers)

        def run(at, updates, groups):
            @pl.when(live_ref[0] > at)
            def _():
                low = at * len(gathers) // len(groups)
                loads = gathers[low : (at + 1) * len(gathers) // len(groups)]
                for place in range(max(len(loads), len(updates))):
                    for piece in loads[place : place + 1] + updates[place : place + 1]:
                        piece()

        cuts = (0, 4, 8)
        groups = [sum(groups[low:high], []) for low, high in zip(cuts, cuts[1:])]
        for at, updates in enumerate(groups):
            run(at, updates, groups)

    @pl.when(step == -bulks)
    def _():
        stacked[...] = jnp.zeros_like(stacked)
        combined[...] = jnp.zeros_like(combined)
        slow[...] = jnp.zeros_like(slow)
        pressure[...] = jnp.zeros_like(pressure)
        sampled[...] = jnp.zeros_like(sampled)

    @pl.when(step < 0)
    def _():
        first = (step + bulks) * bulk_ref.shape[2]
        for part in range(bulk_ref.shape[2] // width):
            build_rows(first, part, bulk_ref, table_select_ref, table_ref, stacked)

    @pl.when(step == -1)
    def _():
        codes_copy(0, 0).start()

    @pl.when(step == 0)
    def _():
        take_codes(0)
        for piece in gather(0):
            piece()

    for parity in range(2):

        @pl.when((step > 0) & (step < tiles) & (step % 2 == parity))
        def _():
            take_codes(parity)
            beyond_ref[...] = outer[...]
            interleave(gather(parity), update_pieces())

    @pl.when(step == tiles)
    def _():
        beyond_ref[...] = outer[...]
        for stage in update_pieces():
            for piece in stage:
                piece()


def boundary_kernel(
    slot_faces,
    powers,
    group,
    fields_ref,
    residue_ref,
    normals_ref,
    scale_ref,
    codes_ref,
    right_ref,
    left_ref,
    below_ref,
    above_ref,
    elems_ref,
    ids_ref,
    coords_ref,
    partial_ref,
    lift_ref,
    inverse_ref,
    fields_out,
    residue_out,
    spread_ref,
    remote,
    sources,
    rates,
    pressure,
    monomials,
):
    reach = fields_ref.shape[2]
    bound_count = reach // 8
    pressure[...] = jnp.zeros_like(pressure)
    monomials[...] = jnp.zeros_like(monomials)
    arrivals = [
        left_ref[2],
        above_ref[1],
        right_ref[2],
        left_ref[0],
        right_ref[0],
        left_ref[1],
        below_ref[1],
        right_ref[1],
    ]
    for heading, source in enumerate(arrivals):
        start = bound_count * heading
        remote[0:48, start : start + 96] = source[:, 0:96]
        for third in range(3):
            place = start + 32 * third
            remote[48:64, place : place + 32] = source[16 * third : 16 * third + 16, 96:128]

    def keep_split(start, value):
        high, low = halves(value)
        sources[start : start + FACE_ROWS, :] = high
        sources[256 + start : 256 + start + FACE_ROWS, :] = high
        sources[512 + start : 512 + start + FACE_ROWS, :] = low

    for face in range(4):
        beyond = -remote[0:16, :]
        for axis_id in range(3):
            facing = normals_ref[axis_id, face : face + 1, :]
            beyond = beyond + facing * remote[16 + 16 * axis_id : 32 + 16 * axis_id, :]
        is_remote = codes_ref[face : face + 1, :] >= slot_faces
        flux = jnp.where(is_remote, -0.5 * scale_ref[face : face + 1, :] * beyond, 0.0)
        keep_split(FACE_ROWS * face, flux)
        for axis_id in range(3):
            facing = normals_ref[axis_id, face : face + 1, :]
            keep_split(64 + 64 * axis_id + FACE_ROWS * face, facing * flux)
    rates[...] = time_step * product(lift_ref[:, 0:768], sources[...])
    for node in range(NODES):
        rate = rates[4 * node : 4 * node + 4, :]
        residue_out[node] = residue_ref[node] + rate
        fields_next = fields_ref[node] + section_gain * rate
        fields_out[node] = fields_next
        pressure[node : node + 1, :] = fields_next[0:1]
    parts = jnp.concatenate(thirds(pressure[...]), axis=0)
    slots = lax.broadcasted_iota(jnp.int32, (reach, elems_ref.shape[1]), 0)
    picks = jnp.where(slots == elems_ref[...], 1.0, 0.0).astype(bf16)
    sampled = partial_ref[...] + product(parts, picks)
    ladders = []
    for axis_id in range(3):
        base = coords_ref[axis_id : axis_id + 1, :]
        square = base * base
        ladders.append([jnp.ones_like(base), base, square, square * base, square * square])
    for node in range(NODES):
        exps = [int(entry) for entry in powers[node]]
        monomials[node : node + 1, :] = (
            ladders[0][exps[0]] * ladders[1][exps[1]] * ladders[2][exps[2]]
        )
    basis = jnp.dot(
        inverse_ref[...], monomials[...], precision=highest, preferred_element_type=f32
    )
    gathered = sampled[0:PAD, :] + sampled[48 : 48 + PAD, :] + sampled[96 : 96 + PAD, :]
    values = jnp.sum(basis * gathered, axis=0, keepdims=True)
    ids = ids_ref[...]
    owner = lax.shift_right_logical(ids * 5243, 20)
    place = ids - group * owner
    owners = lax.broadcasted_iota(jnp.int32, (spread_ref.shape[0], ids.shape[1]), 0)
    held = jnp.where(owners == owner, values, 0.0)
    places = lax.broadcasted_iota(jnp.int32, (spread_ref.shape[2], ids.shape[1]), 0)
    chosen = jnp.where(places == place, 1.0, 0.0).astype(bf16)
    spread = jnp.zeros((spread_ref.shape[0], spread_ref.shape[2]), f32)
    for part in thirds(held):
        spread = spread + product(part, chosen, ((1,), (1,)))
    spread_ref[:, 0, :] = spread


def harmonic_kernel(received_ref, table_ref, groups_ref, out_ref):
    mine = jnp.sum(received_ref[...], axis=0)
    weighted = groups_ref[...] * mine
    out_ref[...] = lax.dot_general(
        weighted,
        table_ref[...],
        (((1,), (1,)), ((), ())),
        precision=highest,
        preferred_element_type=f32,
    )


def in_hbm(array):
    return pltpu.with_memory_space_constraint(array, pltpu.HBM)


def fixed(shape):
    return pl.BlockSpec(shape, lambda *_: (0,) * len(shape))


def local(
    fields,
    residue,
    geometry,
    normals,
    face_scale,
    neighbours,
    send_faces,
    live_counts,
    sample_ids,
    sample_elems,
    sample_coords,
):
    const = {
        name: in_hbm(table) if isinstance(table, jax.Array) else table
        for name, table in constant_tables().items()
    }
    fields = in_hbm(jnp.transpose(fields, (1, 0, 2)))
    residue = in_hbm(jnp.transpose(residue, (1, 0, 2)))
    geometry, normals, face_scale = in_hbm(geometry), in_hbm(normals), in_hbm(face_scale)
    neighbours, sample_coords = in_hbm(neighbours), in_hbm(sample_coords)
    slot_count = fields.shape[2]
    slot_faces = 4 * slot_count
    bound_count = send_faces.shape[1]
    reach = 8 * bound_count
    samples = sample_ids.shape[0]
    devices = lax.axis_size(("px", "py"))
    shape = jax.ShapeDtypeStruct

    elems = in_hbm(sample_elems.reshape(1, samples))
    width = LANES * FACE_TILES
    tiles = slot_count // width
    piece = (3, 48, LANES)

    up, down, left, right, faces = pl.pallas_call(
        functools.partial(pack_kernel, slot_faces),
        grid=(1,),
        in_specs=[
            pl.BlockSpec((NODES, 4, reach), lambda t: (0, 0, 0)),
            fixed((4, slot_count)),
            fixed((256, ROWS)),
        ],
        out_specs=[
            fixed(piece),
            fixed(piece),
            fixed(piece[1:]),
            fixed(piece[1:]),
            fixed((slot_faces // LANES, LANES)),
        ],
        out_shape=[
            pltpu.HBM(piece, f32),
            pltpu.HBM(piece, f32),
            pltpu.HBM(piece[1:], f32),
            pltpu.HBM(piece[1:], f32),
            shape((slot_faces // LANES, LANES), jnp.int32),
        ],
        scratch_shapes=[pltpu.VMEM((reach // LANES, ROWS, LANES), f32)],
        compiler_params=pltpu.CompilerParams(vmem_limit_bytes=16 << 20),
        name="pack",
    )(fields, neighbours, const["trace_select"])

    def steps_along(axis):
        count = lax.axis_size(axis)
        forward = [(i, i + 1) for i in range(count - 1)]
        return forward, [(target, source) for source, target in forward]

    forward, backward = steps_along("px")
    below = lax.ppermute(up, "px", backward)
    above = lax.ppermute(down, "px", forward)
    to_left, to_right = pl.pallas_call(
        relay_kernel,
        out_shape=[pltpu.HBM(piece, f32), pltpu.HBM(piece, f32)],
        name="relay",
    )(left, right, below, above)
    forward, backward = steps_along("py")
    from_right = lax.ppermute(to_left, "py", backward)
    from_left = lax.ppermute(to_right, "py", forward)

    bulk = 3 * width
    bulks = slot_count // bulk

    def behind(rank):
        return lambda t, *_: (0,) * rank + (jnp.maximum(t - bulks - 1, 0),)

    def ahead(rank):
        return lambda t, *_: (0,) * rank + (jnp.clip(t - bulks, 0, tiles - 1),)

    fields_next, residue_next, partial = pl.pallas_call(
        functools.partial(section_kernel, slot_count, reach),
        grid_spec=pltpu.PrefetchScalarGridSpec(
            num_scalar_prefetch=1,
            grid=(bulks + tiles + 1,),
            in_specs=[
                pl.BlockSpec(memory_space=pltpu.HBM),
                pl.BlockSpec((3, 4, width), ahead(2)),
                pl.BlockSpec((NODES, 4, bulk), lambda t, *_: (0, 0, jnp.minimum(t, bulks - 1))),
                pl.BlockSpec((NODES, 4, width), behind(2)),
                pl.BlockSpec((NODES, 4, width), behind(2)),
                pl.BlockSpec((9, width), behind(1)),
                pl.BlockSpec((3, 4, width), behind(2)),
                pl.BlockSpec((4, width), behind(1)),
                pl.BlockSpec((4, width), behind(1)),
                fixed((1, samples)),
                fixed((2 * ROWS, 4 * LANES)),
                fixed((256, 2 * ROWS)),
                fixed((3 * ROWS, 96)),
                fixed((ROWS, 1024)),
            ],
            out_specs=[
                pl.BlockSpec((NODES, 4, width), behind(2)),
                pl.BlockSpec((NODES, 4, width), behind(2)),
                fixed((144, samples)),
            ],
            scratch_shapes=[
                pltpu.VMEM((slot_faces, LANES), f32),
                pltpu.VMEM((width // LANES, ROWS, LANES), f32),
                pltpu.VMEM((128, width), f32),
                pltpu.VMEM((48, width), f32),
                pltpu.VMEM((ROWS, width), f32),
                pltpu.VMEM((64, width), f32),
                pltpu.VMEM((64, width), f32),
                pltpu.VMEM((48, width), f32),
                pltpu.VMEM((width // 256, 2 * ROWS, 256), bf16),
                pltpu.VMEM((width // 256, 96, 256), bf16),
                pltpu.VMEM((width // 256, 256, 256), f32),
                pltpu.VMEM((width // 256, 1024, 256), bf16),
                pltpu.SMEM((4 * width,), jnp.int32),
                pltpu.SMEM((4 * width,), jnp.int32),
                pltpu.SemaphoreType.DMA((2,)),
                *[pltpu.VMEM((LANES, LANES), f32)] * 4,
            ],
        ),
        out_shape=[
            shape(fields.shape, f32),
            shape(residue.shape, f32),
            shape((144, samples), f32),
        ],
        compiler_params=pltpu.CompilerParams(vmem_limit_bytes=48 << 20),
        name="section",
    )(
        live_counts,
        in_hbm(faces.reshape(-1)),
        normals,
        fields,
        fields,
        residue,
        geometry,
        normals,
        face_scale,
        neighbours,
        elems,
        const["table_select"],
        const["twice_select"],
        const["from_p"],
        const["lift"],
    )

    def head(rank):
        return lambda t: (0,) * rank

    fields_next, residue_next, spread = pl.pallas_call(
        functools.partial(boundary_kernel, slot_faces, const["powers"], samples),
        grid=(1,),
        in_specs=[
            pl.BlockSpec((NODES, 4, reach), head(3)),
            pl.BlockSpec((NODES, 4, reach), head(3)),
            pl.BlockSpec((3, 4, reach), head(3)),
            pl.BlockSpec((4, reach), head(2)),
            pl.BlockSpec((4, reach), head(2)),
            fixed(piece),
            fixed(piece),
            fixed(piece),
            fixed(piece),
            fixed((1, samples)),
            fixed((1, samples)),
            fixed((3, samples)),
            fixed((144, samples)),
            fixed((ROWS, 1024)),
            fixed((PAD, PAD)),
        ],
        out_specs=[
            pl.BlockSpec((NODES, 4, reach), head(3)),
            pl.BlockSpec((NODES, 4, reach), head(3)),
            fixed((devices, 1, samples)),
        ],
        out_shape=[
            shape(fields.shape, f32),
            shape(residue.shape, f32),
            shape((devices, 1, samples), f32),
        ],
        scratch_shapes=[
            pltpu.VMEM((64, reach), f32),
            pltpu.VMEM((768, reach), bf16),
            pltpu.VMEM((ROWS, reach), f32),
            pltpu.VMEM((48, reach), f32),
            pltpu.VMEM((PAD, samples), f32),
        ],
        input_output_aliases={0: 0, 1: 1},
        compiler_params=pltpu.CompilerParams(vmem_limit_bytes=24 << 20),
        name="boundary",
    )(
        in_hbm(fields_next),
        in_hbm(residue_next),
        normals,
        face_scale,
        neighbours,
        from_right,
        from_left,
        below,
        above,
        elems,
        in_hbm(sample_ids.reshape(1, samples)),
        sample_coords,
        partial,
        const["lift"],
        const["inverse"],
    )
    received = lax.all_to_all(spread, ("px", "py"), 0, 0, tiled=True)

    receivers = samples // QPTS
    harmonic = np.tile(harmonic_table(), (1, receivers)).astype(np.float32)
    groups = (np.arange(samples)[None] // QPTS == np.arange(receivers)[:, None]).astype(np.float32)
    coefficients = pl.pallas_call(
        harmonic_kernel,
        out_shape=shape((receivers, harmonic.shape[0]), f32),
        name="harmonic",
    )(received, jnp.asarray(harmonic), jnp.asarray(groups))
    return (
        jnp.transpose(fields_next, (1, 0, 2)),
        jnp.transpose(residue_next, (1, 0, 2)),
        coefficients.T,
    )


def solution(mesh):
    placed = (
        P(None, None, ("px", "py")),
        P(None, None, ("px", "py")),
        P(None, ("px", "py")),
        P(None, None, ("px", "py")),
        P(None, ("px", "py")),
        P(None, ("px", "py")),
        P(None, ("px", "py")),
        P(("px", "py")),
        P(("px", "py")),
        P(("px", "py")),
        P(None, ("px", "py")),
    )
    return jax.shard_map(
        local,
        mesh=mesh,
        in_specs=placed,
        out_specs=(P(None, None, ("px", "py")), P(None, None, ("px", "py")), P(None, ("px", "py"))),
        check_vma=False,
    )
```

```python
import functools
import math

import jax
import jax.numpy as jnp
import numpy as np
from jax import lax
from jax.experimental import pallas as pl
from jax.experimental.pallas import tpu as pltpu
from jax.sharding import PartitionSpec as P

QPTS = 50
NODES = 35
PAD = 40
FACE_ROWS = 16
ROWS = 144
LANES = 128
FACE_TILES = 4


highest = lax.Precision.HIGHEST
section_decay = -567301805773.0 / 1357537059087.0
section_gain = 5161836677717.0 / 13612068292357.0
time_step = 0.01
f32 = jnp.float32
bf16 = jnp.bfloat16


def exponent_table():
    listing = []
    for degree in range(5):
        for third in range(degree + 1):
            for second in range(degree + 1 - third):
                listing.append((degree - second - third, second, third))
    return np.array(listing)


def factorials(values):
    lookup = np.array([float(math.factorial(level)) for level in range(24)])
    return lookup[values]


def eliminate(matrix, right_hand):
    order_size = matrix.shape[0]
    work = np.concatenate([matrix, right_hand], axis=1).astype(float)
    for pivot_col in range(order_size):
        best = max(range(pivot_col, order_size), key=lambda row_id: abs(work[row_id, pivot_col]))
        work[[pivot_col, best]] = work[[best, pivot_col]]
        work[pivot_col] = work[pivot_col] / work[pivot_col, pivot_col]
        for row_id in range(order_size):
            if row_id != pivot_col:
                work[row_id] = work[row_id] - work[row_id, pivot_col] * work[pivot_col]
    return work[:, order_size:]


def element_tables():
    powers = exponent_table()
    points = powers / 4.0
    vander = np.prod(points[:, None, :] ** powers[None, :, :], axis=2)
    inverse = eliminate(vander, np.eye(35))
    derivs = []
    for axis_id in range(3):
        lowered = np.maximum(powers - (np.arange(3) == axis_id)[None, :], 0)
        slope_table = powers[None, :, axis_id] * np.prod(
            points[:, None, :] ** lowered[None, :, :], axis=2
        )
        derivs.append(slope_table @ inverse)
    summed = powers[:, None, :] + powers[None, :, :]
    exp_r = summed[..., 0]
    exp_s = summed[..., 1]
    exp_t = summed[..., 2]
    volume = (
        factorials(exp_r)
        * factorials(exp_s)
        * factorials(exp_t)
        / factorials(exp_r + exp_s + exp_t + 3)
    )
    mass_matrix = inverse.T @ volume @ inverse
    face_grams = [
        np.where(
            exp_t == 0, factorials(exp_r) * factorials(exp_s) / factorials(exp_r + exp_s + 2), 0.0
        ),
        np.where(
            exp_s == 0, factorials(exp_r) * factorials(exp_t) / factorials(exp_r + exp_t + 2), 0.0
        ),
        factorials(exp_r)
        * factorials(exp_s)
        * factorials(exp_t)
        / factorials(exp_r + exp_s + exp_t + 2),
        np.where(
            exp_r == 0, factorials(exp_s) * factorials(exp_t) / factorials(exp_s + exp_t + 2), 0.0
        ),
    ]
    listed = [tuple((int(entry) for entry in powers[node_id])) for node_id in range(35)]
    face_nodes = np.array(
        [
            [node_id for node_id in range(35) if listed[node_id][2] == 0],
            [node_id for node_id in range(35) if listed[node_id][1] == 0],
            [node_id for node_id in range(35) if sum(listed[node_id]) == 4],
            [node_id for node_id in range(35) if listed[node_id][0] == 0],
        ]
    )
    surface = np.zeros((35, 60))
    for face_id in range(4):
        face_mass = inverse.T @ face_grams[face_id] @ inverse
        for node_id in range(15):
            surface[:, 4 * node_id + face_id] = face_mass[:, face_nodes[face_id, node_id]]
    lifting = eliminate(mass_matrix, surface)
    return (np.stack(derivs), lifting, face_nodes, inverse, powers)


def associated(degree, order, cosine, sine):
    current = cosine * 0.0 + 1.0
    for step_id in range(1, order + 1):
        current = -(2 * step_id - 1) * sine * current
    if degree == order:
        return current
    following = cosine * (2 * order + 1) * current
    for level in range(order + 2, degree + 1):
        current, following = (
            following,
            ((2 * level - 1) * cosine * following - (level + order - 1) * current)
            / (level - order),
        )
    return following


def harmonic_table():
    inner_node = math.sqrt(5.0 - 2.0 * math.sqrt(10.0 / 7.0)) / 3.0
    outer_node = math.sqrt(5.0 + 2.0 * math.sqrt(10.0 / 7.0)) / 3.0
    inner_weight = (322.0 + 13.0 * math.sqrt(70.0)) / 900.0
    outer_weight = (322.0 - 13.0 * math.sqrt(70.0)) / 900.0
    cosines = np.array([-outer_node, -inner_node, 0.0, inner_node, outer_node])
    weights = np.array([outer_weight, inner_weight, 128.0 / 225.0, inner_weight, outer_weight])
    azimuth = 2.0 * np.pi * (np.arange(10) + 0.5) / 10.0
    polar = np.repeat(cosines, 10)
    circle = np.tile(azimuth, 5)
    point_weight = np.repeat(weights, 10) * 2.0 * np.pi / 10.0
    sine = np.sqrt(1.0 - polar**2)
    table_rows = []
    for degree in range(5):
        for order in range(-degree, degree + 1):
            absolute = abs(order)
            legendre = associated(degree, absolute, polar, sine)
            factor = math.sqrt(
                (2 * degree + 1)
                / (4.0 * math.pi)
                * math.factorial(degree - absolute)
                / math.factorial(degree + absolute)
            )
            if order > 0:
                angular = math.sqrt(2.0) * np.cos(order * circle)
            elif order < 0:
                angular = math.sqrt(2.0) * np.sin(absolute * circle)
            else:
                angular = circle * 0.0 + 1.0
            table_rows.append(factor * legendre * angular * point_weight)
    return np.array(table_rows)


def constant_tables():
    derivs, lifting, face_nodes, inverse, powers = element_tables()
    table_select = np.zeros((ROWS, 4 * LANES), np.float32)
    trace_select = np.zeros((4 * 4 * FACE_ROWS, ROWS), np.float32)
    for face in range(4):
        for field in range(4):
            for place in range(15):
                source = 4 * face_nodes[face, place] + field
                column = FACE_ROWS * field + place
                table_select[source, LANES * face + column] = 1.0
                table_select[source, LANES * face + 64 + column] = 1.0
                trace_select[64 * face + column, source] = 1.0
    whole = np.round(3.0 * derivs)
    into_p = np.zeros((ROWS, 128), np.float32)
    from_p = np.zeros((3 * ROWS, 48), np.float32)
    lift = np.zeros((ROWS, 256), np.float32)
    for node in range(NODES):
        for axis_id in range(3):
            into_p[4 * node, PAD * axis_id : PAD * axis_id + NODES] = -whole[axis_id, node]
            for field in range(1, 4):
                from_p[ROWS * axis_id + 4 * node + field, :NODES] = whole[axis_id, node]
        for face in range(4):
            for place in range(15):
                entry = lifting[node, 4 * place + face]
                column = FACE_ROWS * face + place
                lift[4 * node, column] = entry
                for field in range(1, 4):
                    lift[4 * node + field, 64 * field + column] = -entry
    lift_hi = lift.astype(jnp.bfloat16)
    lift_lo = (lift - lift_hi.astype(np.float32)).astype(jnp.bfloat16)
    return {
        "table_select": jnp.asarray(np.concatenate([table_select] * 2, axis=0), bf16),
        "trace_select": jnp.asarray(trace_select, bf16),
        "twice_select": jnp.asarray(np.concatenate([trace_select] * 2, axis=1), bf16),
        "from_p": jnp.asarray(np.concatenate([from_p, from_p], axis=1), bf16),
        "lift": jnp.asarray(
            np.concatenate(
                [lift_hi, lift_lo, lift_hi] + [into_p.astype(jnp.bfloat16)] * 2, axis=1
            )
        ),
        "inverse": jnp.asarray(np.pad(inverse.T, ((0, 5), (0, 5))), f32),
        "powers": powers,
    }


def halves(values):
    high = values.astype(bf16)
    return high, (values - high.astype(f32)).astype(bf16)


def thirds(values):
    high = values.astype(bf16)
    rest = values - high.astype(f32)
    middle = rest.astype(bf16)
    return high, middle, (rest - middle.astype(f32)).astype(bf16)


def product(left, right, dims=((1,), (0,))):
    return lax.dot_general(left, right, (dims, ((), ())), preferred_element_type=f32)


def stack_nodes(fields_ref, stacked):
    tiles = range(stacked.shape[0])
    for tile in tiles:
        for node in range(NODES):
            stacked[tile, 4 * node : 4 * node + 4, :] = fields_ref[
                node, :, LANES * tile : LANES * tile + LANES
            ]
    return halves(jnp.concatenate([stacked[tile] for tile in tiles], axis=1))


def one_field(stacked, field):
    tiles = range(stacked.shape[0])
    rows = pl.ds(field, NODES, stride=4)
    return jnp.concatenate([stacked[tile, rows, :] for tile in tiles], axis=1)


def pack_kernel(
    slot_faces,
    fields_ref,
    codes_ref,
    select_ref,
    up_ref,
    down_ref,
    left_ref,
    right_ref,
    faces_ref,
    stacked,
):
    stacked[...] = jnp.zeros_like(stacked)
    high, low = stack_nodes(fields_ref, stacked)
    traces = product(select_ref[...], high) + product(select_ref[...], low)
    reach = fields_ref.shape[2]
    count = reach // 8
    chosen = jnp.zeros((64, reach), f32)
    for face in range(4):
        remote = codes_ref[face : face + 1, 0:reach] >= slot_faces
        chosen = jnp.where(remote, traces[64 * face : 64 * face + 64, :], chosen)
    homes = [up_ref.at[0], up_ref.at[1], up_ref.at[2], left_ref, right_ref]
    homes += [down_ref.at[0], down_ref.at[1], down_ref.at[2]]
    for heading, home in enumerate(homes):
        part = chosen[:, count * heading : count * heading + count]
        home[:, 0:96] = part[0:48]
        for third in range(3):
            home[16 * third : 16 * third + 16, 96:128] = part[48:64, 32 * third : 32 * third + 32]
    tiles = codes_ref.shape[1] // LANES
    codes = codes_ref[...]
    codes = jnp.where((codes >= 0) & (codes < slot_faces), codes, 0)
    for face in range(4):
        for tile in range(tiles):
            row = 4 * FACE_TILES * (tile // FACE_TILES) + FACE_TILES * face + tile % FACE_TILES
            faces_ref[row : row + 1, :] = codes[
                face : face + 1, LANES * tile : LANES * tile + LANES
            ]


def relay_kernel(left_ref, right_ref, below_ref, above_ref, to_left_ref, to_right_ref):
    to_left_ref[0] = left_ref[...]
    to_left_ref[1] = below_ref[0]
    to_left_ref[2] = above_ref[0]
    to_right_ref[0] = right_ref[...]
    to_right_ref[1] = below_ref[2]
    to_right_ref[2] = above_ref[2]


def build_rows(first, part, fields_ref, select_ref, table_ref, stacked):
    slot_count = table_ref.shape[0] // 4
    width = LANES * stacked.shape[0]
    high, low = stack_nodes(fields_ref.at[:, :, width * part : width * part + width], stacked)
    both = jnp.concatenate([high, low], axis=0)
    for half in range(2):
        select = select_ref[:, 256 * half : 256 * half + 256]
        rows = product(both, select, ((0,), (0,)))
        for side in range(2):
            start = pl.multiple_of((2 * half + side) * slot_count + first + width * part, width)
            table_ref[pl.ds(start, width), :] = rows[:, LANES * side : LANES * side + LANES]


def gather_pieces(faces_ref, table_ref, normals_ref, outer_ref, rows_refs):
    width = outer_ref.shape[1]
    left_half = lax.broadcasted_iota(jnp.int32, (1, LANES), 1) < 64

    def load(tile, rows):
        for row in rows:
            at = tile * LANES + row
            for half in range(2):
                one = table_ref[pl.ds(faces_ref[2 * half * width + at], 1), :]
                two = table_ref[pl.ds(faces_ref[(2 * half + 1) * width + at], 1), :]
                rows_ref = rows_refs[2 * (tile % 2) + half]
                rows_ref[row : row + 1, :] = jnp.where(left_half, one, two)

    def combine(tile, half):
        turned = rows_refs[2 * (tile % 2) + half][...].T
        lanes = slice(tile * LANES, tile * LANES + LANES)
        for side in range(2):
            face = 2 * half + side
            part = turned[64 * side : 64 * side + 64, :]
            total = -part[0:16]
            for axis_id in range(3):
                facing = normals_ref[axis_id, face : face + 1, lanes]
                total = total + facing * part[16 + 16 * axis_id : 32 + 16 * axis_id]
            outer_ref[FACE_ROWS * face : FACE_ROWS * face + FACE_ROWS, lanes] = total

    for tile in range(width // LANES):
        for part in range(8):
            rows = range(16 * part, 16 * part + 16)
            yield functools.partial(load, tile, rows)
            if tile > 0 and part < 2:
                yield functools.partial(combine, tile - 1, part)
    for half in range(2):
        yield functools.partial(combine, tile, half)


def section_kernel(
    slot_count,
    reach,
    live_ref,
    faces_hbm,
    next_normals_ref,
    bulk_ref,
    fields_ref,
    residue_ref,
    geometry_ref,
    normals_ref,
    scale_ref,
    codes_ref,
    elems_ref,
    table_select_ref,
    select_ref,
    from_ref,
    lift_ref,
    fields_out,
    residue_out,
    sampled,
    table_ref,
    stacked,
    combined,
    slow,
    rates,
    outer,
    beyond_ref,
    pressure,
    fields_split,
    slow_split,
    inner,
    sources,
    even_faces,
    odd_faces,
    arrived,
    *rows_refs,
):
    faces_refs = (even_faces, odd_faces)
    width = fields_ref.shape[2]
    tiles = slot_count // width
    bulks = slot_count // bulk_ref.shape[2]
    step = pl.program_id(0) - bulks
    slot_faces = 4 * slot_count
    half_width = 256

    def codes_copy(tile, parity):
        source = faces_hbm.at[pl.ds(pl.multiple_of(tile * 4 * width, 4 * width), 4 * width)]
        return pltpu.make_async_copy(source, faces_refs[parity], arrived.at[parity])

    def gather(parity):
        return gather_pieces(
            faces_refs[parity], table_ref, next_normals_ref, outer, rows_refs
        )

    def take_codes(parity):
        codes_copy(step, parity).wait()

        @pl.when((step + 1) * width < live_ref[0])
        def _():
            codes_copy(step + 1, 1 - parity).start()

    def update_pieces():
        first = (step - 1) * width

        def stack(at, low, high):
            for tile in range(2 * at, 2 * at + 2):
                for node in range(low, high):
                    stacked[tile, 4 * node : 4 * node + 4, :] = fields_ref[
                        node, :, LANES * tile : LANES * tile + LANES
                    ]

        def split(at):
            for side in range(2):
                lanes = slice(LANES * side, LANES * side + LANES)
                high, low = halves(stacked[2 * at + side])
                fields_split[at, 0:ROWS, lanes] = high
                fields_split[at, ROWS : 2 * ROWS, lanes] = low

        def inside(at):
            return slice(half_width * at, half_width * at + half_width)

        def field_rows(at, field):
            rows = pl.ds(field, NODES, stride=4)
            return jnp.concatenate([stacked[tile, rows, :] for tile in (2 * at, 2 * at + 1)], axis=1)

        def copy_slow(at):
            lanes = inside(at)
            slow[0:NODES, lanes] = field_rows(at, 0)
            slow_split[at, 0:48, :], slow_split[at, 48:96, :] = halves(slow[:, lanes])

        def weigh(at, axis_id):
            lanes = inside(at)
            weighted = jnp.zeros((NODES, half_width), f32)
            for direction in range(3):
                row = 3 * axis_id + direction
                factor = geometry_ref[row : row + 1, lanes] * (1.0 / 3.0)
                weighted = weighted + factor * field_rows(at, 1 + direction)
            combined[PAD * axis_id : PAD * axis_id + NODES, lanes] = weighted

        def split_weighted(at):
            high, low = halves(combined[:, inside(at)])
            sources[at, 768:896, :], sources[at, 896:1024, :] = high, low

        def traces(at):
            inner[at] = product(select_ref[...], fields_split[at])

        def slope(at, axis_id):
            lanes = inside(at)
            place = lax.broadcasted_iota(jnp.int32, (8, half_width), 0) & 3
            value = product(from_ref[ROWS * axis_id : ROWS * axis_id + ROWS, :], slow_split[at])
            pattern = jnp.zeros((8, half_width), f32)
            for direction in range(3):
                row = 3 * axis_id + direction
                factor = geometry_ref[row : row + 1, lanes] * (1.0 / 3.0)
                pattern = jnp.where(place == direction + 1, factor, pattern)
            value = value.reshape(ROWS // 8, 8, half_width) * pattern[None]
            value = value.reshape(ROWS, half_width)
            if axis_id == 0:
                rates[:, lanes] = value
            else:
                rates[:, lanes] += value

        def keep_split(at, start, value):
            high, low = halves(value)
            rows = value.shape[0]
            sources[at, start : start + rows, :] = high
            sources[at, 256 + start : 256 + start + rows, :] = high
            sources[at, 512 + start : 512 + start + rows, :] = low

        def jump(at, face):
            lanes = inside(at)
            inner_p = inner[at, 64 * face : 64 * face + 16, :]
            along = jnp.zeros_like(inner_p)
            for axis_id in range(3):
                facing = normals_ref[axis_id, face : face + 1, lanes]
                start = 64 * face + 16 + 16 * axis_id
                along = along + facing * inner[at, start : start + 16, :]
            wall = codes_ref[face : face + 1, lanes] < 0
            beyond = beyond_ref[FACE_ROWS * face : FACE_ROWS * face + FACE_ROWS, lanes]
            beyond = jnp.where(wall, -along - inner_p, beyond)
            beyond = jnp.where(codes_ref[face : face + 1, lanes] >= slot_faces, 0.0, beyond)
            scale = 0.5 * scale_ref[face : face + 1, lanes]
            value = scale * (along - inner_p - beyond)
            keep_split(at, FACE_ROWS * face, value)
            for axis_id in range(3):
                start = 64 + 64 * axis_id + FACE_ROWS * face
                keep_split(at, start, normals_ref[axis_id, face : face + 1, lanes] * value)

        def lift(at):
            lanes = inside(at)
            rates[:, lanes] = product(lift_ref[...], sources[at]) - rates[:, lanes]

        def advance(at, low, high):
            lanes = inside(at)
            slots = lax.broadcasted_iota(jnp.int32, (1, half_width), 1) + (first + half_width * at)
            keep = slots < live_ref[0]
            for node in range(low, high):
                rate = rates[4 * node : 4 * node + 4, lanes]
                residue_next = section_decay * residue_ref[node, :, lanes] + time_step * rate
                fields_next = fields_ref[node, :, lanes] + section_gain * residue_next
                fields_next = jnp.where(keep, fields_next, 0.0)
                fields_out[node, :, lanes] = fields_next
                residue_out[node, :, lanes] = jnp.where(keep, residue_next, 0.0)
                pressure[node : node + 1, lanes] = fields_next[0:1]

        def sample(at):
            lanes = inside(at)
            parts = jnp.concatenate(thirds(pressure[:, lanes]), axis=0)
            start = first + half_width * at
            slots = lax.broadcasted_iota(jnp.int32, (half_width, elems_ref.shape[1]), 0) + start
            elems = elems_ref[...]
            picks = (slots == elems) & (elems >= reach)
            sampled[...] += product(parts, jnp.where(picks, 1.0, 0.0).astype(bf16))

        call = functools.partial

        def stages(at):
            sevens = range(0, NODES, 7)
            return [
                [call(stack, at, low, low + 7) for low in sevens] + [call(split, at)],
                [call(copy_slow, at)]
                + [call(weigh, at, axis_id) for axis_id in range(3)]
                + [call(split_weighted, at), call(traces, at)],
                [call(slope, at, axis_id) for axis_id in range(3)],
                [call(jump, at, face) for face in range(4)],
                [call(lift, at)],
                [call(advance, at, low, low + 7) for low in sevens],
                [call(sample, at)],
            ]

        both = [stages(at) for at in range(width // half_width)]
        depth = len(both[0])
        return [
            [piece for lag, chain in enumerate(both) if 0 <= at - lag < depth for piece in chain[at - lag]]
            for at in range(depth + len(both) - 1)
        ]

    def interleave(gathers, groups):
        gathers = list(gathers)

        def run(at, updates, groups):
            @pl.when(live_ref[0] > at)
            def _():
                low = at * len(gathers) // len(groups)
                loads = gathers[low : (at + 1) * len(gathers) // len(groups)]
                for place in range(max(len(loads), len(updates))):
                    for piece in loads[place : place + 1] + updates[place : place + 1]:
                        piece()

        cuts = (0, 4, 8)
        groups = [sum(groups[low:high], []) for low, high in zip(cuts, cuts[1:])]
        for at, updates in enumerate(groups):
            run(at, updates, groups)

    @pl.when(step == -bulks)
    def _():
        stacked[...] = jnp.zeros_like(stacked)
        combined[...] = jnp.zeros_like(combined)
        slow[...] = jnp.zeros_like(slow)
        pressure[...] = jnp.zeros_like(pressure)
        sampled[...] = jnp.zeros_like(sampled)

    @pl.when(step < 0)
    def _():
        first = (step + bulks) * bulk_ref.shape[2]
        for part in range(bulk_ref.shape[2] // width):

            @pl.when(first + width * part < live_ref[0])
            def _():
                build_rows(first, part, bulk_ref, table_select_ref, table_ref, stacked)

    @pl.when(step == -1)
    def _():
        codes_copy(0, 0).start()

    @pl.when(step == 0)
    def _():
        take_codes(0)
        for piece in gather(0):
            piece()

    for parity in range(2):

        @pl.when((step > 0) & (step * width < live_ref[0]) & (step % 2 == parity))
        def _():
            take_codes(parity)
            beyond_ref[...] = outer[...]
            interleave(gather(parity), update_pieces())

    @pl.when((step > 0) & ((step - 1) * width >= live_ref[0]))
    def _():
        fields_out[...] = jnp.zeros_like(fields_out)
        residue_out[...] = jnp.zeros_like(residue_out)

    @pl.when((step > 0) & ((step - 1) * width < live_ref[0]) & (step * width >= live_ref[0]))
    def _():
        beyond_ref[...] = outer[...]
        for stage in update_pieces():
            for piece in stage:
                piece()


def boundary_kernel(
    slot_faces,
    powers,
    group,
    fields_ref,
    residue_ref,
    normals_ref,
    scale_ref,
    codes_ref,
    right_ref,
    left_ref,
    below_ref,
    above_ref,
    elems_ref,
    ids_ref,
    coords_ref,
    partial_ref,
    lift_ref,
    inverse_ref,
    fields_out,
    residue_out,
    spread_ref,
    remote,
    sources,
    rates,
    pressure,
    monomials,
):
    reach = fields_ref.shape[2]
    bound_count = reach // 8
    pressure[...] = jnp.zeros_like(pressure)
    monomials[...] = jnp.zeros_like(monomials)
    arrivals = [
        left_ref[2],
        above_ref[1],
        right_ref[2],
        left_ref[0],
        right_ref[0],
        left_ref[1],
        below_ref[1],
        right_ref[1],
    ]
    for heading, source in enumerate(arrivals):
        start = bound_count * heading
        remote[0:48, start : start + 96] = source[:, 0:96]
        for third in range(3):
            place = start + 32 * third
            remote[48:64, place : place + 32] = source[16 * third : 16 * third + 16, 96:128]

    def keep_split(start, value):
        high, low = halves(value)
        sources[start : start + FACE_ROWS, :] = high
        sources[256 + start : 256 + start + FACE_ROWS, :] = high
        sources[512 + start : 512 + start + FACE_ROWS, :] = low

    for face in range(4):
        beyond = -remote[0:16, :]
        for axis_id in range(3):
            facing = normals_ref[axis_id, face : face + 1, :]
            beyond = beyond + facing * remote[16 + 16 * axis_id : 32 + 16 * axis_id, :]
        is_remote = codes_ref[face : face + 1, :] >= slot_faces
        flux = jnp.where(is_remote, -0.5 * scale_ref[face : face + 1, :] * beyond, 0.0)
        keep_split(FACE_ROWS * face, flux)
        for axis_id in range(3):
            facing = normals_ref[axis_id, face : face + 1, :]
            keep_split(64 + 64 * axis_id + FACE_ROWS * face, facing * flux)
    rates[...] = time_step * product(lift_ref[:, 0:768], sources[...])
    for node in range(NODES):
        rate = rates[4 * node : 4 * node + 4, :]
        residue_out[node] = residue_ref[node] + rate
        fields_next = fields_ref[node] + section_gain * rate
        fields_out[node] = fields_next
        pressure[node : node + 1, :] = fields_next[0:1]
    parts = jnp.concatenate(thirds(pressure[...]), axis=0)
    slots = lax.broadcasted_iota(jnp.int32, (reach, elems_ref.shape[1]), 0)
    picks = jnp.where(slots == elems_ref[...], 1.0, 0.0).astype(bf16)
    sampled = partial_ref[...] + product(parts, picks)
    ladders = []
    for axis_id in range(3):
        base = coords_ref[axis_id : axis_id + 1, :]
        square = base * base
        ladders.append([jnp.ones_like(base), base, square, square * base, square * square])
    for node in range(NODES):
        exps = [int(entry) for entry in powers[node]]
        monomials[node : node + 1, :] = (
            ladders[0][exps[0]] * ladders[1][exps[1]] * ladders[2][exps[2]]
        )
    basis = jnp.dot(
        inverse_ref[...], monomials[...], precision=highest, preferred_element_type=f32
    )
    gathered = sampled[0:PAD, :] + sampled[48 : 48 + PAD, :] + sampled[96 : 96 + PAD, :]
    values = jnp.sum(basis * gathered, axis=0, keepdims=True)
    ids = ids_ref[...]
    owner = lax.shift_right_logical(ids * 5243, 20)
    place = ids - group * owner
    owners = lax.broadcasted_iota(jnp.int32, (spread_ref.shape[0], ids.shape[1]), 0)
    held = jnp.where(owners == owner, values, 0.0)
    places = lax.broadcasted_iota(jnp.int32, (spread_ref.shape[2], ids.shape[1]), 0)
    chosen = jnp.where(places == place, 1.0, 0.0).astype(bf16)
    spread = jnp.zeros((spread_ref.shape[0], spread_ref.shape[2]), f32)
    for part in thirds(held):
        spread = spread + product(part, chosen, ((1,), (1,)))
    spread_ref[:, 0, :] = spread


def harmonic_kernel(received_ref, table_ref, groups_ref, out_ref):
    mine = jnp.sum(received_ref[...], axis=0)
    weighted = groups_ref[...] * mine
    out_ref[...] = lax.dot_general(
        weighted,
        table_ref[...],
        (((1,), (1,)), ((), ())),
        precision=highest,
        preferred_element_type=f32,
    )


def in_hbm(array):
    return pltpu.with_memory_space_constraint(array, pltpu.HBM)


def in_vmem(array):
    return pltpu.with_memory_space_constraint(array, pltpu.VMEM)


def fixed(shape):
    return pl.BlockSpec(shape, lambda *_: (0,) * len(shape))


def local(
    fields,
    residue,
    geometry,
    normals,
    face_scale,
    neighbours,
    send_faces,
    live_counts,
    sample_ids,
    sample_elems,
    sample_coords,
):
    const = {
        name: in_hbm(table) if isinstance(table, jax.Array) else table
        for name, table in constant_tables().items()
    }
    fields = in_hbm(jnp.transpose(fields, (1, 0, 2)))
    residue = in_hbm(jnp.transpose(residue, (1, 0, 2)))
    geometry, normals, face_scale = in_hbm(geometry), in_hbm(normals), in_hbm(face_scale)
    neighbours, sample_coords = in_hbm(neighbours), in_hbm(sample_coords)
    slot_count = fields.shape[2]
    slot_faces = 4 * slot_count
    bound_count = send_faces.shape[1]
    reach = 8 * bound_count
    samples = sample_ids.shape[0]
    devices = lax.axis_size(("px", "py"))
    shape = jax.ShapeDtypeStruct

    elems = in_hbm(sample_elems.reshape(1, samples))
    width = LANES * FACE_TILES
    tiles = slot_count // width
    piece = (3, 48, LANES)

    up, down, left, right, faces = pl.pallas_call(
        functools.partial(pack_kernel, slot_faces),
        grid=(1,),
        in_specs=[
            pl.BlockSpec((NODES, 4, reach), lambda t: (0, 0, 0)),
            fixed((4, slot_count)),
            fixed((256, ROWS)),
        ],
        out_specs=[
            fixed(piece),
            fixed(piece),
            fixed(piece[1:]),
            fixed(piece[1:]),
            fixed((slot_faces // LANES, LANES)),
        ],
        out_shape=[
            pltpu.HBM(piece, f32),
            pltpu.HBM(piece, f32),
            pltpu.HBM(piece[1:], f32),
            pltpu.HBM(piece[1:], f32),
            pltpu.HBM((slot_faces // LANES, LANES), jnp.int32),
        ],
        scratch_shapes=[pltpu.VMEM((reach // LANES, ROWS, LANES), f32)],
        compiler_params=pltpu.CompilerParams(vmem_limit_bytes=16 << 20),
        name="pack",
    )(fields, neighbours, const["trace_select"])

    def steps_along(axis):
        count = lax.axis_size(axis)
        forward = [(i, i + 1) for i in range(count - 1)]
        return forward, [(target, source) for source, target in forward]

    forward, backward = steps_along("px")
    below = lax.ppermute(up, "px", backward)
    above = lax.ppermute(down, "px", forward)
    to_left, to_right = pl.pallas_call(
        relay_kernel,
        out_shape=[pltpu.HBM(piece, f32), pltpu.HBM(piece, f32)],
        name="relay",
    )(left, right, in_vmem(below), in_vmem(above))
    forward, backward = steps_along("py")
    from_right = lax.ppermute(to_left, "py", backward)
    from_left = lax.ppermute(to_right, "py", forward)

    bulk = 3 * width
    bulks = slot_count // bulk

    def behind(rank):
        return lambda t, *_: (0,) * rank + (jnp.maximum(t - bulks - 1, 0),)

    def ahead(rank):
        return lambda t, *_: (0,) * rank + (jnp.clip(t - bulks, 0, tiles - 1),)

    fields_next, residue_next, partial = pl.pallas_call(
        functools.partial(section_kernel, slot_count, reach),
        grid_spec=pltpu.PrefetchScalarGridSpec(
            num_scalar_prefetch=1,
            grid=(bulks + tiles + 1,),
            in_specs=[
                pl.BlockSpec(memory_space=pltpu.HBM),
                pl.BlockSpec((3, 4, width), ahead(2)),
                pl.BlockSpec((NODES, 4, bulk), lambda t, *_: (0, 0, jnp.minimum(t, bulks - 1))),
                pl.BlockSpec((NODES, 4, width), behind(2)),
                pl.BlockSpec((NODES, 4, width), behind(2)),
                pl.BlockSpec((9, width), behind(1)),
                pl.BlockSpec((3, 4, width), behind(2)),
                pl.BlockSpec((4, width), behind(1)),
                pl.BlockSpec((4, width), behind(1)),
                fixed((1, samples)),
                fixed((2 * ROWS, 4 * LANES)),
                fixed((256, 2 * ROWS)),
                fixed((3 * ROWS, 96)),
                fixed((ROWS, 1024)),
            ],
            out_specs=[
                pl.BlockSpec((NODES, 4, width), behind(2)),
                pl.BlockSpec((NODES, 4, width), behind(2)),
                fixed((144, samples)),
            ],
            scratch_shapes=[
                pltpu.VMEM((slot_faces, LANES), f32),
                pltpu.VMEM((width // LANES, ROWS, LANES), f32),
                pltpu.VMEM((128, width), f32),
                pltpu.VMEM((48, width), f32),
                pltpu.VMEM((ROWS, width), f32),
                pltpu.VMEM((64, width), f32),
                pltpu.VMEM((64, width), f32),
                pltpu.VMEM((48, width), f32),
                pltpu.VMEM((width // 256, 2 * ROWS, 256), bf16),
                pltpu.VMEM((width // 256, 96, 256), bf16),
                pltpu.VMEM((width // 256, 256, 256), f32),
                pltpu.VMEM((width // 256, 1024, 256), bf16),
                pltpu.SMEM((4 * width,), jnp.int32),
                pltpu.SMEM((4 * width,), jnp.int32),
                pltpu.SemaphoreType.DMA((2,)),
                *[pltpu.VMEM((LANES, LANES), f32)] * 4,
            ],
        ),
        out_shape=[
            shape(fields.shape, f32),
            shape(residue.shape, f32),
            shape((144, samples), f32),
        ],
        compiler_params=pltpu.CompilerParams(vmem_limit_bytes=48 << 20),
        name="section",
    )(
        live_counts,
        in_hbm(faces.reshape(-1)),
        normals,
        fields,
        fields,
        residue,
        geometry,
        normals,
        face_scale,
        neighbours,
        elems,
        const["table_select"],
        const["twice_select"],
        const["from_p"],
        const["lift"],
    )

    def head(rank):
        return lambda t: (0,) * rank

    fields_next, residue_next, spread = pl.pallas_call(
        functools.partial(boundary_kernel, slot_faces, const["powers"], samples),
        grid=(1,),
        in_specs=[
            pl.BlockSpec((NODES, 4, reach), head(3)),
            pl.BlockSpec((NODES, 4, reach), head(3)),
            pl.BlockSpec((3, 4, reach), head(3)),
            pl.BlockSpec((4, reach), head(2)),
            pl.BlockSpec((4, reach), head(2)),
            fixed(piece),
            fixed(piece),
            fixed(piece),
            fixed(piece),
            fixed((1, samples)),
            fixed((1, samples)),
            fixed((3, samples)),
            fixed((144, samples)),
            fixed((ROWS, 1024)),
            fixed((PAD, PAD)),
        ],
        out_specs=[
            pl.BlockSpec((NODES, 4, reach), head(3)),
            pl.BlockSpec((NODES, 4, reach), head(3)),
            fixed((devices, 1, samples)),
        ],
        out_shape=[
            shape(fields.shape, f32),
            shape(residue.shape, f32),
            shape((devices, 1, samples), f32),
        ],
        scratch_shapes=[
            pltpu.VMEM((64, reach), f32),
            pltpu.VMEM((768, reach), bf16),
            pltpu.VMEM((ROWS, reach), f32),
            pltpu.VMEM((48, reach), f32),
            pltpu.VMEM((PAD, samples), f32),
        ],
        input_output_aliases={0: 0, 1: 1},
        compiler_params=pltpu.CompilerParams(vmem_limit_bytes=24 << 20),
        name="boundary",
    )(
        in_hbm(fields_next),
        in_hbm(residue_next),
        normals,
        face_scale,
        neighbours,
        from_right,
        from_left,
        below,
        above,
        elems,
        in_hbm(sample_ids.reshape(1, samples)),
        sample_coords,
        partial,
        const["lift"],
        const["inverse"],
    )
    received = lax.all_to_all(spread, ("px", "py"), 0, 0, tiled=True)

    receivers = samples // QPTS
    harmonic = np.tile(harmonic_table(), (1, receivers)).astype(np.float32)
    groups = (np.arange(samples)[None] // QPTS == np.arange(receivers)[:, None]).astype(np.float32)
    coefficients = pl.pallas_call(
        harmonic_kernel,
        out_shape=shape((receivers, harmonic.shape[0]), f32),
        name="harmonic",
    )(received, jnp.asarray(harmonic), jnp.asarray(groups))
    return (
        jnp.transpose(fields_next, (1, 0, 2)),
        jnp.transpose(residue_next, (1, 0, 2)),
        coefficients.T,
    )


def solution(mesh):
    placed = (
        P(None, None, ("px", "py")),
        P(None, None, ("px", "py")),
        P(None, ("px", "py")),
        P(None, None, ("px", "py")),
        P(None, ("px", "py")),
        P(None, ("px", "py")),
        P(None, ("px", "py")),
        P(("px", "py")),
        P(("px", "py")),
        P(("px", "py")),
        P(None, ("px", "py")),
    )
    return jax.shard_map(
        local,
        mesh=mesh,
        in_specs=placed,
        out_specs=(P(None, None, ("px", "py")), P(None, None, ("px", "py")), P(None, ("px", "py"))),
        check_vma=False,
    )
```

```python
import functools
import math

import jax
import jax.numpy as jnp
import numpy as np
from jax import lax
from jax.experimental import pallas as pl
from jax.experimental.pallas import tpu as pltpu
from jax.sharding import PartitionSpec as P

QPTS = 50
NODES = 35
PAD = 40
FACE_ROWS = 16
ROWS = 144
LANES = 128
FACE_TILES = 4


highest = lax.Precision.HIGHEST
section_decay = -567301805773.0 / 1357537059087.0
section_gain = 5161836677717.0 / 13612068292357.0
time_step = 0.01
f32 = jnp.float32
bf16 = jnp.bfloat16


def exponent_table():
    listing = []
    for degree in range(5):
        for third in range(degree + 1):
            for second in range(degree + 1 - third):
                listing.append((degree - second - third, second, third))
    return np.array(listing)


def factorials(values):
    lookup = np.array([float(math.factorial(level)) for level in range(24)])
    return lookup[values]


def eliminate(matrix, right_hand):
    order_size = matrix.shape[0]
    work = np.concatenate([matrix, right_hand], axis=1).astype(float)
    for pivot_col in range(order_size):
        best = max(range(pivot_col, order_size), key=lambda row_id: abs(work[row_id, pivot_col]))
        work[[pivot_col, best]] = work[[best, pivot_col]]
        work[pivot_col] = work[pivot_col] / work[pivot_col, pivot_col]
        for row_id in range(order_size):
            if row_id != pivot_col:
                work[row_id] = work[row_id] - work[row_id, pivot_col] * work[pivot_col]
    return work[:, order_size:]


def element_tables():
    powers = exponent_table()
    points = powers / 4.0
    vander = np.prod(points[:, None, :] ** powers[None, :, :], axis=2)
    inverse = eliminate(vander, np.eye(35))
    derivs = []
    for axis_id in range(3):
        lowered = np.maximum(powers - (np.arange(3) == axis_id)[None, :], 0)
        slope_table = powers[None, :, axis_id] * np.prod(
            points[:, None, :] ** lowered[None, :, :], axis=2
        )
        derivs.append(slope_table @ inverse)
    summed = powers[:, None, :] + powers[None, :, :]
    exp_r = summed[..., 0]
    exp_s = summed[..., 1]
    exp_t = summed[..., 2]
    volume = (
        factorials(exp_r)
        * factorials(exp_s)
        * factorials(exp_t)
        / factorials(exp_r + exp_s + exp_t + 3)
    )
    mass_matrix = inverse.T @ volume @ inverse
    face_grams = [
        np.where(
            exp_t == 0, factorials(exp_r) * factorials(exp_s) / factorials(exp_r + exp_s + 2), 0.0
        ),
        np.where(
            exp_s == 0, factorials(exp_r) * factorials(exp_t) / factorials(exp_r + exp_t + 2), 0.0
        ),
        factorials(exp_r)
        * factorials(exp_s)
        * factorials(exp_t)
        / factorials(exp_r + exp_s + exp_t + 2),
        np.where(
            exp_r == 0, factorials(exp_s) * factorials(exp_t) / factorials(exp_s + exp_t + 2), 0.0
        ),
    ]
    listed = [tuple((int(entry) for entry in powers[node_id])) for node_id in range(35)]
    face_nodes = np.array(
        [
            [node_id for node_id in range(35) if listed[node_id][2] == 0],
            [node_id for node_id in range(35) if listed[node_id][1] == 0],
            [node_id for node_id in range(35) if sum(listed[node_id]) == 4],
            [node_id for node_id in range(35) if listed[node_id][0] == 0],
        ]
    )
    surface = np.zeros((35, 60))
    for face_id in range(4):
        face_mass = inverse.T @ face_grams[face_id] @ inverse
        for node_id in range(15):
            surface[:, 4 * node_id + face_id] = face_mass[:, face_nodes[face_id, node_id]]
    lifting = eliminate(mass_matrix, surface)
    return (np.stack(derivs), lifting, face_nodes, inverse, powers)


def associated(degree, order, cosine, sine):
    current = cosine * 0.0 + 1.0
    for step_id in range(1, order + 1):
        current = -(2 * step_id - 1) * sine * current
    if degree == order:
        return current
    following = cosine * (2 * order + 1) * current
    for level in range(order + 2, degree + 1):
        current, following = (
            following,
            ((2 * level - 1) * cosine * following - (level + order - 1) * current)
            / (level - order),
        )
    return following


def harmonic_table():
    inner_node = math.sqrt(5.0 - 2.0 * math.sqrt(10.0 / 7.0)) / 3.0
    outer_node = math.sqrt(5.0 + 2.0 * math.sqrt(10.0 / 7.0)) / 3.0
    inner_weight = (322.0 + 13.0 * math.sqrt(70.0)) / 900.0
    outer_weight = (322.0 - 13.0 * math.sqrt(70.0)) / 900.0
    cosines = np.array([-outer_node, -inner_node, 0.0, inner_node, outer_node])
    weights = np.array([outer_weight, inner_weight, 128.0 / 225.0, inner_weight, outer_weight])
    azimuth = 2.0 * np.pi * (np.arange(10) + 0.5) / 10.0
    polar = np.repeat(cosines, 10)
    circle = np.tile(azimuth, 5)
    point_weight = np.repeat(weights, 10) * 2.0 * np.pi / 10.0
    sine = np.sqrt(1.0 - polar**2)
    table_rows = []
    for degree in range(5):
        for order in range(-degree, degree + 1):
            absolute = abs(order)
            legendre = associated(degree, absolute, polar, sine)
            factor = math.sqrt(
                (2 * degree + 1)
                / (4.0 * math.pi)
                * math.factorial(degree - absolute)
                / math.factorial(degree + absolute)
            )
            if order > 0:
                angular = math.sqrt(2.0) * np.cos(order * circle)
            elif order < 0:
                angular = math.sqrt(2.0) * np.sin(absolute * circle)
            else:
                angular = circle * 0.0 + 1.0
            table_rows.append(factor * legendre * angular * point_weight)
    return np.array(table_rows)


def constant_tables():
    derivs, lifting, face_nodes, inverse, powers = element_tables()
    table_select = np.zeros((ROWS, 4 * LANES), np.float32)
    trace_select = np.zeros((4 * 4 * FACE_ROWS, ROWS), np.float32)
    for face in range(4):
        for field in range(4):
            for place in range(15):
                source = 4 * face_nodes[face, place] + field
                column = FACE_ROWS * field + place
                table_select[source, LANES * face + column] = 1.0
                table_select[source, LANES * face + 64 + column] = 1.0
                trace_select[64 * face + column, source] = 1.0
    whole = np.round(3.0 * derivs)
    into_p = np.zeros((ROWS, 128), np.float32)
    from_p = np.zeros((3 * ROWS, 48), np.float32)
    lift = np.zeros((ROWS, 256), np.float32)
    for node in range(NODES):
        for axis_id in range(3):
            into_p[4 * node, PAD * axis_id : PAD * axis_id + NODES] = -whole[axis_id, node]
            for field in range(1, 4):
                from_p[ROWS * axis_id + 4 * node + field, :NODES] = whole[axis_id, node]
        for face in range(4):
            for place in range(15):
                entry = lifting[node, 4 * place + face]
                column = FACE_ROWS * face + place
                lift[4 * node, column] = entry
                for field in range(1, 4):
                    lift[4 * node + field, 64 * field + column] = -entry
    lift_hi = lift.astype(jnp.bfloat16)
    lift_lo = (lift - lift_hi.astype(np.float32)).astype(jnp.bfloat16)
    return {
        "table_select": jnp.asarray(np.concatenate([table_select] * 2, axis=0), bf16),
        "trace_select": jnp.asarray(trace_select, bf16),
        "twice_select": jnp.asarray(np.concatenate([trace_select] * 2, axis=1), bf16),
        "from_p": jnp.asarray(np.concatenate([from_p, from_p], axis=1), bf16),
        "lift": jnp.asarray(
            np.concatenate(
                [lift_hi, lift_lo, lift_hi] + [into_p.astype(jnp.bfloat16)] * 2, axis=1
            )
        ),
        "inverse": jnp.asarray(np.pad(inverse.T, ((0, 5), (0, 5))), f32),
        "powers": powers,
    }


def halves(values):
    high = values.astype(bf16)
    return high, (values - high.astype(f32)).astype(bf16)


def thirds(values):
    high = values.astype(bf16)
    rest = values - high.astype(f32)
    middle = rest.astype(bf16)
    return high, middle, (rest - middle.astype(f32)).astype(bf16)


def product(left, right, dims=((1,), (0,))):
    return lax.dot_general(left, right, (dims, ((), ())), preferred_element_type=f32)


def stack_nodes(fields_ref, stacked):
    tiles = range(stacked.shape[0])
    for tile in tiles:
        for node in range(NODES):
            stacked[tile, 4 * node : 4 * node + 4, :] = fields_ref[
                node, :, LANES * tile : LANES * tile + LANES
            ]
    return halves(jnp.concatenate([stacked[tile] for tile in tiles], axis=1))


def one_field(stacked, field):
    tiles = range(stacked.shape[0])
    rows = pl.ds(field, NODES, stride=4)
    return jnp.concatenate([stacked[tile, rows, :] for tile in tiles], axis=1)


def pack_kernel(
    slot_faces,
    fields_ref,
    codes_ref,
    select_ref,
    up_ref,
    down_ref,
    left_ref,
    right_ref,
    faces_ref,
    stacked,
):
    stacked[...] = jnp.zeros_like(stacked)
    high, low = stack_nodes(fields_ref, stacked)
    traces = product(select_ref[...], high) + product(select_ref[...], low)
    reach = fields_ref.shape[2]
    count = reach // 8
    chosen = jnp.zeros((64, reach), f32)
    for face in range(4):
        remote = codes_ref[face : face + 1, 0:reach] >= slot_faces
        chosen = jnp.where(remote, traces[64 * face : 64 * face + 64, :], chosen)
    homes = [up_ref.at[0], up_ref.at[1], up_ref.at[2], left_ref, right_ref]
    homes += [down_ref.at[0], down_ref.at[1], down_ref.at[2]]
    for heading, home in enumerate(homes):
        part = chosen[:, count * heading : count * heading + count]
        home[:, 0:96] = part[0:48]
        for third in range(3):
            home[16 * third : 16 * third + 16, 96:128] = part[48:64, 32 * third : 32 * third + 32]
    tiles = codes_ref.shape[1] // LANES
    codes = codes_ref[...]
    codes = jnp.where((codes >= 0) & (codes < slot_faces), codes, 0)
    for face in range(4):
        for tile in range(tiles):
            row = 4 * FACE_TILES * (tile // FACE_TILES) + FACE_TILES * face + tile % FACE_TILES
            faces_ref[row : row + 1, :] = codes[
                face : face + 1, LANES * tile : LANES * tile + LANES
            ]


def relay_kernel(left_ref, right_ref, below_ref, above_ref, to_left_ref, to_right_ref):
    to_left_ref[0] = left_ref[...]
    to_left_ref[1] = below_ref[0]
    to_left_ref[2] = above_ref[0]
    to_right_ref[0] = right_ref[...]
    to_right_ref[1] = below_ref[2]
    to_right_ref[2] = above_ref[2]


def build_rows(first, part, fields_ref, select_ref, table_ref, stacked):
    slot_count = table_ref.shape[0] // 4
    width = LANES * stacked.shape[0]
    high, low = stack_nodes(fields_ref.at[:, :, width * part : width * part + width], stacked)
    both = jnp.concatenate([high, low], axis=0)
    for half in range(2):
        select = select_ref[:, 256 * half : 256 * half + 256]
        rows = product(both, select, ((0,), (0,)))
        for side in range(2):
            start = pl.multiple_of((2 * half + side) * slot_count + first + width * part, width)
            table_ref[pl.ds(start, width), :] = rows[:, LANES * side : LANES * side + LANES]


def gather_pieces(faces_ref, table_ref, normals_ref, outer_ref, rows_refs):
    width = outer_ref.shape[1]
    left_half = lax.broadcasted_iota(jnp.int32, (1, LANES), 1) < 64

    def load(tile, rows):
        for row in rows:
            at = tile * LANES + row
            for half in range(2):
                one = table_ref[pl.ds(faces_ref[2 * half * width + at], 1), :]
                two = table_ref[pl.ds(faces_ref[(2 * half + 1) * width + at], 1), :]
                rows_ref = rows_refs[2 * (tile % 2) + half]
                rows_ref[row : row + 1, :] = jnp.where(left_half, one, two)

    def combine(tile, half):
        turned = rows_refs[2 * (tile % 2) + half][...].T
        lanes = slice(tile * LANES, tile * LANES + LANES)
        for side in range(2):
            face = 2 * half + side
            part = turned[64 * side : 64 * side + 64, :]
            total = -part[0:16]
            for axis_id in range(3):
                facing = normals_ref[axis_id, face : face + 1, lanes]
                total = total + facing * part[16 + 16 * axis_id : 32 + 16 * axis_id]
            outer_ref[FACE_ROWS * face : FACE_ROWS * face + FACE_ROWS, lanes] = total

    for tile in range(width // LANES):
        for part in range(8):
            rows = range(16 * part, 16 * part + 16)
            yield functools.partial(load, tile, rows)
            if tile > 0 and part < 2:
                yield functools.partial(combine, tile - 1, part)
    for half in range(2):
        yield functools.partial(combine, tile, half)


def section_kernel(
    slot_count,
    reach,
    live_ref,
    faces_hbm,
    next_normals_ref,
    bulk_ref,
    fields_ref,
    residue_ref,
    geometry_ref,
    normals_ref,
    scale_ref,
    codes_ref,
    elems_ref,
    table_select_ref,
    select_ref,
    from_ref,
    lift_ref,
    fields_out,
    residue_out,
    sampled,
    table_ref,
    stacked,
    combined,
    slow,
    rates,
    outer,
    beyond_ref,
    pressure,
    fields_split,
    slow_split,
    inner,
    sources,
    even_faces,
    odd_faces,
    arrived,
    *rows_refs,
):
    faces_refs = (even_faces, odd_faces)
    width = fields_ref.shape[2]
    tiles = slot_count // width
    bulks = slot_count // bulk_ref.shape[2]
    step = pl.program_id(0) - bulks
    slot_faces = 4 * slot_count
    half_width = 256

    def codes_copy(tile, parity):
        source = faces_hbm.at[pl.ds(pl.multiple_of(tile * 4 * width, 4 * width), 4 * width)]
        return pltpu.make_async_copy(source, faces_refs[parity], arrived.at[parity])

    def gather(parity):
        return gather_pieces(
            faces_refs[parity], table_ref, next_normals_ref, outer, rows_refs
        )

    def take_codes(parity):
        codes_copy(step, parity).wait()

        @pl.when((step + 1) * width < live_ref[0])
        def _():
            codes_copy(step + 1, 1 - parity).start()

    def update_pieces():
        first = (step - 1) * width

        def stack(at, low, high):
            for tile in range(2 * at, 2 * at + 2):
                for node in range(low, high):
                    stacked[tile, 4 * node : 4 * node + 4, :] = fields_ref[
                        node, :, LANES * tile : LANES * tile + LANES
                    ]

        def split(at):
            for side in range(2):
                lanes = slice(LANES * side, LANES * side + LANES)
                high, low = halves(stacked[2 * at + side])
                fields_split[at, 0:ROWS, lanes] = high
                fields_split[at, ROWS : 2 * ROWS, lanes] = low

        def inside(at):
            return slice(half_width * at, half_width * at + half_width)

        def field_rows(at, field):
            rows = pl.ds(field, NODES, stride=4)
            return jnp.concatenate([stacked[tile, rows, :] for tile in (2 * at, 2 * at + 1)], axis=1)

        def copy_slow(at):
            lanes = inside(at)
            slow[0:NODES, lanes] = field_rows(at, 0)
            slow_split[at, 0:48, :], slow_split[at, 48:96, :] = halves(slow[:, lanes])

        def weigh(at, axis_id):
            lanes = inside(at)
            weighted = jnp.zeros((NODES, half_width), f32)
            for direction in range(3):
                row = 3 * axis_id + direction
                factor = geometry_ref[row : row + 1, lanes] * (1.0 / 3.0)
                weighted = weighted + factor * field_rows(at, 1 + direction)
            combined[PAD * axis_id : PAD * axis_id + NODES, lanes] = weighted

        def split_weighted(at):
            high, low = halves(combined[:, inside(at)])
            sources[at, 768:896, :], sources[at, 896:1024, :] = high, low

        def traces(at):
            inner[at] = product(select_ref[...], fields_split[at])

        def slope(at, axis_id):
            lanes = inside(at)
            place = lax.broadcasted_iota(jnp.int32, (8, half_width), 0) & 3
            value = product(from_ref[ROWS * axis_id : ROWS * axis_id + ROWS, :], slow_split[at])
            pattern = jnp.zeros((8, half_width), f32)
            for direction in range(3):
                row = 3 * axis_id + direction
                factor = geometry_ref[row : row + 1, lanes] * (1.0 / 3.0)
                pattern = jnp.where(place == direction + 1, factor, pattern)
            value = value.reshape(ROWS // 8, 8, half_width) * pattern[None]
            value = value.reshape(ROWS, half_width)
            if axis_id == 0:
                rates[:, lanes] = value
            else:
                rates[:, lanes] += value

        def keep_split(at, start, value):
            high, low = halves(value)
            rows = value.shape[0]
            sources[at, start : start + rows, :] = high
            sources[at, 256 + start : 256 + start + rows, :] = high
            sources[at, 512 + start : 512 + start + rows, :] = low

        def jump(at, face):
            lanes = inside(at)
            inner_p = inner[at, 64 * face : 64 * face + 16, :]
            along = jnp.zeros_like(inner_p)
            for axis_id in range(3):
                facing = normals_ref[axis_id, face : face + 1, lanes]
                start = 64 * face + 16 + 16 * axis_id
                along = along + facing * inner[at, start : start + 16, :]
            wall = codes_ref[face : face + 1, lanes] < 0
            beyond = beyond_ref[FACE_ROWS * face : FACE_ROWS * face + FACE_ROWS, lanes]
            beyond = jnp.where(wall, -along - inner_p, beyond)
            beyond = jnp.where(codes_ref[face : face + 1, lanes] >= slot_faces, 0.0, beyond)
            scale = 0.5 * scale_ref[face : face + 1, lanes]
            value = scale * (along - inner_p - beyond)
            keep_split(at, FACE_ROWS * face, value)
            for axis_id in range(3):
                start = 64 + 64 * axis_id + FACE_ROWS * face
                keep_split(at, start, normals_ref[axis_id, face : face + 1, lanes] * value)

        def lift(at):
            lanes = inside(at)
            rates[:, lanes] = product(lift_ref[...], sources[at]) - rates[:, lanes]

        def advance(at, low, high):
            lanes = inside(at)
            slots = lax.broadcasted_iota(jnp.int32, (1, half_width), 1) + (first + half_width * at)
            keep = slots < live_ref[0]
            for node in range(low, high):
                rate = rates[4 * node : 4 * node + 4, lanes]
                residue_next = section_decay * residue_ref[node, :, lanes] + time_step * rate
                fields_next = fields_ref[node, :, lanes] + section_gain * residue_next
                fields_next = jnp.where(keep, fields_next, 0.0)
                fields_out[node, :, lanes] = fields_next
                residue_out[node, :, lanes] = jnp.where(keep, residue_next, 0.0)
                pressure[node : node + 1, lanes] = fields_next[0:1]

        def sample(at):
            lanes = inside(at)
            parts = jnp.concatenate(thirds(pressure[:, lanes]), axis=0)
            start = first + half_width * at
            slots = lax.broadcasted_iota(jnp.int32, (half_width, elems_ref.shape[1]), 0) + start
            elems = elems_ref[...]
            picks = (slots == elems) & (elems >= reach)
            sampled[...] += product(parts, jnp.where(picks, 1.0, 0.0).astype(bf16))

        call = functools.partial

        def stages(at):
            sevens = range(0, NODES, 7)
            return [
                [call(stack, at, low, low + 7) for low in sevens] + [call(split, at)],
                [call(copy_slow, at)]
                + [call(weigh, at, axis_id) for axis_id in range(3)]
                + [call(split_weighted, at), call(traces, at)],
                [call(slope, at, axis_id) for axis_id in range(3)],
                [call(jump, at, face) for face in range(4)],
                [call(lift, at)],
                [call(advance, at, low, low + 7) for low in sevens],
                [call(sample, at)],
            ]

        both = [stages(at) for at in range(width // half_width)]
        depth = len(both[0])
        return [
            [piece for lag, chain in enumerate(both) if 0 <= at - lag < depth for piece in chain[at - lag]]
            for at in range(depth + len(both) - 1)
        ]

    def interleave(gathers, groups):
        gathers = list(gathers)

        def run(at, updates, groups):
            @pl.when(live_ref[0] > at)
            def _():
                low = at * len(gathers) // len(groups)
                loads = gathers[low : (at + 1) * len(gathers) // len(groups)]
                order = [(place / len(loads), 0, place) for place in range(len(loads))]
                order += [((place + 1) / len(updates), 1, place) for place in range(len(updates))]
                for _, kind, place in sorted(order):
                    (loads, updates)[kind][place]()

        cuts = (0, 4, 8)
        groups = [sum(groups[low:high], []) for low, high in zip(cuts, cuts[1:])]
        for at, updates in enumerate(groups):
            run(at, updates, groups)

    @pl.when(step == -bulks)
    def _():
        stacked[...] = jnp.zeros_like(stacked)
        combined[...] = jnp.zeros_like(combined)
        slow[...] = jnp.zeros_like(slow)
        pressure[...] = jnp.zeros_like(pressure)
        sampled[...] = jnp.zeros_like(sampled)

    @pl.when(step < 0)
    def _():
        first = (step + bulks) * bulk_ref.shape[2]
        for part in range(bulk_ref.shape[2] // width):

            @pl.when(first + width * part < live_ref[0])
            def _():
                build_rows(first, part, bulk_ref, table_select_ref, table_ref, stacked)

    @pl.when(step == -1)
    def _():
        codes_copy(0, 0).start()

    @pl.when(step == 0)
    def _():
        take_codes(0)
        for piece in gather(0):
            piece()

    for parity in range(2):

        @pl.when((step > 0) & (step * width < live_ref[0]) & (step % 2 == parity))
        def _():
            take_codes(parity)
            beyond_ref[...] = outer[...]
            interleave(gather(parity), update_pieces())

    @pl.when((step > 0) & ((step - 1) * width >= live_ref[0]))
    def _():
        fields_out[...] = jnp.zeros_like(fields_out)
        residue_out[...] = jnp.zeros_like(residue_out)

    @pl.when((step > 0) & ((step - 1) * width < live_ref[0]) & (step * width >= live_ref[0]))
    def _():
        beyond_ref[...] = outer[...]
        for stage in update_pieces():
            for piece in stage:
                piece()


def boundary_kernel(
    slot_faces,
    powers,
    group,
    fields_ref,
    residue_ref,
    normals_ref,
    scale_ref,
    codes_ref,
    right_ref,
    left_ref,
    below_ref,
    above_ref,
    elems_ref,
    ids_ref,
    coords_ref,
    partial_ref,
    lift_ref,
    inverse_ref,
    fields_out,
    residue_out,
    spread_ref,
    remote,
    sources,
    rates,
    pressure,
    monomials,
):
    reach = fields_ref.shape[2]
    bound_count = reach // 8
    pressure[...] = jnp.zeros_like(pressure)
    monomials[...] = jnp.zeros_like(monomials)
    arrivals = [
        left_ref[2],
        above_ref[1],
        right_ref[2],
        left_ref[0],
        right_ref[0],
        left_ref[1],
        below_ref[1],
        right_ref[1],
    ]
    for heading, source in enumerate(arrivals):
        start = bound_count * heading
        remote[0:48, start : start + 96] = source[:, 0:96]
        for third in range(3):
            place = start + 32 * third
            remote[48:64, place : place + 32] = source[16 * third : 16 * third + 16, 96:128]

    def keep_split(start, value):
        high, low = halves(value)
        sources[start : start + FACE_ROWS, :] = high
        sources[256 + start : 256 + start + FACE_ROWS, :] = high
        sources[512 + start : 512 + start + FACE_ROWS, :] = low

    for face in range(4):
        beyond = -remote[0:16, :]
        for axis_id in range(3):
            facing = normals_ref[axis_id, face : face + 1, :]
            beyond = beyond + facing * remote[16 + 16 * axis_id : 32 + 16 * axis_id, :]
        is_remote = codes_ref[face : face + 1, :] >= slot_faces
        flux = jnp.where(is_remote, -0.5 * scale_ref[face : face + 1, :] * beyond, 0.0)
        keep_split(FACE_ROWS * face, flux)
        for axis_id in range(3):
            facing = normals_ref[axis_id, face : face + 1, :]
            keep_split(64 + 64 * axis_id + FACE_ROWS * face, facing * flux)
    rates[...] = time_step * product(lift_ref[:, 0:768], sources[...])
    for node in range(NODES):
        rate = rates[4 * node : 4 * node + 4, :]
        residue_out[node] = residue_ref[node] + rate
        fields_next = fields_ref[node] + section_gain * rate
        fields_out[node] = fields_next
        pressure[node : node + 1, :] = fields_next[0:1]
    parts = jnp.concatenate(thirds(pressure[...]), axis=0)
    slots = lax.broadcasted_iota(jnp.int32, (reach, elems_ref.shape[1]), 0)
    picks = jnp.where(slots == elems_ref[...], 1.0, 0.0).astype(bf16)
    sampled = partial_ref[...] + product(parts, picks)
    ladders = []
    for axis_id in range(3):
        base = coords_ref[axis_id : axis_id + 1, :]
        square = base * base
        ladders.append([jnp.ones_like(base), base, square, square * base, square * square])
    for node in range(NODES):
        exps = [int(entry) for entry in powers[node]]
        monomials[node : node + 1, :] = (
            ladders[0][exps[0]] * ladders[1][exps[1]] * ladders[2][exps[2]]
        )
    basis = jnp.dot(
        inverse_ref[...], monomials[...], precision=highest, preferred_element_type=f32
    )
    gathered = sampled[0:PAD, :] + sampled[48 : 48 + PAD, :] + sampled[96 : 96 + PAD, :]
    values = jnp.sum(basis * gathered, axis=0, keepdims=True)
    ids = ids_ref[...]
    owner = lax.shift_right_logical(ids * 5243, 20)
    place = ids - group * owner
    owners = lax.broadcasted_iota(jnp.int32, (spread_ref.shape[0], ids.shape[1]), 0)
    held = jnp.where(owners == owner, values, 0.0)
    places = lax.broadcasted_iota(jnp.int32, (spread_ref.shape[2], ids.shape[1]), 0)
    chosen = jnp.where(places == place, 1.0, 0.0).astype(bf16)
    spread = jnp.zeros((spread_ref.shape[0], spread_ref.shape[2]), f32)
    for part in thirds(held):
        spread = spread + product(part, chosen, ((1,), (1,)))
    spread_ref[:, 0, :] = spread


def harmonic_kernel(received_ref, table_ref, groups_ref, out_ref):
    mine = jnp.sum(received_ref[...], axis=0)
    weighted = groups_ref[...] * mine
    out_ref[...] = lax.dot_general(
        weighted,
        table_ref[...],
        (((1,), (1,)), ((), ())),
        precision=highest,
        preferred_element_type=f32,
    )


def in_hbm(array):
    return pltpu.with_memory_space_constraint(array, pltpu.HBM)


def in_vmem(array):
    return pltpu.with_memory_space_constraint(array, pltpu.VMEM)


def fixed(shape):
    return pl.BlockSpec(shape, lambda *_: (0,) * len(shape))


def local(
    fields,
    residue,
    geometry,
    normals,
    face_scale,
    neighbours,
    send_faces,
    live_counts,
    sample_ids,
    sample_elems,
    sample_coords,
):
    const = {
        name: in_hbm(table) if isinstance(table, jax.Array) else table
        for name, table in constant_tables().items()
    }
    fields = in_hbm(jnp.transpose(fields, (1, 0, 2)))
    residue = in_hbm(jnp.transpose(residue, (1, 0, 2)))
    geometry, normals, face_scale = in_hbm(geometry), in_hbm(normals), in_hbm(face_scale)
    neighbours, sample_coords = in_hbm(neighbours), in_hbm(sample_coords)
    slot_count = fields.shape[2]
    slot_faces = 4 * slot_count
    bound_count = send_faces.shape[1]
    reach = 8 * bound_count
    samples = sample_ids.shape[0]
    devices = lax.axis_size(("px", "py"))
    shape = jax.ShapeDtypeStruct

    elems = in_hbm(sample_elems.reshape(1, samples))
    width = LANES * FACE_TILES
    tiles = slot_count // width
    piece = (3, 48, LANES)

    up, down, left, right, faces = pl.pallas_call(
        functools.partial(pack_kernel, slot_faces),
        grid=(1,),
        in_specs=[
            pl.BlockSpec((NODES, 4, reach), lambda t: (0, 0, 0)),
            fixed((4, slot_count)),
            fixed((256, ROWS)),
        ],
        out_specs=[
            fixed(piece),
            fixed(piece),
            fixed(piece[1:]),
            fixed(piece[1:]),
            fixed((slot_faces // LANES, LANES)),
        ],
        out_shape=[
            pltpu.HBM(piece, f32),
            pltpu.HBM(piece, f32),
            pltpu.HBM(piece[1:], f32),
            pltpu.HBM(piece[1:], f32),
            pltpu.HBM((slot_faces // LANES, LANES), jnp.int32),
        ],
        scratch_shapes=[pltpu.VMEM((reach // LANES, ROWS, LANES), f32)],
        compiler_params=pltpu.CompilerParams(vmem_limit_bytes=16 << 20),
        name="pack",
    )(fields, neighbours, const["trace_select"])

    def steps_along(axis):
        count = lax.axis_size(axis)
        forward = [(i, i + 1) for i in range(count - 1)]
        return forward, [(target, source) for source, target in forward]

    forward, backward = steps_along("px")
    below = lax.ppermute(up, "px", backward)
    above = lax.ppermute(down, "px", forward)
    bulk = 3 * width
    bulks = slot_count // bulk

    def behind(rank):
        return lambda t, *_: (0,) * rank + (jnp.maximum(t - bulks - 1, 0),)

    def ahead(rank):
        return lambda t, *_: (0,) * rank + (jnp.clip(t - bulks, 0, tiles - 1),)

    fields_next, residue_next, partial = pl.pallas_call(
        functools.partial(section_kernel, slot_count, reach),
        grid_spec=pltpu.PrefetchScalarGridSpec(
            num_scalar_prefetch=1,
            grid=(bulks + tiles + 1,),
            in_specs=[
                pl.BlockSpec(memory_space=pltpu.HBM),
                pl.BlockSpec((3, 4, width), ahead(2)),
                pl.BlockSpec((NODES, 4, bulk), lambda t, *_: (0, 0, jnp.minimum(t, bulks - 1))),
                pl.BlockSpec((NODES, 4, width), behind(2)),
                pl.BlockSpec((NODES, 4, width), behind(2)),
                pl.BlockSpec((9, width), behind(1)),
                pl.BlockSpec((3, 4, width), behind(2)),
                pl.BlockSpec((4, width), behind(1)),
                pl.BlockSpec((4, width), behind(1)),
                fixed((1, samples)),
                fixed((2 * ROWS, 4 * LANES)),
                fixed((256, 2 * ROWS)),
                fixed((3 * ROWS, 96)),
                fixed((ROWS, 1024)),
            ],
            out_specs=[
                pl.BlockSpec((NODES, 4, width), behind(2)),
                pl.BlockSpec((NODES, 4, width), behind(2)),
                fixed((144, samples)),
            ],
            scratch_shapes=[
                pltpu.VMEM((slot_faces, LANES), f32),
                pltpu.VMEM((width // LANES, ROWS, LANES), f32),
                pltpu.VMEM((128, width), f32),
                pltpu.VMEM((48, width), f32),
                pltpu.VMEM((ROWS, width), f32),
                pltpu.VMEM((64, width), f32),
                pltpu.VMEM((64, width), f32),
                pltpu.VMEM((48, width), f32),
                pltpu.VMEM((width // 256, 2 * ROWS, 256), bf16),
                pltpu.VMEM((width // 256, 96, 256), bf16),
                pltpu.VMEM((width // 256, 256, 256), f32),
                pltpu.VMEM((width // 256, 1024, 256), bf16),
                pltpu.SMEM((4 * width,), jnp.int32),
                pltpu.SMEM((4 * width,), jnp.int32),
                pltpu.SemaphoreType.DMA((2,)),
                *[pltpu.VMEM((LANES, LANES), f32)] * 4,
            ],
        ),
        out_shape=[
            shape(fields.shape, f32),
            shape(residue.shape, f32),
            shape((144, samples), f32),
        ],
        compiler_params=pltpu.CompilerParams(vmem_limit_bytes=48 << 20),
        name="section",
    )(
        live_counts,
        in_hbm(faces.reshape(-1)),
        normals,
        fields,
        fields,
        residue,
        geometry,
        normals,
        face_scale,
        neighbours,
        elems,
        const["table_select"],
        const["twice_select"],
        const["from_p"],
        const["lift"],
    )

    below, above, partial = lax.optimization_barrier((below, above, partial))
    to_left, to_right = pl.pallas_call(
        relay_kernel,
        out_shape=[pltpu.HBM(piece, f32), pltpu.HBM(piece, f32)],
        name="relay",
    )(left, right, in_vmem(below), in_vmem(above))
    forward, backward = steps_along("py")
    from_right = lax.ppermute(to_left, "py", backward)
    from_left = lax.ppermute(to_right, "py", forward)

    def head(rank):
        return lambda t: (0,) * rank

    fields_next, residue_next, spread = pl.pallas_call(
        functools.partial(boundary_kernel, slot_faces, const["powers"], samples),
        grid=(1,),
        in_specs=[
            pl.BlockSpec((NODES, 4, reach), head(3)),
            pl.BlockSpec((NODES, 4, reach), head(3)),
            pl.BlockSpec((3, 4, reach), head(3)),
            pl.BlockSpec((4, reach), head(2)),
            pl.BlockSpec((4, reach), head(2)),
            fixed(piece),
            fixed(piece),
            fixed(piece),
            fixed(piece),
            fixed((1, samples)),
            fixed((1, samples)),
            fixed((3, samples)),
            fixed((144, samples)),
            fixed((ROWS, 1024)),
            fixed((PAD, PAD)),
        ],
        out_specs=[
            pl.BlockSpec((NODES, 4, reach), head(3)),
            pl.BlockSpec((NODES, 4, reach), head(3)),
            fixed((devices, 1, samples)),
        ],
        out_shape=[
            shape(fields.shape, f32),
            shape(residue.shape, f32),
            shape((devices, 1, samples), f32),
        ],
        scratch_shapes=[
            pltpu.VMEM((64, reach), f32),
            pltpu.VMEM((768, reach), bf16),
            pltpu.VMEM((ROWS, reach), f32),
            pltpu.VMEM((48, reach), f32),
            pltpu.VMEM((PAD, samples), f32),
        ],
        input_output_aliases={0: 0, 1: 1},
        compiler_params=pltpu.CompilerParams(vmem_limit_bytes=24 << 20),
        name="boundary",
    )(
        in_hbm(fields_next),
        in_hbm(residue_next),
        normals,
        face_scale,
        neighbours,
        from_right,
        from_left,
        below,
        above,
        elems,
        in_hbm(sample_ids.reshape(1, samples)),
        sample_coords,
        partial,
        const["lift"],
        const["inverse"],
    )
    received = lax.all_to_all(spread, ("px", "py"), 0, 0, tiled=True)

    receivers = samples // QPTS
    harmonic = np.tile(harmonic_table(), (1, receivers)).astype(np.float32)
    groups = (np.arange(samples)[None] // QPTS == np.arange(receivers)[:, None]).astype(np.float32)
    coefficients = pl.pallas_call(
        harmonic_kernel,
        out_shape=shape((receivers, harmonic.shape[0]), f32),
        name="harmonic",
    )(received, jnp.asarray(harmonic), jnp.asarray(groups))
    return (
        jnp.transpose(fields_next, (1, 0, 2)),
        jnp.transpose(residue_next, (1, 0, 2)),
        coefficients.T,
    )


def solution(mesh):
    placed = (
        P(None, None, ("px", "py")),
        P(None, None, ("px", "py")),
        P(None, ("px", "py")),
        P(None, None, ("px", "py")),
        P(None, ("px", "py")),
        P(None, ("px", "py")),
        P(None, ("px", "py")),
        P(("px", "py")),
        P(("px", "py")),
        P(("px", "py")),
        P(None, ("px", "py")),
    )
    return jax.shard_map(
        local,
        mesh=mesh,
        in_specs=placed,
        out_specs=(P(None, None, ("px", "py")), P(None, None, ("px", "py")), P(None, ("px", "py"))),
        check_vma=False,
    )
```

```python
import functools
import math

import jax
import jax.numpy as jnp
import numpy as np
from jax import lax
from jax.experimental import pallas as pl
from jax.experimental.pallas import tpu as pltpu
from jax.sharding import PartitionSpec as P

QPTS = 50
NODES = 35
PAD = 40
FACE_ROWS = 16
ROWS = 144
LANES = 128
FACE_TILES = 4


highest = lax.Precision.HIGHEST
section_decay = -567301805773.0 / 1357537059087.0
section_gain = 5161836677717.0 / 13612068292357.0
time_step = 0.01
f32 = jnp.float32
bf16 = jnp.bfloat16


def exponent_table():
    listing = []
    for degree in range(5):
        for third in range(degree + 1):
            for second in range(degree + 1 - third):
                listing.append((degree - second - third, second, third))
    return np.array(listing)


def factorials(values):
    lookup = np.array([float(math.factorial(level)) for level in range(24)])
    return lookup[values]


def eliminate(matrix, right_hand):
    order_size = matrix.shape[0]
    work = np.concatenate([matrix, right_hand], axis=1).astype(float)
    for pivot_col in range(order_size):
        best = max(range(pivot_col, order_size), key=lambda row_id: abs(work[row_id, pivot_col]))
        work[[pivot_col, best]] = work[[best, pivot_col]]
        work[pivot_col] = work[pivot_col] / work[pivot_col, pivot_col]
        for row_id in range(order_size):
            if row_id != pivot_col:
                work[row_id] = work[row_id] - work[row_id, pivot_col] * work[pivot_col]
    return work[:, order_size:]


def element_tables():
    powers = exponent_table()
    points = powers / 4.0
    vander = np.prod(points[:, None, :] ** powers[None, :, :], axis=2)
    inverse = eliminate(vander, np.eye(35))
    derivs = []
    for axis_id in range(3):
        lowered = np.maximum(powers - (np.arange(3) == axis_id)[None, :], 0)
        slope_table = powers[None, :, axis_id] * np.prod(
            points[:, None, :] ** lowered[None, :, :], axis=2
        )
        derivs.append(slope_table @ inverse)
    summed = powers[:, None, :] + powers[None, :, :]
    exp_r = summed[..., 0]
    exp_s = summed[..., 1]
    exp_t = summed[..., 2]
    volume = (
        factorials(exp_r)
        * factorials(exp_s)
        * factorials(exp_t)
        / factorials(exp_r + exp_s + exp_t + 3)
    )
    mass_matrix = inverse.T @ volume @ inverse
    face_grams = [
        np.where(
            exp_t == 0, factorials(exp_r) * factorials(exp_s) / factorials(exp_r + exp_s + 2), 0.0
        ),
        np.where(
            exp_s == 0, factorials(exp_r) * factorials(exp_t) / factorials(exp_r + exp_t + 2), 0.0
        ),
        factorials(exp_r)
        * factorials(exp_s)
        * factorials(exp_t)
        / factorials(exp_r + exp_s + exp_t + 2),
        np.where(
            exp_r == 0, factorials(exp_s) * factorials(exp_t) / factorials(exp_s + exp_t + 2), 0.0
        ),
    ]
    listed = [tuple((int(entry) for entry in powers[node_id])) for node_id in range(35)]
    face_nodes = np.array(
        [
            [node_id for node_id in range(35) if listed[node_id][2] == 0],
            [node_id for node_id in range(35) if listed[node_id][1] == 0],
            [node_id for node_id in range(35) if sum(listed[node_id]) == 4],
            [node_id for node_id in range(35) if listed[node_id][0] == 0],
        ]
    )
    surface = np.zeros((35, 60))
    for face_id in range(4):
        face_mass = inverse.T @ face_grams[face_id] @ inverse
        for node_id in range(15):
            surface[:, 4 * node_id + face_id] = face_mass[:, face_nodes[face_id, node_id]]
    lifting = eliminate(mass_matrix, surface)
    return (np.stack(derivs), lifting, face_nodes, inverse, powers)


def associated(degree, order, cosine, sine):
    current = cosine * 0.0 + 1.0
    for step_id in range(1, order + 1):
        current = -(2 * step_id - 1) * sine * current
    if degree == order:
        return current
    following = cosine * (2 * order + 1) * current
    for level in range(order + 2, degree + 1):
        current, following = (
            following,
            ((2 * level - 1) * cosine * following - (level + order - 1) * current)
            / (level - order),
        )
    return following


def harmonic_table():
    inner_node = math.sqrt(5.0 - 2.0 * math.sqrt(10.0 / 7.0)) / 3.0
    outer_node = math.sqrt(5.0 + 2.0 * math.sqrt(10.0 / 7.0)) / 3.0
    inner_weight = (322.0 + 13.0 * math.sqrt(70.0)) / 900.0
    outer_weight = (322.0 - 13.0 * math.sqrt(70.0)) / 900.0
    cosines = np.array([-outer_node, -inner_node, 0.0, inner_node, outer_node])
    weights = np.array([outer_weight, inner_weight, 128.0 / 225.0, inner_weight, outer_weight])
    azimuth = 2.0 * np.pi * (np.arange(10) + 0.5) / 10.0
    polar = np.repeat(cosines, 10)
    circle = np.tile(azimuth, 5)
    point_weight = np.repeat(weights, 10) * 2.0 * np.pi / 10.0
    sine = np.sqrt(1.0 - polar**2)
    table_rows = []
    for degree in range(5):
        for order in range(-degree, degree + 1):
            absolute = abs(order)
            legendre = associated(degree, absolute, polar, sine)
            factor = math.sqrt(
                (2 * degree + 1)
                / (4.0 * math.pi)
                * math.factorial(degree - absolute)
                / math.factorial(degree + absolute)
            )
            if order > 0:
                angular = math.sqrt(2.0) * np.cos(order * circle)
            elif order < 0:
                angular = math.sqrt(2.0) * np.sin(absolute * circle)
            else:
                angular = circle * 0.0 + 1.0
            table_rows.append(factor * legendre * angular * point_weight)
    return np.array(table_rows)


def constant_tables():
    derivs, lifting, face_nodes, inverse, powers = element_tables()
    table_select = np.zeros((ROWS, 4 * LANES), np.float32)
    trace_select = np.zeros((4 * 4 * FACE_ROWS, ROWS), np.float32)
    for face in range(4):
        for field in range(4):
            for place in range(15):
                source = 4 * face_nodes[face, place] + field
                column = FACE_ROWS * field + place
                table_select[source, LANES * face + column] = 1.0
                table_select[source, LANES * face + 64 + column] = 1.0
                trace_select[64 * face + column, source] = 1.0
    whole = np.round(3.0 * derivs)
    into_p = np.zeros((ROWS, 128), np.float32)
    from_p = np.zeros((3 * ROWS, 48), np.float32)
    lift = np.zeros((ROWS, 256), np.float32)
    for node in range(NODES):
        for axis_id in range(3):
            into_p[4 * node, PAD * axis_id : PAD * axis_id + NODES] = -whole[axis_id, node]
            for field in range(1, 4):
                from_p[ROWS * axis_id + 4 * node + field, :NODES] = whole[axis_id, node]
        for face in range(4):
            for place in range(15):
                entry = lifting[node, 4 * place + face]
                column = FACE_ROWS * face + place
                lift[4 * node, column] = entry
                for field in range(1, 4):
                    lift[4 * node + field, 64 * field + column] = -entry
    lift_hi = lift.astype(jnp.bfloat16)
    lift_lo = (lift - lift_hi.astype(np.float32)).astype(jnp.bfloat16)
    return {
        "table_select": jnp.asarray(np.concatenate([table_select] * 2, axis=0), bf16),
        "trace_select": jnp.asarray(trace_select, bf16),
        "twice_select": jnp.asarray(np.concatenate([trace_select] * 2, axis=1), bf16),
        "from_p": jnp.asarray(np.concatenate([from_p, from_p], axis=1), bf16),
        "lift": jnp.asarray(
            np.concatenate(
                [lift_hi, lift_lo, lift_hi] + [into_p.astype(jnp.bfloat16)] * 2, axis=1
            )
        ),
        "inverse": jnp.asarray(np.pad(inverse.T, ((0, 5), (0, 5))), f32),
        "powers": powers,
    }


def halves(values):
    high = values.astype(bf16)
    return high, (values - high.astype(f32)).astype(bf16)


def thirds(values):
    high = values.astype(bf16)
    rest = values - high.astype(f32)
    middle = rest.astype(bf16)
    return high, middle, (rest - middle.astype(f32)).astype(bf16)


def product(left, right, dims=((1,), (0,))):
    return lax.dot_general(left, right, (dims, ((), ())), preferred_element_type=f32)


def stack_nodes(fields_ref, stacked):
    tiles = range(stacked.shape[0])
    for tile in tiles:
        for node in range(NODES):
            stacked[tile, 4 * node : 4 * node + 4, :] = fields_ref[
                node, :, LANES * tile : LANES * tile + LANES
            ]
    return halves(jnp.concatenate([stacked[tile] for tile in tiles], axis=1))


def one_field(stacked, field):
    tiles = range(stacked.shape[0])
    rows = pl.ds(field, NODES, stride=4)
    return jnp.concatenate([stacked[tile, rows, :] for tile in tiles], axis=1)


def pack_kernel(
    slot_faces,
    fields_ref,
    codes_ref,
    select_ref,
    up_ref,
    down_ref,
    left_ref,
    right_ref,
    faces_ref,
    stacked,
):
    stacked[...] = jnp.zeros_like(stacked)
    high, low = stack_nodes(fields_ref, stacked)
    traces = product(select_ref[...], high) + product(select_ref[...], low)
    reach = fields_ref.shape[2]
    count = reach // 8
    chosen = jnp.zeros((64, reach), f32)
    for face in range(4):
        remote = codes_ref[face : face + 1, 0:reach] >= slot_faces
        chosen = jnp.where(remote, traces[64 * face : 64 * face + 64, :], chosen)
    homes = [up_ref.at[0], up_ref.at[1], up_ref.at[2], left_ref, right_ref]
    homes += [down_ref.at[0], down_ref.at[1], down_ref.at[2]]
    for heading, home in enumerate(homes):
        part = chosen[:, count * heading : count * heading + count]
        home[:, 0:96] = part[0:48]
        for third in range(3):
            home[16 * third : 16 * third + 16, 96:128] = part[48:64, 32 * third : 32 * third + 32]
    tiles = codes_ref.shape[1] // LANES
    codes = codes_ref[...]
    codes = jnp.where((codes >= 0) & (codes < slot_faces), codes, 0)
    for face in range(4):
        for tile in range(tiles):
            row = 4 * FACE_TILES * (tile // FACE_TILES) + FACE_TILES * face + tile % FACE_TILES
            faces_ref[row : row + 1, :] = codes[
                face : face + 1, LANES * tile : LANES * tile + LANES
            ]


def relay_kernel(left_ref, right_ref, below_ref, above_ref, to_left_ref, to_right_ref):
    to_left_ref[0] = left_ref[...]
    to_left_ref[1] = below_ref[0]
    to_left_ref[2] = above_ref[0]
    to_right_ref[0] = right_ref[...]
    to_right_ref[1] = below_ref[2]
    to_right_ref[2] = above_ref[2]


def build_rows(first, part, fields_ref, select_ref, table_ref, stacked):
    slot_count = table_ref.shape[0] // 4
    width = LANES * stacked.shape[0]
    high, low = stack_nodes(fields_ref.at[:, :, width * part : width * part + width], stacked)
    both = jnp.concatenate([high, low], axis=0)
    for half in range(2):
        select = select_ref[:, 256 * half : 256 * half + 256]
        rows = product(both, select, ((0,), (0,)))
        for side in range(2):
            start = pl.multiple_of((2 * half + side) * slot_count + first + width * part, width)
            table_ref[pl.ds(start, width), :] = rows[:, LANES * side : LANES * side + LANES]


def gather_pieces(faces_ref, table_ref, normals_ref, outer_ref, rows_refs):
    width = outer_ref.shape[1]
    left_half = lax.broadcasted_iota(jnp.int32, (1, LANES), 1) < 64

    def load(tile, rows):
        for row in rows:
            at = tile * LANES + row
            for half in range(2):
                one = table_ref[pl.ds(faces_ref[2 * half * width + at], 1), :]
                two = table_ref[pl.ds(faces_ref[(2 * half + 1) * width + at], 1), :]
                rows_ref = rows_refs[2 * (tile % 2) + half]
                rows_ref[row : row + 1, :] = jnp.where(left_half, one, two)

    def combine(tile, half):
        turned = rows_refs[2 * (tile % 2) + half][...].T
        lanes = slice(tile * LANES, tile * LANES + LANES)
        for side in range(2):
            face = 2 * half + side
            part = turned[64 * side : 64 * side + 64, :]
            total = -part[0:16]
            for axis_id in range(3):
                facing = normals_ref[axis_id, face : face + 1, lanes]
                total = total + facing * part[16 + 16 * axis_id : 32 + 16 * axis_id]
            outer_ref[FACE_ROWS * face : FACE_ROWS * face + FACE_ROWS, lanes] = total

    for tile in range(width // LANES):
        for part in range(8):
            rows = range(16 * part, 16 * part + 16)
            yield functools.partial(load, tile, rows)
            if tile > 0 and part < 2:
                yield functools.partial(combine, tile - 1, part)
    for half in range(2):
        yield functools.partial(combine, tile, half)


def section_kernel(
    slot_count,
    reach,
    live_ref,
    faces_hbm,
    next_normals_ref,
    bulk_ref,
    fields_ref,
    residue_ref,
    geometry_ref,
    normals_ref,
    scale_ref,
    codes_ref,
    elems_ref,
    table_select_ref,
    select_ref,
    from_ref,
    lift_ref,
    fields_out,
    residue_out,
    sampled,
    table_ref,
    stacked,
    combined,
    slow,
    rates,
    outer,
    beyond_ref,
    pressure,
    fields_split,
    slow_split,
    inner,
    sources,
    even_faces,
    odd_faces,
    arrived,
    *rows_refs,
):
    faces_refs = (even_faces, odd_faces)
    width = fields_ref.shape[2]
    tiles = slot_count // width
    bulks = slot_count // bulk_ref.shape[2]
    step = pl.program_id(0) - bulks
    slot_faces = 4 * slot_count
    half_width = 256

    def codes_copy(tile, parity):
        source = faces_hbm.at[pl.ds(pl.multiple_of(tile * 4 * width, 4 * width), 4 * width)]
        return pltpu.make_async_copy(source, faces_refs[parity], arrived.at[parity])

    def gather(parity):
        return gather_pieces(
            faces_refs[parity], table_ref, next_normals_ref, outer, rows_refs
        )

    def take_codes(parity):
        codes_copy(step, parity).wait()

        @pl.when((step + 1) * width < live_ref[0])
        def _():
            codes_copy(step + 1, 1 - parity).start()

    def update_pieces():
        first = (step - 1) * width

        def stack(at, low, high):
            for tile in range(2 * at, 2 * at + 2):
                for node in range(low, high):
                    stacked[tile, 4 * node : 4 * node + 4, :] = fields_ref[
                        node, :, LANES * tile : LANES * tile + LANES
                    ]

        def split(at):
            for side in range(2):
                lanes = slice(LANES * side, LANES * side + LANES)
                high, low = halves(stacked[2 * at + side])
                fields_split[at, 0:ROWS, lanes] = high
                fields_split[at, ROWS : 2 * ROWS, lanes] = low

        def inside(at):
            return slice(half_width * at, half_width * at + half_width)

        def field_rows(at, field):
            rows = pl.ds(field, NODES, stride=4)
            return jnp.concatenate([stacked[tile, rows, :] for tile in (2 * at, 2 * at + 1)], axis=1)

        def copy_slow(at):
            lanes = inside(at)
            slow[0:NODES, lanes] = field_rows(at, 0)
            slow_split[at, 0:48, :], slow_split[at, 48:96, :] = halves(slow[:, lanes])

        def weigh(at, axis_id):
            lanes = inside(at)
            weighted = jnp.zeros((NODES, half_width), f32)
            for direction in range(3):
                row = 3 * axis_id + direction
                factor = geometry_ref[row : row + 1, lanes] * (1.0 / 3.0)
                weighted = weighted + factor * field_rows(at, 1 + direction)
            combined[PAD * axis_id : PAD * axis_id + NODES, lanes] = weighted

        def split_weighted(at):
            high, low = halves(combined[:, inside(at)])
            sources[at, 768:896, :], sources[at, 896:1024, :] = high, low

        def traces(at):
            inner[at] = product(select_ref[...], fields_split[at])

        def slope(at, axis_id):
            lanes = inside(at)
            place = lax.broadcasted_iota(jnp.int32, (8, half_width), 0) & 3
            value = product(from_ref[ROWS * axis_id : ROWS * axis_id + ROWS, :], slow_split[at])
            pattern = jnp.zeros((8, half_width), f32)
            for direction in range(3):
                row = 3 * axis_id + direction
                factor = geometry_ref[row : row + 1, lanes] * (1.0 / 3.0)
                pattern = jnp.where(place == direction + 1, factor, pattern)
            value = value.reshape(ROWS // 8, 8, half_width) * pattern[None]
            value = value.reshape(ROWS, half_width)
            if axis_id == 0:
                rates[:, lanes] = value
            else:
                rates[:, lanes] += value

        def keep_split(at, start, value):
            high, low = halves(value)
            rows = value.shape[0]
            sources[at, start : start + rows, :] = high
            sources[at, 256 + start : 256 + start + rows, :] = high
            sources[at, 512 + start : 512 + start + rows, :] = low

        def jump(at, face):
            lanes = inside(at)
            inner_p = inner[at, 64 * face : 64 * face + 16, :]
            along = jnp.zeros_like(inner_p)
            for axis_id in range(3):
                facing = normals_ref[axis_id, face : face + 1, lanes]
                start = 64 * face + 16 + 16 * axis_id
                along = along + facing * inner[at, start : start + 16, :]
            wall = codes_ref[face : face + 1, lanes] < 0
            beyond = beyond_ref[FACE_ROWS * face : FACE_ROWS * face + FACE_ROWS, lanes]
            beyond = jnp.where(wall, -along - inner_p, beyond)
            beyond = jnp.where(codes_ref[face : face + 1, lanes] >= slot_faces, 0.0, beyond)
            scale = 0.5 * scale_ref[face : face + 1, lanes]
            value = scale * (along - inner_p - beyond)
            keep_split(at, FACE_ROWS * face, value)
            for axis_id in range(3):
                start = 64 + 64 * axis_id + FACE_ROWS * face
                keep_split(at, start, normals_ref[axis_id, face : face + 1, lanes] * value)

        def lift(at):
            lanes = inside(at)
            rates[:, lanes] = product(lift_ref[...], sources[at]) - rates[:, lanes]

        def advance(at, low, high):
            lanes = inside(at)
            slots = lax.broadcasted_iota(jnp.int32, (1, half_width), 1) + (first + half_width * at)
            keep = slots < live_ref[0]
            for node in range(low, high):
                rate = rates[4 * node : 4 * node + 4, lanes]
                residue_next = section_decay * residue_ref[node, :, lanes] + time_step * rate
                fields_next = fields_ref[node, :, lanes] + section_gain * residue_next
                fields_next = jnp.where(keep, fields_next, 0.0)
                fields_out[node, :, lanes] = fields_next
                residue_out[node, :, lanes] = jnp.where(keep, residue_next, 0.0)
                pressure[node : node + 1, lanes] = fields_next[0:1]

        def sample(at):
            lanes = inside(at)
            parts = jnp.concatenate(thirds(pressure[:, lanes]), axis=0)
            start = first + half_width * at
            slots = lax.broadcasted_iota(jnp.int32, (half_width, elems_ref.shape[1]), 0) + start
            elems = elems_ref[...]
            picks = (slots == elems) & (elems >= reach)
            sampled[...] += product(parts, jnp.where(picks, 1.0, 0.0).astype(bf16))

        call = functools.partial

        def stages(at):
            sevens = range(0, NODES, 7)
            return [
                [call(stack, at, low, low + 7) for low in sevens] + [call(split, at)],
                [call(copy_slow, at)]
                + [call(weigh, at, axis_id) for axis_id in range(3)]
                + [call(split_weighted, at), call(traces, at)],
                [call(slope, at, axis_id) for axis_id in range(3)],
                [call(jump, at, face) for face in range(4)],
                [call(lift, at)],
                [call(advance, at, low, low + 7) for low in sevens],
                [call(sample, at)],
            ]

        both = [stages(at) for at in range(width // half_width)]
        depth = len(both[0])
        return [
            [piece for lag, chain in enumerate(both) if 0 <= at - lag < depth for piece in chain[at - lag]]
            for at in range(depth + len(both) - 1)
        ]

    def interleave(gathers, groups):
        gathers = list(gathers)

        def run(at, updates, groups):
            @pl.when(live_ref[0] > at)
            def _():
                low = at * len(gathers) // len(groups)
                loads = gathers[low : (at + 1) * len(gathers) // len(groups)]
                order = [(place / len(loads), 0, place) for place in range(len(loads))]
                order += [((place + 1) / len(updates), 1, place) for place in range(len(updates))]
                for _, kind, place in sorted(order):
                    (loads, updates)[kind][place]()

        cuts = (0, 4, 8)
        groups = [sum(groups[low:high], []) for low, high in zip(cuts, cuts[1:])]
        for at, updates in enumerate(groups):
            run(at, updates, groups)

    @pl.when(step == -bulks)
    def _():
        stacked[...] = jnp.zeros_like(stacked)
        combined[...] = jnp.zeros_like(combined)
        slow[...] = jnp.zeros_like(slow)
        pressure[...] = jnp.zeros_like(pressure)
        sampled[...] = jnp.zeros_like(sampled)

    @pl.when(step < 0)
    def _():
        first = (step + bulks) * bulk_ref.shape[2]
        for part in range(bulk_ref.shape[2] // width):

            @pl.when(first + width * part < live_ref[0])
            def _():
                build_rows(first, part, bulk_ref, table_select_ref, table_ref, stacked)

    @pl.when(step == -1)
    def _():
        codes_copy(0, 0).start()

    @pl.when(step == 0)
    def _():
        take_codes(0)
        for piece in gather(0):
            piece()

    for parity in range(2):

        @pl.when((step > 0) & (step * width < live_ref[0]) & (step % 2 == parity))
        def _():
            take_codes(parity)
            beyond_ref[...] = outer[...]
            interleave(gather(parity), update_pieces())

    @pl.when((step > 0) & ((step - 1) * width >= live_ref[0]))
    def _():
        fields_out[...] = jnp.zeros_like(fields_out)
        residue_out[...] = jnp.zeros_like(residue_out)

    @pl.when((step > 0) & ((step - 1) * width < live_ref[0]) & (step * width >= live_ref[0]))
    def _():
        beyond_ref[...] = outer[...]
        for stage in update_pieces():
            for piece in stage:
                piece()


def boundary_kernel(
    slot_faces,
    powers,
    group,
    fields_ref,
    residue_ref,
    normals_ref,
    scale_ref,
    codes_ref,
    right_ref,
    left_ref,
    below_ref,
    above_ref,
    elems_ref,
    ids_ref,
    coords_ref,
    partial_ref,
    lift_ref,
    inverse_ref,
    fields_out,
    residue_out,
    spread_ref,
    remote,
    sources,
    rates,
    pressure,
    monomials,
    sampled,
):
    step = pl.program_id(0)
    width = fields_ref.shape[2]
    bound_count = remote.shape[1] // 8
    lanes = pl.ds(pl.multiple_of(step * width, width), width)

    @pl.when(step == 0)
    def _():
        pressure[...] = jnp.zeros_like(pressure)
        monomials[...] = jnp.zeros_like(monomials)
        sampled[...] = partial_ref[...]
        arrivals = [
            left_ref[2],
            above_ref[1],
            right_ref[2],
            left_ref[0],
            right_ref[0],
            left_ref[1],
            below_ref[1],
            right_ref[1],
        ]
        for heading, source in enumerate(arrivals):
            start = bound_count * heading
            remote[0:48, start : start + 96] = source[:, 0:96]
            for third in range(3):
                place = start + 32 * third
                remote[48:64, place : place + 32] = source[16 * third : 16 * third + 16, 96:128]

    def keep_split(start, value):
        high, low = halves(value)
        sources[start : start + FACE_ROWS, :] = high
        sources[256 + start : 256 + start + FACE_ROWS, :] = high
        sources[512 + start : 512 + start + FACE_ROWS, :] = low

    for face in range(4):
        beyond = -remote[0:16, lanes]
        for axis_id in range(3):
            facing = normals_ref[axis_id, face : face + 1, :]
            beyond = beyond + facing * remote[16 + 16 * axis_id : 32 + 16 * axis_id, lanes]
        is_remote = codes_ref[face : face + 1, :] >= slot_faces
        flux = jnp.where(is_remote, -0.5 * scale_ref[face : face + 1, :] * beyond, 0.0)
        keep_split(FACE_ROWS * face, flux)
        for axis_id in range(3):
            facing = normals_ref[axis_id, face : face + 1, :]
            keep_split(64 + 64 * axis_id + FACE_ROWS * face, facing * flux)
    rates[...] = time_step * product(lift_ref[:, 0:768], sources[...])
    for node in range(NODES):
        rate = rates[4 * node : 4 * node + 4, :]
        residue_out[node] = residue_ref[node] + rate
        fields_next = fields_ref[node] + section_gain * rate
        fields_out[node] = fields_next
        pressure[node : node + 1, :] = fields_next[0:1]
    parts = jnp.concatenate(thirds(pressure[...]), axis=0)
    slots = lax.broadcasted_iota(jnp.int32, (width, elems_ref.shape[1]), 0) + step * width
    picks = jnp.where(slots == elems_ref[...], 1.0, 0.0).astype(bf16)
    sampled[...] += product(parts, picks)

    @pl.when(step == pl.num_programs(0) - 1)
    def _():
        ladders = []
        for axis_id in range(3):
            base = coords_ref[axis_id : axis_id + 1, :]
            square = base * base
            ladders.append([jnp.ones_like(base), base, square, square * base, square * square])
        for node in range(NODES):
            exps = [int(entry) for entry in powers[node]]
            monomials[node : node + 1, :] = (
                ladders[0][exps[0]] * ladders[1][exps[1]] * ladders[2][exps[2]]
            )
        basis = jnp.dot(
            inverse_ref[...], monomials[...], precision=highest, preferred_element_type=f32
        )
        gathered = sampled[0:PAD, :] + sampled[48 : 48 + PAD, :] + sampled[96 : 96 + PAD, :]
        values = jnp.sum(basis * gathered, axis=0, keepdims=True)
        ids = ids_ref[...]
        owner = lax.shift_right_logical(ids * 5243, 20)
        place = ids - group * owner
        owners = lax.broadcasted_iota(jnp.int32, (spread_ref.shape[0], ids.shape[1]), 0)
        held = jnp.where(owners == owner, values, 0.0)
        places = lax.broadcasted_iota(jnp.int32, (spread_ref.shape[2], ids.shape[1]), 0)
        chosen = jnp.where(places == place, 1.0, 0.0).astype(bf16)
        spread = jnp.zeros((spread_ref.shape[0], spread_ref.shape[2]), f32)
        for part in thirds(held):
            spread = spread + product(part, chosen, ((1,), (1,)))
        spread_ref[:, 0, :] = spread


def harmonic_kernel(received_ref, table_ref, groups_ref, out_ref):
    mine = jnp.sum(received_ref[...], axis=0)
    weighted = groups_ref[...] * mine
    out_ref[...] = lax.dot_general(
        weighted,
        table_ref[...],
        (((1,), (1,)), ((), ())),
        precision=highest,
        preferred_element_type=f32,
    )


def in_hbm(array):
    return pltpu.with_memory_space_constraint(array, pltpu.HBM)


def in_vmem(array):
    return pltpu.with_memory_space_constraint(array, pltpu.VMEM)


def fixed(shape):
    return pl.BlockSpec(shape, lambda *_: (0,) * len(shape))


def local(
    fields,
    residue,
    geometry,
    normals,
    face_scale,
    neighbours,
    send_faces,
    live_counts,
    sample_ids,
    sample_elems,
    sample_coords,
):
    const = {
        name: in_hbm(table) if isinstance(table, jax.Array) else table
        for name, table in constant_tables().items()
    }
    fields = in_hbm(jnp.transpose(fields, (1, 0, 2)))
    residue = in_hbm(jnp.transpose(residue, (1, 0, 2)))
    geometry, normals, face_scale = in_hbm(geometry), in_hbm(normals), in_hbm(face_scale)
    neighbours, sample_coords = in_hbm(neighbours), in_hbm(sample_coords)
    slot_count = fields.shape[2]
    slot_faces = 4 * slot_count
    bound_count = send_faces.shape[1]
    reach = 8 * bound_count
    samples = sample_ids.shape[0]
    devices = lax.axis_size(("px", "py"))
    shape = jax.ShapeDtypeStruct

    elems = in_hbm(sample_elems.reshape(1, samples))
    width = LANES * FACE_TILES
    tiles = slot_count // width
    piece = (3, 48, LANES)

    up, down, left, right, faces = pl.pallas_call(
        functools.partial(pack_kernel, slot_faces),
        grid=(1,),
        in_specs=[
            pl.BlockSpec((NODES, 4, reach), lambda t: (0, 0, 0)),
            fixed((4, slot_count)),
            fixed((256, ROWS)),
        ],
        out_specs=[
            fixed(piece),
            fixed(piece),
            fixed(piece[1:]),
            fixed(piece[1:]),
            fixed((slot_faces // LANES, LANES)),
        ],
        out_shape=[
            pltpu.HBM(piece, f32),
            pltpu.HBM(piece, f32),
            shape(piece[1:], f32),
            shape(piece[1:], f32),
            pltpu.HBM((slot_faces // LANES, LANES), jnp.int32),
        ],
        scratch_shapes=[pltpu.VMEM((reach // LANES, ROWS, LANES), f32)],
        compiler_params=pltpu.CompilerParams(vmem_limit_bytes=16 << 20),
        name="pack",
    )(fields, neighbours, const["trace_select"])

    def steps_along(axis):
        count = lax.axis_size(axis)
        forward = [(i, i + 1) for i in range(count - 1)]
        return forward, [(target, source) for source, target in forward]

    forward, backward = steps_along("px")
    below = lax.ppermute(up, "px", backward)
    above = lax.ppermute(down, "px", forward)
    bulk = 3 * width
    bulks = slot_count // bulk

    def behind(rank):
        return lambda t, *_: (0,) * rank + (jnp.maximum(t - bulks - 1, 0),)

    def ahead(rank):
        return lambda t, *_: (0,) * rank + (jnp.clip(t - bulks, 0, tiles - 1),)

    fields_next, residue_next, partial = pl.pallas_call(
        functools.partial(section_kernel, slot_count, reach),
        grid_spec=pltpu.PrefetchScalarGridSpec(
            num_scalar_prefetch=1,
            grid=(bulks + tiles + 1,),
            in_specs=[
                pl.BlockSpec(memory_space=pltpu.HBM),
                pl.BlockSpec((3, 4, width), ahead(2)),
                pl.BlockSpec((NODES, 4, bulk), lambda t, *_: (0, 0, jnp.minimum(t, bulks - 1))),
                pl.BlockSpec((NODES, 4, width), behind(2)),
                pl.BlockSpec((NODES, 4, width), behind(2)),
                pl.BlockSpec((9, width), behind(1)),
                pl.BlockSpec((3, 4, width), behind(2)),
                pl.BlockSpec((4, width), behind(1)),
                pl.BlockSpec((4, width), behind(1)),
                fixed((1, samples)),
                fixed((2 * ROWS, 4 * LANES)),
                fixed((256, 2 * ROWS)),
                fixed((3 * ROWS, 96)),
                fixed((ROWS, 1024)),
            ],
            out_specs=[
                pl.BlockSpec((NODES, 4, width), behind(2)),
                pl.BlockSpec((NODES, 4, width), behind(2)),
                fixed((144, samples)),
            ],
            scratch_shapes=[
                pltpu.VMEM((slot_faces, LANES), f32),
                pltpu.VMEM((width // LANES, ROWS, LANES), f32),
                pltpu.VMEM((128, width), f32),
                pltpu.VMEM((48, width), f32),
                pltpu.VMEM((ROWS, width), f32),
                pltpu.VMEM((64, width), f32),
                pltpu.VMEM((64, width), f32),
                pltpu.VMEM((48, width), f32),
                pltpu.VMEM((width // 256, 2 * ROWS, 256), bf16),
                pltpu.VMEM((width // 256, 96, 256), bf16),
                pltpu.VMEM((width // 256, 256, 256), f32),
                pltpu.VMEM((width // 256, 1024, 256), bf16),
                pltpu.SMEM((4 * width,), jnp.int32),
                pltpu.SMEM((4 * width,), jnp.int32),
                pltpu.SemaphoreType.DMA((2,)),
                *[pltpu.VMEM((LANES, LANES), f32)] * 4,
            ],
        ),
        out_shape=[
            shape(fields.shape, f32),
            shape(residue.shape, f32),
            shape((144, samples), f32),
        ],
        compiler_params=pltpu.CompilerParams(vmem_limit_bytes=48 << 20),
        name="section",
    )(
        live_counts,
        in_hbm(faces.reshape(-1)),
        normals,
        fields,
        fields,
        residue,
        geometry,
        normals,
        face_scale,
        neighbours,
        elems,
        const["table_select"],
        const["twice_select"],
        const["from_p"],
        const["lift"],
    )

    below, above, partial = lax.optimization_barrier((below, above, partial))
    to_left, to_right = pl.pallas_call(
        relay_kernel,
        out_shape=[pltpu.VMEM(piece, f32), pltpu.VMEM(piece, f32)],
        name="relay",
    )(in_vmem(left), in_vmem(right), in_vmem(below), in_vmem(above))
    forward, backward = steps_along("py")
    from_right = lax.ppermute(to_left, "py", backward)
    from_left = lax.ppermute(to_right, "py", forward)

    def head(rank):
        return lambda t: (0,) * (rank - 1) + (t,)

    part = 256

    fields_next, residue_next, spread = pl.pallas_call(
        functools.partial(boundary_kernel, slot_faces, const["powers"], samples),
        grid=(reach // part,),
        in_specs=[
            pl.BlockSpec((NODES, 4, part), head(3)),
            pl.BlockSpec((NODES, 4, part), head(3)),
            pl.BlockSpec((3, 4, part), head(3)),
            pl.BlockSpec((4, part), head(2)),
            pl.BlockSpec((4, part), head(2)),
            fixed(piece),
            fixed(piece),
            fixed(piece),
            fixed(piece),
            fixed((1, samples)),
            fixed((1, samples)),
            fixed((3, samples)),
            fixed((144, samples)),
            fixed((ROWS, 1024)),
            fixed((PAD, PAD)),
        ],
        out_specs=[
            pl.BlockSpec((NODES, 4, part), head(3)),
            pl.BlockSpec((NODES, 4, part), head(3)),
            fixed((devices, 1, samples)),
        ],
        out_shape=[
            shape(fields.shape, f32),
            shape(residue.shape, f32),
            shape((devices, 1, samples), f32),
        ],
        scratch_shapes=[
            pltpu.VMEM((64, reach), f32),
            pltpu.VMEM((768, part), bf16),
            pltpu.VMEM((ROWS, part), f32),
            pltpu.VMEM((48, part), f32),
            pltpu.VMEM((PAD, samples), f32),
            pltpu.VMEM((144, samples), f32),
        ],
        input_output_aliases={0: 0, 1: 1},
        compiler_params=pltpu.CompilerParams(vmem_limit_bytes=24 << 20),
        name="boundary",
    )(
        in_hbm(fields_next),
        in_hbm(residue_next),
        normals,
        face_scale,
        neighbours,
        from_right,
        from_left,
        below,
        above,
        elems,
        in_hbm(sample_ids.reshape(1, samples)),
        sample_coords,
        partial,
        const["lift"],
        const["inverse"],
    )
    received = lax.all_to_all(spread, ("px", "py"), 0, 0, tiled=True)

    receivers = samples // QPTS
    harmonic = np.tile(harmonic_table(), (1, receivers)).astype(np.float32)
    groups = (np.arange(samples)[None] // QPTS == np.arange(receivers)[:, None]).astype(np.float32)
    coefficients = pl.pallas_call(
        harmonic_kernel,
        out_shape=shape((receivers, harmonic.shape[0]), f32),
        name="harmonic",
    )(received, jnp.asarray(harmonic), jnp.asarray(groups))
    return (
        jnp.transpose(fields_next, (1, 0, 2)),
        jnp.transpose(residue_next, (1, 0, 2)),
        coefficients.T,
    )


def solution(mesh):
    placed = (
        P(None, None, ("px", "py")),
        P(None, None, ("px", "py")),
        P(None, ("px", "py")),
        P(None, None, ("px", "py")),
        P(None, ("px", "py")),
        P(None, ("px", "py")),
        P(None, ("px", "py")),
        P(("px", "py")),
        P(("px", "py")),
        P(("px", "py")),
        P(None, ("px", "py")),
    )
    return jax.shard_map(
        local,
        mesh=mesh,
        in_specs=placed,
        out_specs=(P(None, None, ("px", "py")), P(None, None, ("px", "py")), P(None, ("px", "py"))),
        check_vma=False,
    )
```

```python
import functools
import math

import jax
import jax.numpy as jnp
import numpy as np
from jax import lax
from jax.experimental import pallas as pl
from jax.experimental.pallas import tpu as pltpu
from jax.sharding import PartitionSpec as P

QPTS = 50
NODES = 35
PAD = 40
FACE_ROWS = 16
ROWS = 144
LANES = 128
FACE_TILES = 4


highest = lax.Precision.HIGHEST
section_decay = -567301805773.0 / 1357537059087.0
section_gain = 5161836677717.0 / 13612068292357.0
time_step = 0.01
f32 = jnp.float32
bf16 = jnp.bfloat16


def exponent_table():
    listing = []
    for degree in range(5):
        for third in range(degree + 1):
            for second in range(degree + 1 - third):
                listing.append((degree - second - third, second, third))
    return np.array(listing)


def factorials(values):
    lookup = np.array([float(math.factorial(level)) for level in range(24)])
    return lookup[values]


def eliminate(matrix, right_hand):
    order_size = matrix.shape[0]
    work = np.concatenate([matrix, right_hand], axis=1).astype(float)
    for pivot_col in range(order_size):
        best = max(range(pivot_col, order_size), key=lambda row_id: abs(work[row_id, pivot_col]))
        work[[pivot_col, best]] = work[[best, pivot_col]]
        work[pivot_col] = work[pivot_col] / work[pivot_col, pivot_col]
        for row_id in range(order_size):
            if row_id != pivot_col:
                work[row_id] = work[row_id] - work[row_id, pivot_col] * work[pivot_col]
    return work[:, order_size:]


def element_tables():
    powers = exponent_table()
    points = powers / 4.0
    vander = np.prod(points[:, None, :] ** powers[None, :, :], axis=2)
    inverse = eliminate(vander, np.eye(35))
    derivs = []
    for axis_id in range(3):
        lowered = np.maximum(powers - (np.arange(3) == axis_id)[None, :], 0)
        slope_table = powers[None, :, axis_id] * np.prod(
            points[:, None, :] ** lowered[None, :, :], axis=2
        )
        derivs.append(slope_table @ inverse)
    summed = powers[:, None, :] + powers[None, :, :]
    exp_r = summed[..., 0]
    exp_s = summed[..., 1]
    exp_t = summed[..., 2]
    volume = (
        factorials(exp_r)
        * factorials(exp_s)
        * factorials(exp_t)
        / factorials(exp_r + exp_s + exp_t + 3)
    )
    mass_matrix = inverse.T @ volume @ inverse
    face_grams = [
        np.where(
            exp_t == 0, factorials(exp_r) * factorials(exp_s) / factorials(exp_r + exp_s + 2), 0.0
        ),
        np.where(
            exp_s == 0, factorials(exp_r) * factorials(exp_t) / factorials(exp_r + exp_t + 2), 0.0
        ),
        factorials(exp_r)
        * factorials(exp_s)
        * factorials(exp_t)
        / factorials(exp_r + exp_s + exp_t + 2),
        np.where(
            exp_r == 0, factorials(exp_s) * factorials(exp_t) / factorials(exp_s + exp_t + 2), 0.0
        ),
    ]
    listed = [tuple((int(entry) for entry in powers[node_id])) for node_id in range(35)]
    face_nodes = np.array(
        [
            [node_id for node_id in range(35) if listed[node_id][2] == 0],
            [node_id for node_id in range(35) if listed[node_id][1] == 0],
            [node_id for node_id in range(35) if sum(listed[node_id]) == 4],
            [node_id for node_id in range(35) if listed[node_id][0] == 0],
        ]
    )
    surface = np.zeros((35, 60))
    for face_id in range(4):
        face_mass = inverse.T @ face_grams[face_id] @ inverse
        for node_id in range(15):
            surface[:, 4 * node_id + face_id] = face_mass[:, face_nodes[face_id, node_id]]
    lifting = eliminate(mass_matrix, surface)
    return (np.stack(derivs), lifting, face_nodes, inverse, powers)


def associated(degree, order, cosine, sine):
    current = cosine * 0.0 + 1.0
    for step_id in range(1, order + 1):
        current = -(2 * step_id - 1) * sine * current
    if degree == order:
        return current
    following = cosine * (2 * order + 1) * current
    for level in range(order + 2, degree + 1):
        current, following = (
            following,
            ((2 * level - 1) * cosine * following - (level + order - 1) * current)
            / (level - order),
        )
    return following


def harmonic_table():
    inner_node = math.sqrt(5.0 - 2.0 * math.sqrt(10.0 / 7.0)) / 3.0
    outer_node = math.sqrt(5.0 + 2.0 * math.sqrt(10.0 / 7.0)) / 3.0
    inner_weight = (322.0 + 13.0 * math.sqrt(70.0)) / 900.0
    outer_weight = (322.0 - 13.0 * math.sqrt(70.0)) / 900.0
    cosines = np.array([-outer_node, -inner_node, 0.0, inner_node, outer_node])
    weights = np.array([outer_weight, inner_weight, 128.0 / 225.0, inner_weight, outer_weight])
    azimuth = 2.0 * np.pi * (np.arange(10) + 0.5) / 10.0
    polar = np.repeat(cosines, 10)
    circle = np.tile(azimuth, 5)
    point_weight = np.repeat(weights, 10) * 2.0 * np.pi / 10.0
    sine = np.sqrt(1.0 - polar**2)
    table_rows = []
    for degree in range(5):
        for order in range(-degree, degree + 1):
            absolute = abs(order)
            legendre = associated(degree, absolute, polar, sine)
            factor = math.sqrt(
                (2 * degree + 1)
                / (4.0 * math.pi)
                * math.factorial(degree - absolute)
                / math.factorial(degree + absolute)
            )
            if order > 0:
                angular = math.sqrt(2.0) * np.cos(order * circle)
            elif order < 0:
                angular = math.sqrt(2.0) * np.sin(absolute * circle)
            else:
                angular = circle * 0.0 + 1.0
            table_rows.append(factor * legendre * angular * point_weight)
    return np.array(table_rows)


def constant_tables():
    derivs, lifting, face_nodes, inverse, powers = element_tables()
    table_select = np.zeros((ROWS, 4 * LANES), np.float32)
    trace_select = np.zeros((4 * 4 * FACE_ROWS, ROWS), np.float32)
    for face in range(4):
        for field in range(4):
            for place in range(15):
                source = 4 * face_nodes[face, place] + field
                column = FACE_ROWS * field + place
                table_select[source, LANES * face + column] = 1.0
                table_select[source, LANES * face + 64 + column] = 1.0
                trace_select[64 * face + column, source] = 1.0
    whole = np.round(3.0 * derivs)
    into_p = np.zeros((ROWS, 128), np.float32)
    from_p = np.zeros((3 * ROWS, 48), np.float32)
    lift = np.zeros((ROWS, 256), np.float32)
    for node in range(NODES):
        for axis_id in range(3):
            into_p[4 * node, PAD * axis_id : PAD * axis_id + NODES] = -whole[axis_id, node]
            for field in range(1, 4):
                from_p[ROWS * axis_id + 4 * node + field, :NODES] = whole[axis_id, node]
        for face in range(4):
            for place in range(15):
                entry = lifting[node, 4 * place + face]
                column = FACE_ROWS * face + place
                lift[4 * node, column] = entry
                for field in range(1, 4):
                    lift[4 * node + field, 64 * field + column] = -entry
    lift_hi = lift.astype(jnp.bfloat16)
    lift_lo = (lift - lift_hi.astype(np.float32)).astype(jnp.bfloat16)
    return {
        "table_select": jnp.asarray(np.concatenate([table_select] * 2, axis=0), bf16),
        "trace_select": jnp.asarray(trace_select, bf16),
        "twice_select": jnp.asarray(np.concatenate([trace_select] * 2, axis=1), bf16),
        "from_p": jnp.asarray(np.concatenate([from_p, from_p], axis=1), bf16),
        "lift": jnp.asarray(
            np.concatenate(
                [lift_hi, lift_lo, lift_hi] + [into_p.astype(jnp.bfloat16)] * 2, axis=1
            )
        ),
        "inverse": jnp.asarray(np.pad(inverse.T, ((0, 5), (0, 5))), f32),
        "powers": powers,
    }


def halves(values):
    high = values.astype(bf16)
    return high, (values - high.astype(f32)).astype(bf16)


def thirds(values):
    high = values.astype(bf16)
    rest = values - high.astype(f32)
    middle = rest.astype(bf16)
    return high, middle, (rest - middle.astype(f32)).astype(bf16)


def product(left, right, dims=((1,), (0,))):
    return lax.dot_general(left, right, (dims, ((), ())), preferred_element_type=f32)


def stack_nodes(fields_ref, stacked):
    tiles = range(stacked.shape[0])
    for tile in tiles:
        for node in range(NODES):
            stacked[tile, 4 * node : 4 * node + 4, :] = fields_ref[
                node, :, LANES * tile : LANES * tile + LANES
            ]
    return halves(jnp.concatenate([stacked[tile] for tile in tiles], axis=1))


def one_field(stacked, field):
    tiles = range(stacked.shape[0])
    rows = pl.ds(field, NODES, stride=4)
    return jnp.concatenate([stacked[tile, rows, :] for tile in tiles], axis=1)


def pack_kernel(
    slot_faces,
    fields_ref,
    codes_ref,
    select_ref,
    up_ref,
    down_ref,
    left_ref,
    right_ref,
    faces_ref,
    stacked,
):
    stacked[...] = jnp.zeros_like(stacked)
    high, low = stack_nodes(fields_ref, stacked)
    traces = product(select_ref[...], high) + product(select_ref[...], low)
    reach = fields_ref.shape[2]
    count = reach // 8
    chosen = jnp.zeros((64, reach), f32)
    for face in range(4):
        remote = codes_ref[face : face + 1, 0:reach] >= slot_faces
        chosen = jnp.where(remote, traces[64 * face : 64 * face + 64, :], chosen)
    homes = [up_ref.at[0], up_ref.at[1], up_ref.at[2], left_ref, right_ref]
    homes += [down_ref.at[0], down_ref.at[1], down_ref.at[2]]
    for heading, home in enumerate(homes):
        part = chosen[:, count * heading : count * heading + count]
        home[:, 0:96] = part[0:48]
        for third in range(3):
            home[16 * third : 16 * third + 16, 96:128] = part[48:64, 32 * third : 32 * third + 32]
    tiles = codes_ref.shape[1] // LANES
    codes = codes_ref[...]
    codes = jnp.where((codes >= 0) & (codes < slot_faces), codes, 0)
    for face in range(4):
        for tile in range(tiles):
            row = 4 * FACE_TILES * (tile // FACE_TILES) + FACE_TILES * face + tile % FACE_TILES
            faces_ref[row : row + 1, :] = codes[
                face : face + 1, LANES * tile : LANES * tile + LANES
            ]


def relay_kernel(left_ref, right_ref, below_ref, above_ref, to_left_ref, to_right_ref):
    to_left_ref[0] = left_ref[...]
    to_left_ref[1] = below_ref[0]
    to_left_ref[2] = above_ref[0]
    to_right_ref[0] = right_ref[...]
    to_right_ref[1] = below_ref[2]
    to_right_ref[2] = above_ref[2]


def build_rows(first, part, fields_ref, select_ref, table_ref, stacked):
    slot_count = table_ref.shape[0] // 4
    width = LANES * stacked.shape[0]
    high, low = stack_nodes(fields_ref.at[:, :, width * part : width * part + width], stacked)
    both = jnp.concatenate([high, low], axis=0)
    for half in range(2):
        select = select_ref[:, 256 * half : 256 * half + 256]
        rows = product(both, select, ((0,), (0,)))
        for side in range(2):
            start = pl.multiple_of((2 * half + side) * slot_count + first + width * part, width)
            table_ref[pl.ds(start, width), :] = rows[:, LANES * side : LANES * side + LANES]


def gather_pieces(faces_ref, table_ref, normals_ref, outer_ref, rows_refs):
    width = outer_ref.shape[1]
    left_half = lax.broadcasted_iota(jnp.int32, (1, LANES), 1) < 64

    def load(tile, rows):
        for row in rows:
            at = tile * LANES + row
            for half in range(2):
                one = table_ref[pl.ds(faces_ref[2 * half * width + at], 1), :]
                two = table_ref[pl.ds(faces_ref[(2 * half + 1) * width + at], 1), :]
                rows_ref = rows_refs[2 * (tile % 2) + half]
                rows_ref[row : row + 1, :] = jnp.where(left_half, one, two)

    def combine(tile, half):
        turned = rows_refs[2 * (tile % 2) + half][...].T
        lanes = slice(tile * LANES, tile * LANES + LANES)
        for side in range(2):
            face = 2 * half + side
            part = turned[64 * side : 64 * side + 64, :]
            total = -part[0:16]
            for axis_id in range(3):
                facing = normals_ref[axis_id, face : face + 1, lanes]
                total = total + facing * part[16 + 16 * axis_id : 32 + 16 * axis_id]
            outer_ref[FACE_ROWS * face : FACE_ROWS * face + FACE_ROWS, lanes] = total

    for tile in range(width // LANES):
        for part in range(8):
            rows = range(16 * part, 16 * part + 16)
            yield functools.partial(load, tile, rows)
            if tile > 0 and part < 2:
                yield functools.partial(combine, tile - 1, part)
    for half in range(2):
        yield functools.partial(combine, tile, half)


def section_kernel(
    slot_count,
    reach,
    live_ref,
    faces_hbm,
    next_normals_ref,
    bulk_ref,
    fields_ref,
    residue_ref,
    geometry_ref,
    normals_ref,
    scale_ref,
    codes_ref,
    elems_ref,
    table_select_ref,
    select_ref,
    from_ref,
    lift_ref,
    fields_out,
    residue_out,
    sampled,
    table_ref,
    stacked,
    combined,
    slow,
    rates,
    outer,
    beyond_ref,
    pressure,
    fields_split,
    slow_split,
    inner,
    sources,
    even_faces,
    odd_faces,
    arrived,
    *rows_refs,
):
    faces_refs = (even_faces, odd_faces)
    width = fields_ref.shape[2]
    tiles = slot_count // width
    bulks = slot_count // bulk_ref.shape[2]
    step = pl.program_id(0) - bulks
    slot_faces = 4 * slot_count
    half_width = 256

    def codes_copy(tile, parity):
        source = faces_hbm.at[pl.ds(pl.multiple_of(tile * 4 * width, 4 * width), 4 * width)]
        return pltpu.make_async_copy(source, faces_refs[parity], arrived.at[parity])

    def gather(parity):
        return gather_pieces(
            faces_refs[parity], table_ref, next_normals_ref, outer, rows_refs
        )

    def take_codes(parity):
        codes_copy(step, parity).wait()

        @pl.when((step + 1) * width < live_ref[0])
        def _():
            codes_copy(step + 1, 1 - parity).start()

    def update_pieces():
        first = (step - 1) * width

        def stack(at, low, high):
            for tile in range(2 * at, 2 * at + 2):
                for node in range(low, high):
                    stacked[tile, 4 * node : 4 * node + 4, :] = fields_ref[
                        node, :, LANES * tile : LANES * tile + LANES
                    ]

        def split(at):
            for side in range(2):
                lanes = slice(LANES * side, LANES * side + LANES)
                high, low = halves(stacked[2 * at + side])
                fields_split[at, 0:ROWS, lanes] = high
                fields_split[at, ROWS : 2 * ROWS, lanes] = low

        def inside(at):
            return slice(half_width * at, half_width * at + half_width)

        def field_rows(at, field):
            rows = pl.ds(field, NODES, stride=4)
            return jnp.concatenate([stacked[tile, rows, :] for tile in (2 * at, 2 * at + 1)], axis=1)

        def copy_slow(at):
            lanes = inside(at)
            slow[0:NODES, lanes] = field_rows(at, 0)
            slow_split[at, 0:48, :], slow_split[at, 48:96, :] = halves(slow[:, lanes])

        def weigh(at, axis_id):
            lanes = inside(at)
            weighted = jnp.zeros((NODES, half_width), f32)
            for direction in range(3):
                row = 3 * axis_id + direction
                factor = geometry_ref[row : row + 1, lanes] * (1.0 / 3.0)
                weighted = weighted + factor * field_rows(at, 1 + direction)
            combined[PAD * axis_id : PAD * axis_id + NODES, lanes] = weighted

        def split_weighted(at):
            high, low = halves(combined[:, inside(at)])
            sources[at, 768:896, :], sources[at, 896:1024, :] = high, low

        def traces(at):
            inner[at] = product(select_ref[...], fields_split[at])

        def slope(at, axis_id):
            lanes = inside(at)
            place = lax.broadcasted_iota(jnp.int32, (8, half_width), 0) & 3
            value = product(from_ref[ROWS * axis_id : ROWS * axis_id + ROWS, :], slow_split[at])
            pattern = jnp.zeros((8, half_width), f32)
            for direction in range(3):
                row = 3 * axis_id + direction
                factor = geometry_ref[row : row + 1, lanes] * (1.0 / 3.0)
                pattern = jnp.where(place == direction + 1, factor, pattern)
            value = value.reshape(ROWS // 8, 8, half_width) * pattern[None]
            value = value.reshape(ROWS, half_width)
            if axis_id == 0:
                rates[:, lanes] = value
            else:
                rates[:, lanes] += value

        def keep_split(at, start, value):
            high, low = halves(value)
            rows = value.shape[0]
            sources[at, start : start + rows, :] = high
            sources[at, 256 + start : 256 + start + rows, :] = high
            sources[at, 512 + start : 512 + start + rows, :] = low

        def jump(at, face):
            lanes = inside(at)
            inner_p = inner[at, 64 * face : 64 * face + 16, :]
            along = jnp.zeros_like(inner_p)
            for axis_id in range(3):
                facing = normals_ref[axis_id, face : face + 1, lanes]
                start = 64 * face + 16 + 16 * axis_id
                along = along + facing * inner[at, start : start + 16, :]
            wall = codes_ref[face : face + 1, lanes] < 0
            beyond = beyond_ref[FACE_ROWS * face : FACE_ROWS * face + FACE_ROWS, lanes]
            beyond = jnp.where(wall, -along - inner_p, beyond)
            beyond = jnp.where(codes_ref[face : face + 1, lanes] >= slot_faces, 0.0, beyond)
            scale = 0.5 * scale_ref[face : face + 1, lanes]
            value = scale * (along - inner_p - beyond)
            keep_split(at, FACE_ROWS * face, value)
            for axis_id in range(3):
                start = 64 + 64 * axis_id + FACE_ROWS * face
                keep_split(at, start, normals_ref[axis_id, face : face + 1, lanes] * value)

        def lift(at):
            lanes = inside(at)
            rates[:, lanes] = product(lift_ref[...], sources[at]) - rates[:, lanes]

        def advance(at, low, high):
            lanes = inside(at)
            slots = lax.broadcasted_iota(jnp.int32, (1, half_width), 1) + (first + half_width * at)
            keep = slots < live_ref[0]
            for node in range(low, high):
                rate = rates[4 * node : 4 * node + 4, lanes]
                residue_next = section_decay * residue_ref[node, :, lanes] + time_step * rate
                fields_next = fields_ref[node, :, lanes] + section_gain * residue_next
                fields_next = jnp.where(keep, fields_next, 0.0)
                fields_out[node, :, lanes] = fields_next
                residue_out[node, :, lanes] = jnp.where(keep, residue_next, 0.0)
                pressure[node : node + 1, lanes] = fields_next[0:1]

        def sample(at):
            lanes = inside(at)
            parts = jnp.concatenate(thirds(pressure[:, lanes]), axis=0)
            start = first + half_width * at
            slots = lax.broadcasted_iota(jnp.int32, (half_width, elems_ref.shape[1]), 0) + start
            elems = elems_ref[...]
            picks = (slots == elems) & (elems >= reach)
            sampled[...] += product(parts, jnp.where(picks, 1.0, 0.0).astype(bf16))

        call = functools.partial

        def stages(at):
            sevens = range(0, NODES, 7)
            return [
                [call(stack, at, low, low + 7) for low in sevens] + [call(split, at)],
                [call(copy_slow, at)]
                + [call(weigh, at, axis_id) for axis_id in range(3)]
                + [call(split_weighted, at), call(traces, at)],
                [call(slope, at, axis_id) for axis_id in range(3)],
                [call(jump, at, face) for face in range(4)],
                [call(lift, at)],
                [call(advance, at, low, low + 7) for low in sevens],
                [call(sample, at)],
            ]

        both = [stages(at) for at in range(width // half_width)]
        depth = len(both[0])
        return [
            [piece for lag, chain in enumerate(both) if 0 <= at - lag < depth for piece in chain[at - lag]]
            for at in range(depth + len(both) - 1)
        ]

    def interleave(gathers, groups):
        gathers = list(gathers)

        def run(at, updates, groups):
            @pl.when(live_ref[0] > at)
            def _():
                low = at * len(gathers) // len(groups)
                loads = gathers[low : (at + 1) * len(gathers) // len(groups)]
                order = [(place / len(loads), 0, place) for place in range(len(loads))]
                order += [((place + 1) / len(updates), 1, place) for place in range(len(updates))]
                for _, kind, place in sorted(order):
                    (loads, updates)[kind][place]()

        cuts = (0, 4, 8)
        groups = [sum(groups[low:high], []) for low, high in zip(cuts, cuts[1:])]
        for at, updates in enumerate(groups):
            run(at, updates, groups)

    @pl.when(step == -bulks)
    def _():
        stacked[...] = jnp.zeros_like(stacked)
        combined[...] = jnp.zeros_like(combined)
        slow[...] = jnp.zeros_like(slow)
        pressure[...] = jnp.zeros_like(pressure)
        sampled[...] = jnp.zeros_like(sampled)

    @pl.when(step < 0)
    def _():
        first = (step + bulks) * bulk_ref.shape[2]
        for part in range(bulk_ref.shape[2] // width):

            @pl.when(first + width * part < live_ref[0])
            def _():
                build_rows(first, part, bulk_ref, table_select_ref, table_ref, stacked)

    @pl.when(step == -1)
    def _():
        codes_copy(0, 0).start()

    @pl.when(step == 0)
    def _():
        take_codes(0)
        for piece in gather(0):
            piece()

    for parity in range(2):

        @pl.when((step > 0) & (step * width < live_ref[0]) & (step % 2 == parity))
        def _():
            take_codes(parity)
            beyond_ref[...] = outer[...]
            interleave(gather(parity), update_pieces())

    @pl.when((step > 0) & ((step - 1) * width >= live_ref[0]))
    def _():
        fields_out[...] = jnp.zeros_like(fields_out)
        residue_out[...] = jnp.zeros_like(residue_out)

    @pl.when((step > 0) & ((step - 1) * width < live_ref[0]) & (step * width >= live_ref[0]))
    def _():
        beyond_ref[...] = outer[...]
        for stage in update_pieces():
            for piece in stage:
                piece()


def boundary_kernel(
    slot_faces,
    powers,
    group,
    fields_ref,
    residue_ref,
    normals_ref,
    scale_ref,
    codes_ref,
    right_ref,
    left_ref,
    below_ref,
    above_ref,
    elems_ref,
    ids_ref,
    coords_ref,
    partial_ref,
    lift_ref,
    inverse_ref,
    fields_out,
    residue_out,
    spread_ref,
    remote,
    sources,
    rates,
    pressure,
    monomials,
):
    reach = fields_ref.shape[2]
    bound_count = reach // 8
    pressure[...] = jnp.zeros_like(pressure)
    monomials[...] = jnp.zeros_like(monomials)
    arrivals = [
        left_ref[2],
        above_ref[1],
        right_ref[2],
        left_ref[0],
        right_ref[0],
        left_ref[1],
        below_ref[1],
        right_ref[1],
    ]
    for heading, source in enumerate(arrivals):
        start = bound_count * heading
        remote[0:48, start : start + 96] = source[:, 0:96]
        for third in range(3):
            place = start + 32 * third
            remote[48:64, place : place + 32] = source[16 * third : 16 * third + 16, 96:128]

    def keep_split(start, value):
        high, low = halves(value)
        sources[start : start + FACE_ROWS, :] = high
        sources[256 + start : 256 + start + FACE_ROWS, :] = high
        sources[512 + start : 512 + start + FACE_ROWS, :] = low

    for face in range(4):
        beyond = -remote[0:16, :]
        for axis_id in range(3):
            facing = normals_ref[axis_id, face : face + 1, :]
            beyond = beyond + facing * remote[16 + 16 * axis_id : 32 + 16 * axis_id, :]
        is_remote = codes_ref[face : face + 1, :] >= slot_faces
        flux = jnp.where(is_remote, -0.5 * scale_ref[face : face + 1, :] * beyond, 0.0)
        keep_split(FACE_ROWS * face, flux)
        for axis_id in range(3):
            facing = normals_ref[axis_id, face : face + 1, :]
            keep_split(64 + 64 * axis_id + FACE_ROWS * face, facing * flux)
    rates[...] = time_step * product(lift_ref[:, 0:768], sources[...])
    for node in range(NODES):
        rate = rates[4 * node : 4 * node + 4, :]
        residue_out[node] = residue_ref[node] + rate
        fields_next = fields_ref[node] + section_gain * rate
        fields_out[node] = fields_next
        pressure[node : node + 1, :] = fields_next[0:1]
    parts = jnp.concatenate(thirds(pressure[...]), axis=0)
    slots = lax.broadcasted_iota(jnp.int32, (reach, elems_ref.shape[1]), 0)
    picks = jnp.where(slots == elems_ref[...], 1.0, 0.0).astype(bf16)
    sampled = partial_ref[...] + product(parts, picks)
    ladders = []
    for axis_id in range(3):
        base = coords_ref[axis_id : axis_id + 1, :]
        square = base * base
        ladders.append([jnp.ones_like(base), base, square, square * base, square * square])
    for node in range(NODES):
        exps = [int(entry) for entry in powers[node]]
        monomials[node : node + 1, :] = (
            ladders[0][exps[0]] * ladders[1][exps[1]] * ladders[2][exps[2]]
        )
    basis = jnp.dot(
        inverse_ref[...], monomials[...], precision=highest, preferred_element_type=f32
    )
    gathered = sampled[0:PAD, :] + sampled[48 : 48 + PAD, :] + sampled[96 : 96 + PAD, :]
    values = jnp.sum(basis * gathered, axis=0, keepdims=True)
    ids = ids_ref[...]
    owner = lax.shift_right_logical(ids * 5243, 20)
    place = ids - group * owner
    owners = lax.broadcasted_iota(jnp.int32, (spread_ref.shape[0], ids.shape[1]), 0)
    held = jnp.where(owners == owner, values, 0.0)
    places = lax.broadcasted_iota(jnp.int32, (spread_ref.shape[2], ids.shape[1]), 0)
    chosen = jnp.where(places == place, 1.0, 0.0).astype(bf16)
    spread = jnp.zeros((spread_ref.shape[0], spread_ref.shape[2]), f32)
    for part in thirds(held):
        spread = spread + product(part, chosen, ((1,), (1,)))
    spread_ref[:, 0, :] = spread


def harmonic_kernel(received_ref, table_ref, groups_ref, out_ref):
    mine = jnp.sum(received_ref[...], axis=0)
    weighted = groups_ref[...] * mine
    out_ref[...] = lax.dot_general(
        weighted,
        table_ref[...],
        (((1,), (1,)), ((), ())),
        precision=highest,
        preferred_element_type=f32,
    )


def in_hbm(array):
    return pltpu.with_memory_space_constraint(array, pltpu.HBM)


def in_vmem(array):
    return pltpu.with_memory_space_constraint(array, pltpu.VMEM)


def fixed(shape):
    return pl.BlockSpec(shape, lambda *_: (0,) * len(shape))


def local(
    fields,
    residue,
    geometry,
    normals,
    face_scale,
    neighbours,
    send_faces,
    live_counts,
    sample_ids,
    sample_elems,
    sample_coords,
):
    const = {
        name: in_hbm(table) if isinstance(table, jax.Array) else table
        for name, table in constant_tables().items()
    }
    fields = in_hbm(jnp.transpose(fields, (1, 0, 2)))
    residue = in_hbm(jnp.transpose(residue, (1, 0, 2)))
    geometry, normals, face_scale = in_hbm(geometry), in_hbm(normals), in_hbm(face_scale)
    neighbours, sample_coords = in_hbm(neighbours), in_hbm(sample_coords)
    slot_count = fields.shape[2]
    slot_faces = 4 * slot_count
    bound_count = send_faces.shape[1]
    reach = 8 * bound_count
    samples = sample_ids.shape[0]
    devices = lax.axis_size(("px", "py"))
    shape = jax.ShapeDtypeStruct

    elems = in_hbm(sample_elems.reshape(1, samples))
    width = LANES * FACE_TILES
    tiles = slot_count // width
    piece = (3, 48, LANES)

    up, down, left, right, faces = pl.pallas_call(
        functools.partial(pack_kernel, slot_faces),
        grid=(1,),
        in_specs=[
            pl.BlockSpec((NODES, 4, reach), lambda t: (0, 0, 0)),
            fixed((4, slot_count)),
            fixed((256, ROWS)),
        ],
        out_specs=[
            fixed(piece),
            fixed(piece),
            fixed(piece[1:]),
            fixed(piece[1:]),
            fixed((slot_faces // LANES, LANES)),
        ],
        out_shape=[
            pltpu.HBM(piece, f32),
            pltpu.HBM(piece, f32),
            shape(piece[1:], f32),
            shape(piece[1:], f32),
            pltpu.HBM((slot_faces // LANES, LANES), jnp.int32),
        ],
        scratch_shapes=[pltpu.VMEM((reach // LANES, ROWS, LANES), f32)],
        compiler_params=pltpu.CompilerParams(vmem_limit_bytes=16 << 20),
        name="pack",
    )(fields, neighbours, const["trace_select"])

    def steps_along(axis):
        count = lax.axis_size(axis)
        forward = [(i, i + 1) for i in range(count - 1)]
        return forward, [(target, source) for source, target in forward]

    forward, backward = steps_along("px")
    below = lax.ppermute(up, "px", backward)
    above = lax.ppermute(down, "px", forward)
    bulk = 3 * width
    bulks = slot_count // bulk

    def behind(rank):
        return lambda t, *_: (0,) * rank + (jnp.maximum(t - bulks - 1, 0),)

    def ahead(rank):
        return lambda t, *_: (0,) * rank + (jnp.clip(t - bulks, 0, tiles - 1),)

    fields_next, residue_next, partial = pl.pallas_call(
        functools.partial(section_kernel, slot_count, reach),
        grid_spec=pltpu.PrefetchScalarGridSpec(
            num_scalar_prefetch=1,
            grid=(bulks + tiles + 1,),
            in_specs=[
                pl.BlockSpec(memory_space=pltpu.HBM),
                pl.BlockSpec((3, 4, width), ahead(2)),
                pl.BlockSpec((NODES, 4, bulk), lambda t, *_: (0, 0, jnp.minimum(t, bulks - 1))),
                pl.BlockSpec((NODES, 4, width), behind(2)),
                pl.BlockSpec((NODES, 4, width), behind(2)),
                pl.BlockSpec((9, width), behind(1)),
                pl.BlockSpec((3, 4, width), behind(2)),
                pl.BlockSpec((4, width), behind(1)),
                pl.BlockSpec((4, width), behind(1)),
                fixed((1, samples)),
                fixed((2 * ROWS, 4 * LANES)),
                fixed((256, 2 * ROWS)),
                fixed((3 * ROWS, 96)),
                fixed((ROWS, 1024)),
            ],
            out_specs=[
                pl.BlockSpec((NODES, 4, width), behind(2)),
                pl.BlockSpec((NODES, 4, width), behind(2)),
                fixed((144, samples)),
            ],
            scratch_shapes=[
                pltpu.VMEM((slot_faces, LANES), f32),
                pltpu.VMEM((width // LANES, ROWS, LANES), f32),
                pltpu.VMEM((128, width), f32),
                pltpu.VMEM((48, width), f32),
                pltpu.VMEM((ROWS, width), f32),
                pltpu.VMEM((64, width), f32),
                pltpu.VMEM((64, width), f32),
                pltpu.VMEM((48, width), f32),
                pltpu.VMEM((width // 256, 2 * ROWS, 256), bf16),
                pltpu.VMEM((width // 256, 96, 256), bf16),
                pltpu.VMEM((width // 256, 256, 256), f32),
                pltpu.VMEM((width // 256, 1024, 256), bf16),
                pltpu.SMEM((4 * width,), jnp.int32),
                pltpu.SMEM((4 * width,), jnp.int32),
                pltpu.SemaphoreType.DMA((2,)),
                *[pltpu.VMEM((LANES, LANES), f32)] * 4,
            ],
        ),
        out_shape=[
            shape(fields.shape, f32),
            shape(residue.shape, f32),
            shape((144, samples), f32),
        ],
        compiler_params=pltpu.CompilerParams(vmem_limit_bytes=48 << 20),
        name="section",
    )(
        live_counts,
        in_hbm(faces.reshape(-1)),
        normals,
        fields,
        fields,
        residue,
        geometry,
        normals,
        face_scale,
        neighbours,
        elems,
        const["table_select"],
        const["twice_select"],
        const["from_p"],
        const["lift"],
    )

    below, above, partial = lax.optimization_barrier((below, above, partial))
    to_left, to_right = pl.pallas_call(
        relay_kernel,
        out_shape=[pltpu.VMEM(piece, f32), pltpu.VMEM(piece, f32)],
        name="relay",
    )(in_vmem(left), in_vmem(right), in_vmem(below), in_vmem(above))
    forward, backward = steps_along("py")
    from_right = lax.ppermute(to_left, "py", backward)
    from_left = lax.ppermute(to_right, "py", forward)

    def head(rank):
        return lambda t: (0,) * rank

    fields_next, residue_next, spread = pl.pallas_call(
        functools.partial(boundary_kernel, slot_faces, const["powers"], samples),
        grid=(1,),
        in_specs=[
            pl.BlockSpec((NODES, 4, reach), head(3)),
            pl.BlockSpec((NODES, 4, reach), head(3)),
            pl.BlockSpec((3, 4, reach), head(3)),
            pl.BlockSpec((4, reach), head(2)),
            pl.BlockSpec((4, reach), head(2)),
            fixed(piece),
            fixed(piece),
            fixed(piece),
            fixed(piece),
            fixed((1, samples)),
            fixed((1, samples)),
            fixed((3, samples)),
            fixed((144, samples)),
            fixed((ROWS, 1024)),
            fixed((PAD, PAD)),
        ],
        out_specs=[
            pl.BlockSpec((NODES, 4, reach), head(3)),
            pl.BlockSpec((NODES, 4, reach), head(3)),
            fixed((devices, 1, samples)),
        ],
        out_shape=[
            shape(fields.shape, f32),
            shape(residue.shape, f32),
            shape((devices, 1, samples), f32),
        ],
        scratch_shapes=[
            pltpu.VMEM((64, reach), f32),
            pltpu.VMEM((768, reach), bf16),
            pltpu.VMEM((ROWS, reach), f32),
            pltpu.VMEM((48, reach), f32),
            pltpu.VMEM((PAD, samples), f32),
        ],
        input_output_aliases={0: 0, 1: 1},
        compiler_params=pltpu.CompilerParams(vmem_limit_bytes=24 << 20),
        name="boundary",
    )(
        in_hbm(fields_next),
        in_hbm(residue_next),
        normals,
        face_scale,
        neighbours,
        from_right,
        from_left,
        below,
        above,
        elems,
        in_hbm(sample_ids.reshape(1, samples)),
        sample_coords,
        partial,
        const["lift"],
        const["inverse"],
    )
    received = lax.all_to_all(spread, ("px", "py"), 0, 0, tiled=True)

    receivers = samples // QPTS
    harmonic = np.tile(harmonic_table(), (1, receivers)).astype(np.float32)
    groups = (np.arange(samples)[None] // QPTS == np.arange(receivers)[:, None]).astype(np.float32)
    coefficients = pl.pallas_call(
        harmonic_kernel,
        out_shape=shape((receivers, harmonic.shape[0]), f32),
        name="harmonic",
    )(received, jnp.asarray(harmonic), jnp.asarray(groups))
    return (
        jnp.transpose(fields_next, (1, 0, 2)),
        jnp.transpose(residue_next, (1, 0, 2)),
        coefficients.T,
    )


def solution(mesh):
    placed = (
        P(None, None, ("px", "py")),
        P(None, None, ("px", "py")),
        P(None, ("px", "py")),
        P(None, None, ("px", "py")),
        P(None, ("px", "py")),
        P(None, ("px", "py")),
        P(None, ("px", "py")),
        P(("px", "py")),
        P(("px", "py")),
        P(("px", "py")),
        P(None, ("px", "py")),
    )
    return jax.shard_map(
        local,
        mesh=mesh,
        in_specs=placed,
        out_specs=(P(None, None, ("px", "py")), P(None, None, ("px", "py")), P(None, ("px", "py"))),
        check_vma=False,
    )
```

```python
import functools
import math

import jax
import jax.numpy as jnp
import numpy as np
from jax import lax
from jax.experimental import pallas as pl
from jax.experimental.pallas import tpu as pltpu
from jax.sharding import PartitionSpec as P

QPTS = 50
NODES = 35
PAD = 40
FACE_ROWS = 16
ROWS = 144
LANES = 128
FACE_TILES = 4


highest = lax.Precision.HIGHEST
section_decay = -567301805773.0 / 1357537059087.0
section_gain = 5161836677717.0 / 13612068292357.0
time_step = 0.01
f32 = jnp.float32
bf16 = jnp.bfloat16


def exponent_table():
    listing = []
    for degree in range(5):
        for third in range(degree + 1):
            for second in range(degree + 1 - third):
                listing.append((degree - second - third, second, third))
    return np.array(listing)


def factorials(values):
    lookup = np.array([float(math.factorial(level)) for level in range(24)])
    return lookup[values]


def eliminate(matrix, right_hand):
    order_size = matrix.shape[0]
    work = np.concatenate([matrix, right_hand], axis=1).astype(float)
    for pivot_col in range(order_size):
        best = max(range(pivot_col, order_size), key=lambda row_id: abs(work[row_id, pivot_col]))
        work[[pivot_col, best]] = work[[best, pivot_col]]
        work[pivot_col] = work[pivot_col] / work[pivot_col, pivot_col]
        for row_id in range(order_size):
            if row_id != pivot_col:
                work[row_id] = work[row_id] - work[row_id, pivot_col] * work[pivot_col]
    return work[:, order_size:]


def element_tables():
    powers = exponent_table()
    points = powers / 4.0
    vander = np.prod(points[:, None, :] ** powers[None, :, :], axis=2)
    inverse = eliminate(vander, np.eye(35))
    derivs = []
    for axis_id in range(3):
        lowered = np.maximum(powers - (np.arange(3) == axis_id)[None, :], 0)
        slope_table = powers[None, :, axis_id] * np.prod(
            points[:, None, :] ** lowered[None, :, :], axis=2
        )
        derivs.append(slope_table @ inverse)
    summed = powers[:, None, :] + powers[None, :, :]
    exp_r = summed[..., 0]
    exp_s = summed[..., 1]
    exp_t = summed[..., 2]
    volume = (
        factorials(exp_r)
        * factorials(exp_s)
        * factorials(exp_t)
        / factorials(exp_r + exp_s + exp_t + 3)
    )
    mass_matrix = inverse.T @ volume @ inverse
    face_grams = [
        np.where(
            exp_t == 0, factorials(exp_r) * factorials(exp_s) / factorials(exp_r + exp_s + 2), 0.0
        ),
        np.where(
            exp_s == 0, factorials(exp_r) * factorials(exp_t) / factorials(exp_r + exp_t + 2), 0.0
        ),
        factorials(exp_r)
        * factorials(exp_s)
        * factorials(exp_t)
        / factorials(exp_r + exp_s + exp_t + 2),
        np.where(
            exp_r == 0, factorials(exp_s) * factorials(exp_t) / factorials(exp_s + exp_t + 2), 0.0
        ),
    ]
    listed = [tuple((int(entry) for entry in powers[node_id])) for node_id in range(35)]
    face_nodes = np.array(
        [
            [node_id for node_id in range(35) if listed[node_id][2] == 0],
            [node_id for node_id in range(35) if listed[node_id][1] == 0],
            [node_id for node_id in range(35) if sum(listed[node_id]) == 4],
            [node_id for node_id in range(35) if listed[node_id][0] == 0],
        ]
    )
    surface = np.zeros((35, 60))
    for face_id in range(4):
        face_mass = inverse.T @ face_grams[face_id] @ inverse
        for node_id in range(15):
            surface[:, 4 * node_id + face_id] = face_mass[:, face_nodes[face_id, node_id]]
    lifting = eliminate(mass_matrix, surface)
    return (np.stack(derivs), lifting, face_nodes, inverse, powers)


def associated(degree, order, cosine, sine):
    current = cosine * 0.0 + 1.0
    for step_id in range(1, order + 1):
        current = -(2 * step_id - 1) * sine * current
    if degree == order:
        return current
    following = cosine * (2 * order + 1) * current
    for level in range(order + 2, degree + 1):
        current, following = (
            following,
            ((2 * level - 1) * cosine * following - (level + order - 1) * current)
            / (level - order),
        )
    return following


def harmonic_table():
    inner_node = math.sqrt(5.0 - 2.0 * math.sqrt(10.0 / 7.0)) / 3.0
    outer_node = math.sqrt(5.0 + 2.0 * math.sqrt(10.0 / 7.0)) / 3.0
    inner_weight = (322.0 + 13.0 * math.sqrt(70.0)) / 900.0
    outer_weight = (322.0 - 13.0 * math.sqrt(70.0)) / 900.0
    cosines = np.array([-outer_node, -inner_node, 0.0, inner_node, outer_node])
    weights = np.array([outer_weight, inner_weight, 128.0 / 225.0, inner_weight, outer_weight])
    azimuth = 2.0 * np.pi * (np.arange(10) + 0.5) / 10.0
    polar = np.repeat(cosines, 10)
    circle = np.tile(azimuth, 5)
    point_weight = np.repeat(weights, 10) * 2.0 * np.pi / 10.0
    sine = np.sqrt(1.0 - polar**2)
    table_rows = []
    for degree in range(5):
        for order in range(-degree, degree + 1):
            absolute = abs(order)
            legendre = associated(degree, absolute, polar, sine)
            factor = math.sqrt(
                (2 * degree + 1)
                / (4.0 * math.pi)
                * math.factorial(degree - absolute)
                / math.factorial(degree + absolute)
            )
            if order > 0:
                angular = math.sqrt(2.0) * np.cos(order * circle)
            elif order < 0:
                angular = math.sqrt(2.0) * np.sin(absolute * circle)
            else:
                angular = circle * 0.0 + 1.0
            table_rows.append(factor * legendre * angular * point_weight)
    return np.array(table_rows)


def constant_tables():
    derivs, lifting, face_nodes, inverse, powers = element_tables()
    table_select = np.zeros((ROWS, 4 * LANES), np.float32)
    trace_select = np.zeros((4 * 4 * FACE_ROWS, ROWS), np.float32)
    for face in range(4):
        for field in range(4):
            for place in range(15):
                source = 4 * face_nodes[face, place] + field
                column = FACE_ROWS * field + place
                table_select[source, LANES * face + column] = 1.0
                table_select[source, LANES * face + 64 + column] = 1.0
                trace_select[64 * face + column, source] = 1.0
    whole = np.round(3.0 * derivs)
    into_p = np.zeros((ROWS, 128), np.float32)
    from_p = np.zeros((3 * ROWS, 48), np.float32)
    lift = np.zeros((ROWS, 256), np.float32)
    for node in range(NODES):
        for axis_id in range(3):
            into_p[4 * node, PAD * axis_id : PAD * axis_id + NODES] = -whole[axis_id, node]
            for field in range(1, 4):
                from_p[ROWS * axis_id + 4 * node + field, :NODES] = whole[axis_id, node]
        for face in range(4):
            for place in range(15):
                entry = lifting[node, 4 * place + face]
                column = FACE_ROWS * face + place
                lift[4 * node, column] = entry
                for field in range(1, 4):
                    lift[4 * node + field, 64 * field + column] = -entry
    lift_hi = lift.astype(jnp.bfloat16)
    lift_lo = (lift - lift_hi.astype(np.float32)).astype(jnp.bfloat16)
    return {
        "table_select": jnp.asarray(np.concatenate([table_select] * 2, axis=0), bf16),
        "trace_select": jnp.asarray(trace_select, bf16),
        "twice_select": jnp.asarray(np.concatenate([trace_select] * 2, axis=1), bf16),
        "from_p": jnp.asarray(np.concatenate([from_p, from_p], axis=1), bf16),
        "lift": jnp.asarray(
            np.concatenate(
                [lift_hi, lift_lo, lift_hi] + [into_p.astype(jnp.bfloat16)] * 2, axis=1
            )
        ),
        "inverse": jnp.asarray(np.pad(inverse.T, ((0, 5), (0, 5))), f32),
        "powers": powers,
    }


def halves(values):
    high = values.astype(bf16)
    return high, (values - high.astype(f32)).astype(bf16)


def thirds(values):
    high = values.astype(bf16)
    rest = values - high.astype(f32)
    middle = rest.astype(bf16)
    return high, middle, (rest - middle.astype(f32)).astype(bf16)


def product(left, right, dims=((1,), (0,))):
    return lax.dot_general(left, right, (dims, ((), ())), preferred_element_type=f32)


def stack_nodes(fields_ref, stacked):
    tiles = range(stacked.shape[0])
    for tile in tiles:
        for node in range(NODES):
            stacked[tile, 4 * node : 4 * node + 4, :] = fields_ref[
                node, :, LANES * tile : LANES * tile + LANES
            ]
    return halves(jnp.concatenate([stacked[tile] for tile in tiles], axis=1))


def one_field(stacked, field):
    tiles = range(stacked.shape[0])
    rows = pl.ds(field, NODES, stride=4)
    return jnp.concatenate([stacked[tile, rows, :] for tile in tiles], axis=1)


def pack_kernel(
    slot_faces,
    fields_ref,
    codes_ref,
    select_ref,
    up_ref,
    down_ref,
    left_ref,
    right_ref,
    faces_ref,
    stacked,
):
    stacked[...] = jnp.zeros_like(stacked)
    high, low = stack_nodes(fields_ref, stacked)
    traces = product(select_ref[...], high) + product(select_ref[...], low)
    reach = fields_ref.shape[2]
    count = reach // 8
    chosen = jnp.zeros((64, reach), f32)
    for face in range(4):
        remote = codes_ref[face : face + 1, 0:reach] >= slot_faces
        chosen = jnp.where(remote, traces[64 * face : 64 * face + 64, :], chosen)
    homes = [up_ref.at[0], up_ref.at[1], up_ref.at[2], left_ref, right_ref]
    homes += [down_ref.at[0], down_ref.at[1], down_ref.at[2]]
    for heading, home in enumerate(homes):
        part = chosen[:, count * heading : count * heading + count]
        home[:, 0:96] = part[0:48]
        for third in range(3):
            home[16 * third : 16 * third + 16, 96:128] = part[48:64, 32 * third : 32 * third + 32]
    tiles = codes_ref.shape[1] // LANES
    codes = codes_ref[...]
    codes = jnp.where((codes >= 0) & (codes < slot_faces), codes, 0)
    for face in range(4):
        for tile in range(tiles):
            row = 4 * FACE_TILES * (tile // FACE_TILES) + FACE_TILES * face + tile % FACE_TILES
            faces_ref[row : row + 1, :] = codes[
                face : face + 1, LANES * tile : LANES * tile + LANES
            ]


def relay_kernel(left_ref, right_ref, below_ref, above_ref, to_left_ref, to_right_ref):
    to_left_ref[0] = left_ref[...]
    to_left_ref[1] = below_ref[0]
    to_left_ref[2] = above_ref[0]
    to_right_ref[0] = right_ref[...]
    to_right_ref[1] = below_ref[2]
    to_right_ref[2] = above_ref[2]


def build_rows(first, part, fields_ref, select_ref, table_ref, stacked):
    slot_count = table_ref.shape[0] // 4
    width = LANES * stacked.shape[0]
    high, low = stack_nodes(fields_ref.at[:, :, width * part : width * part + width], stacked)
    both = jnp.concatenate([high, low], axis=0)
    for half in range(2):
        select = select_ref[:, 256 * half : 256 * half + 256]
        rows = product(both, select, ((0,), (0,)))
        for side in range(2):
            start = pl.multiple_of((2 * half + side) * slot_count + first + width * part, width)
            table_ref[pl.ds(start, width), :] = rows[:, LANES * side : LANES * side + LANES]


def gather_pieces(faces_ref, table_ref, normals_ref, outer_ref, rows_refs):
    width = outer_ref.shape[1]
    left_half = lax.broadcasted_iota(jnp.int32, (1, LANES), 1) < 64

    def load(tile, rows):
        for row in rows:
            at = tile * LANES + row
            for half in range(2):
                one = table_ref[pl.ds(faces_ref[2 * half * width + at], 1), :]
                two = table_ref[pl.ds(faces_ref[(2 * half + 1) * width + at], 1), :]
                rows_ref = rows_refs[2 * (tile % 2) + half]
                rows_ref[row : row + 1, :] = jnp.where(left_half, one, two)

    def combine(tile, half):
        turned = rows_refs[2 * (tile % 2) + half][...].T
        lanes = slice(tile * LANES, tile * LANES + LANES)
        for side in range(2):
            face = 2 * half + side
            part = turned[64 * side : 64 * side + 64, :]
            total = -part[0:16]
            for axis_id in range(3):
                facing = normals_ref[axis_id, face : face + 1, lanes]
                total = total + facing * part[16 + 16 * axis_id : 32 + 16 * axis_id]
            outer_ref[FACE_ROWS * face : FACE_ROWS * face + FACE_ROWS, lanes] = total

    for tile in range(width // LANES):
        for part in range(8):
            rows = range(16 * part, 16 * part + 16)
            yield functools.partial(load, tile, rows)
            if tile > 0 and part < 2:
                yield functools.partial(combine, tile - 1, part)
    for half in range(2):
        yield functools.partial(combine, tile, half)


def section_kernel(
    slot_count,
    reach,
    live_ref,
    faces_hbm,
    next_normals_ref,
    bulk_ref,
    fields_ref,
    residue_ref,
    geometry_ref,
    normals_ref,
    scale_ref,
    codes_ref,
    elems_ref,
    table_select_ref,
    select_ref,
    from_ref,
    lift_ref,
    fields_out,
    residue_out,
    sampled,
    table_ref,
    stacked,
    combined,
    slow,
    rates,
    outer,
    beyond_ref,
    pressure,
    fields_split,
    slow_split,
    inner,
    sources,
    even_faces,
    odd_faces,
    arrived,
    *rows_refs,
):
    faces_refs = (even_faces, odd_faces)
    width = fields_ref.shape[2]
    tiles = slot_count // width
    bulks = slot_count // bulk_ref.shape[2]
    step = pl.program_id(0) - bulks
    slot_faces = 4 * slot_count
    half_width = 256

    def codes_copy(tile, parity):
        source = faces_hbm.at[pl.ds(pl.multiple_of(tile * 4 * width, 4 * width), 4 * width)]
        return pltpu.make_async_copy(source, faces_refs[parity], arrived.at[parity])

    def gather(parity):
        return gather_pieces(
            faces_refs[parity], table_ref, next_normals_ref, outer, rows_refs
        )

    def take_codes(parity):
        codes_copy(step, parity).wait()

        @pl.when((step + 1) * width < live_ref[0])
        def _():
            codes_copy(step + 1, 1 - parity).start()

    def update_pieces():
        first = (step - 1) * width

        def stack(at, low, high):
            for tile in range(2 * at, 2 * at + 2):
                for node in range(low, high):
                    stacked[tile, 4 * node : 4 * node + 4, :] = fields_ref[
                        node, :, LANES * tile : LANES * tile + LANES
                    ]

        def split(at):
            for side in range(2):
                lanes = slice(LANES * side, LANES * side + LANES)
                high, low = halves(stacked[2 * at + side])
                fields_split[at, 0:ROWS, lanes] = high
                fields_split[at, ROWS : 2 * ROWS, lanes] = low

        def inside(at):
            return slice(half_width * at, half_width * at + half_width)

        def field_rows(at, field):
            rows = pl.ds(field, NODES, stride=4)
            return jnp.concatenate([stacked[tile, rows, :] for tile in (2 * at, 2 * at + 1)], axis=1)

        def copy_slow(at):
            lanes = inside(at)
            slow[0:NODES, lanes] = field_rows(at, 0)
            slow_split[at, 0:48, :], slow_split[at, 48:96, :] = halves(slow[:, lanes])

        def weigh(at, axis_id):
            lanes = inside(at)
            weighted = jnp.zeros((NODES, half_width), f32)
            for direction in range(3):
                row = 3 * axis_id + direction
                factor = geometry_ref[row : row + 1, lanes] * (1.0 / 3.0)
                weighted = weighted + factor * field_rows(at, 1 + direction)
            combined[PAD * axis_id : PAD * axis_id + NODES, lanes] = weighted

        def split_weighted(at):
            high, low = halves(combined[:, inside(at)])
            sources[at, 768:896, :], sources[at, 896:1024, :] = high, low

        def traces(at):
            inner[at] = product(select_ref[...], fields_split[at])

        def slope(at, axis_id):
            lanes = inside(at)
            place = lax.broadcasted_iota(jnp.int32, (8, half_width), 0) & 3
            value = product(from_ref[ROWS * axis_id : ROWS * axis_id + ROWS, :], slow_split[at])
            pattern = jnp.zeros((8, half_width), f32)
            for direction in range(3):
                row = 3 * axis_id + direction
                factor = geometry_ref[row : row + 1, lanes] * (1.0 / 3.0)
                pattern = jnp.where(place == direction + 1, factor, pattern)
            value = value.reshape(ROWS // 8, 8, half_width) * pattern[None]
            value = value.reshape(ROWS, half_width)
            if axis_id == 0:
                rates[:, lanes] = value
            else:
                rates[:, lanes] += value

        def keep_split(at, start, value):
            high, low = halves(value)
            rows = value.shape[0]
            sources[at, start : start + rows, :] = high
            sources[at, 256 + start : 256 + start + rows, :] = high
            sources[at, 512 + start : 512 + start + rows, :] = low

        def jump(at, face):
            lanes = inside(at)
            inner_p = inner[at, 64 * face : 64 * face + 16, :]
            along = jnp.zeros_like(inner_p)
            for axis_id in range(3):
                facing = normals_ref[axis_id, face : face + 1, lanes]
                start = 64 * face + 16 + 16 * axis_id
                along = along + facing * inner[at, start : start + 16, :]
            wall = codes_ref[face : face + 1, lanes] < 0
            beyond = beyond_ref[FACE_ROWS * face : FACE_ROWS * face + FACE_ROWS, lanes]
            beyond = jnp.where(wall, -along - inner_p, beyond)
            beyond = jnp.where(codes_ref[face : face + 1, lanes] >= slot_faces, 0.0, beyond)
            scale = 0.5 * scale_ref[face : face + 1, lanes]
            value = scale * (along - inner_p - beyond)
            keep_split(at, FACE_ROWS * face, value)
            for axis_id in range(3):
                start = 64 + 64 * axis_id + FACE_ROWS * face
                keep_split(at, start, normals_ref[axis_id, face : face + 1, lanes] * value)

        def lift(at):
            lanes = inside(at)
            rates[:, lanes] = product(lift_ref[...], sources[at]) - rates[:, lanes]

        def advance(at, low, high):
            lanes = inside(at)
            slots = lax.broadcasted_iota(jnp.int32, (1, half_width), 1) + (first + half_width * at)
            keep = slots < live_ref[0]
            for node in range(low, high):
                rate = rates[4 * node : 4 * node + 4, lanes]
                residue_next = section_decay * residue_ref[node, :, lanes] + time_step * rate
                fields_next = fields_ref[node, :, lanes] + section_gain * residue_next
                fields_next = jnp.where(keep, fields_next, 0.0)
                fields_out[node, :, lanes] = fields_next
                residue_out[node, :, lanes] = jnp.where(keep, residue_next, 0.0)
                pressure[node : node + 1, lanes] = fields_next[0:1]

        def sample(at):
            lanes = inside(at)
            parts = jnp.concatenate(thirds(pressure[:, lanes]), axis=0)
            start = first + half_width * at
            slots = lax.broadcasted_iota(jnp.int32, (half_width, elems_ref.shape[1]), 0) + start
            elems = elems_ref[...]
            picks = (slots == elems) & (elems >= reach)
            sampled[...] += product(parts, jnp.where(picks, 1.0, 0.0).astype(bf16))

        call = functools.partial

        def stages(at):
            sevens = range(0, NODES, 7)
            return [
                [call(stack, at, low, low + 7) for low in sevens] + [call(split, at)],
                [call(copy_slow, at)]
                + [call(weigh, at, axis_id) for axis_id in range(3)]
                + [call(split_weighted, at), call(traces, at)],
                [call(slope, at, axis_id) for axis_id in range(3)],
                [call(jump, at, face) for face in range(4)],
                [call(lift, at)],
                [call(advance, at, low, low + 7) for low in sevens],
                [call(sample, at)],
            ]

        both = [stages(at) for at in range(width // half_width)]
        depth = len(both[0])
        return [
            [piece for lag, chain in enumerate(both) if 0 <= at - lag < depth for piece in chain[at - lag]]
            for at in range(depth + len(both) - 1)
        ]

    def interleave(gathers, groups):
        gathers = list(gathers)

        def run(at, updates, groups):
            @pl.when(live_ref[0] > at)
            def _():
                low = at * len(gathers) // len(groups)
                loads = gathers[low : (at + 1) * len(gathers) // len(groups)]
                order = [(place / len(loads), 0, place) for place in range(len(loads))]
                order += [((place + 1) / len(updates), 1, place) for place in range(len(updates))]
                for _, kind, place in sorted(order):
                    (loads, updates)[kind][place]()

        cuts = (0, 4, 8)
        groups = [sum(groups[low:high], []) for low, high in zip(cuts, cuts[1:])]
        for at, updates in enumerate(groups):
            run(at, updates, groups)

    @pl.when(step == -bulks)
    def _():
        stacked[...] = jnp.zeros_like(stacked)
        combined[...] = jnp.zeros_like(combined)
        slow[...] = jnp.zeros_like(slow)
        pressure[...] = jnp.zeros_like(pressure)
        sampled[...] = jnp.zeros_like(sampled)

    @pl.when(step < 0)
    def _():
        first = (step + bulks) * bulk_ref.shape[2]
        for part in range(bulk_ref.shape[2] // width):

            @pl.when(first + width * part < live_ref[0])
            def _():
                build_rows(first, part, bulk_ref, table_select_ref, table_ref, stacked)

    @pl.when(step == -1)
    def _():
        codes_copy(0, 0).start()

    @pl.when(step == 0)
    def _():
        take_codes(0)
        for piece in gather(0):
            piece()

    for parity in range(2):

        @pl.when((step > 0) & (step * width < live_ref[0]) & (step % 2 == parity))
        def _():
            take_codes(parity)
            beyond_ref[...] = outer[...]
            interleave(gather(parity), update_pieces())

    @pl.when((step > 0) & ((step - 1) * width >= live_ref[0]))
    def _():
        fields_out[...] = jnp.zeros_like(fields_out)
        residue_out[...] = jnp.zeros_like(residue_out)

    @pl.when((step > 0) & ((step - 1) * width < live_ref[0]) & (step * width >= live_ref[0]))
    def _():
        beyond_ref[...] = outer[...]
        for stage in update_pieces():
            for piece in stage:
                piece()


def boundary_kernel(
    slot_faces,
    powers,
    group,
    fields_ref,
    residue_ref,
    normals_ref,
    scale_ref,
    codes_ref,
    right_ref,
    left_ref,
    below_ref,
    above_ref,
    elems_ref,
    ids_ref,
    coords_ref,
    partial_ref,
    lift_ref,
    inverse_ref,
    fields_out,
    residue_out,
    spread_ref,
    remote,
    sources,
    rates,
    pressure,
    monomials,
):
    reach = fields_ref.shape[2]
    bound_count = reach // 8
    pressure[...] = jnp.zeros_like(pressure)
    monomials[...] = jnp.zeros_like(monomials)
    arrivals = [
        left_ref[2],
        above_ref[1],
        right_ref[2],
        left_ref[0],
        right_ref[0],
        left_ref[1],
        below_ref[1],
        right_ref[1],
    ]
    for heading, source in enumerate(arrivals):
        start = bound_count * heading
        remote[0:48, start : start + 96] = source[:, 0:96]
        for third in range(3):
            place = start + 32 * third
            remote[48:64, place : place + 32] = source[16 * third : 16 * third + 16, 96:128]

    def keep_split(start, value):
        high, low = halves(value)
        sources[start : start + FACE_ROWS, :] = high
        sources[256 + start : 256 + start + FACE_ROWS, :] = high
        sources[512 + start : 512 + start + FACE_ROWS, :] = low

    for face in range(4):
        beyond = -remote[0:16, :]
        for axis_id in range(3):
            facing = normals_ref[axis_id, face : face + 1, :]
            beyond = beyond + facing * remote[16 + 16 * axis_id : 32 + 16 * axis_id, :]
        is_remote = codes_ref[face : face + 1, :] >= slot_faces
        flux = jnp.where(is_remote, -0.5 * scale_ref[face : face + 1, :] * beyond, 0.0)
        keep_split(FACE_ROWS * face, flux)
        for axis_id in range(3):
            facing = normals_ref[axis_id, face : face + 1, :]
            keep_split(64 + 64 * axis_id + FACE_ROWS * face, facing * flux)
    rates[...] = time_step * product(lift_ref[:, 0:768], sources[...])
    for node in range(NODES):
        rate = rates[4 * node : 4 * node + 4, :]
        residue_out[node] = residue_ref[node] + rate
        fields_next = fields_ref[node] + section_gain * rate
        fields_out[node] = fields_next
        pressure[node : node + 1, :] = fields_next[0:1]
    parts = jnp.concatenate(thirds(pressure[...]), axis=0)
    slots = lax.broadcasted_iota(jnp.int32, (reach, elems_ref.shape[1]), 0)
    picks = jnp.where(slots == elems_ref[...], 1.0, 0.0).astype(bf16)
    sampled = partial_ref[...] + product(parts, picks)
    ladders = []
    for axis_id in range(3):
        base = coords_ref[axis_id : axis_id + 1, :]
        square = base * base
        ladders.append([jnp.ones_like(base), base, square, square * base, square * square])
    for node in range(NODES):
        exps = [int(entry) for entry in powers[node]]
        monomials[node : node + 1, :] = (
            ladders[0][exps[0]] * ladders[1][exps[1]] * ladders[2][exps[2]]
        )
    basis = jnp.dot(
        inverse_ref[...], monomials[...], precision=highest, preferred_element_type=f32
    )
    gathered = sampled[0:PAD, :] + sampled[48 : 48 + PAD, :] + sampled[96 : 96 + PAD, :]
    values = jnp.sum(basis * gathered, axis=0, keepdims=True)
    ids = ids_ref[...]
    owner = lax.shift_right_logical(ids * 5243, 20)
    place = ids - group * owner
    owners = lax.broadcasted_iota(jnp.int32, (spread_ref.shape[0], ids.shape[1]), 0)
    held = jnp.where(owners == owner, values, 0.0)
    places = lax.broadcasted_iota(jnp.int32, (spread_ref.shape[2], ids.shape[1]), 0)
    chosen = jnp.where(places == place, 1.0, 0.0).astype(bf16)
    spread = jnp.zeros((spread_ref.shape[0], spread_ref.shape[2]), f32)
    for part in thirds(held):
        spread = spread + product(part, chosen, ((1,), (1,)))
    spread_ref[:, 0, :] = spread


def harmonic_kernel(received_ref, table_ref, groups_ref, out_ref):
    mine = jnp.sum(received_ref[...], axis=0)
    weighted = groups_ref[...] * mine
    out_ref[...] = lax.dot_general(
        weighted,
        table_ref[...],
        (((1,), (1,)), ((), ())),
        precision=highest,
        preferred_element_type=f32,
    )


def in_hbm(array):
    return pltpu.with_memory_space_constraint(array, pltpu.HBM)


def in_vmem(array):
    return pltpu.with_memory_space_constraint(array, pltpu.VMEM)


def fixed(shape):
    return pl.BlockSpec(shape, lambda *_: (0,) * len(shape))


def local(
    fields,
    residue,
    geometry,
    normals,
    face_scale,
    neighbours,
    send_faces,
    live_counts,
    sample_ids,
    sample_elems,
    sample_coords,
):
    const = {
        name: in_hbm(table) if isinstance(table, jax.Array) else table
        for name, table in constant_tables().items()
    }
    fields = in_hbm(jnp.transpose(fields, (1, 0, 2)))
    residue = in_hbm(jnp.transpose(residue, (1, 0, 2)))
    geometry, normals, face_scale = in_hbm(geometry), in_hbm(normals), in_hbm(face_scale)
    neighbours, sample_coords = in_hbm(neighbours), in_hbm(sample_coords)
    slot_count = fields.shape[2]
    slot_faces = 4 * slot_count
    bound_count = send_faces.shape[1]
    reach = 8 * bound_count
    samples = sample_ids.shape[0]
    devices = lax.axis_size(("px", "py"))
    shape = jax.ShapeDtypeStruct

    elems = in_hbm(sample_elems.reshape(1, samples))
    width = LANES * FACE_TILES
    tiles = slot_count // width
    piece = (3, 48, LANES)

    up, down, left, right, faces = pl.pallas_call(
        functools.partial(pack_kernel, slot_faces),
        grid=(1,),
        in_specs=[
            pl.BlockSpec((NODES, 4, reach), lambda t: (0, 0, 0)),
            fixed((4, slot_count)),
            fixed((256, ROWS)),
        ],
        out_specs=[
            fixed(piece),
            fixed(piece),
            fixed(piece[1:]),
            fixed(piece[1:]),
            fixed((slot_faces // LANES, LANES)),
        ],
        out_shape=[
            pltpu.VMEM(piece, f32),
            pltpu.VMEM(piece, f32),
            shape(piece[1:], f32),
            shape(piece[1:], f32),
            pltpu.HBM((slot_faces // LANES, LANES), jnp.int32),
        ],
        scratch_shapes=[pltpu.VMEM((reach // LANES, ROWS, LANES), f32)],
        compiler_params=pltpu.CompilerParams(vmem_limit_bytes=16 << 20),
        name="pack",
    )(fields, neighbours, const["trace_select"])

    def steps_along(axis):
        count = lax.axis_size(axis)
        forward = [(i, i + 1) for i in range(count - 1)]
        return forward, [(target, source) for source, target in forward]

    forward, backward = steps_along("px")
    below = lax.ppermute(up, "px", backward)
    above = lax.ppermute(down, "px", forward)
    bulk = 3 * width
    bulks = slot_count // bulk

    def behind(rank):
        return lambda t, *_: (0,) * rank + (jnp.maximum(t - bulks - 1, 0),)

    def ahead(rank):
        return lambda t, *_: (0,) * rank + (jnp.clip(t - bulks, 0, tiles - 1),)

    fields_next, residue_next, partial = pl.pallas_call(
        functools.partial(section_kernel, slot_count, reach),
        grid_spec=pltpu.PrefetchScalarGridSpec(
            num_scalar_prefetch=1,
            grid=(bulks + tiles + 1,),
            in_specs=[
                pl.BlockSpec(memory_space=pltpu.HBM),
                pl.BlockSpec((3, 4, width), ahead(2)),
                pl.BlockSpec((NODES, 4, bulk), lambda t, *_: (0, 0, jnp.minimum(t, bulks - 1))),
                pl.BlockSpec((NODES, 4, width), behind(2)),
                pl.BlockSpec((NODES, 4, width), behind(2)),
                pl.BlockSpec((9, width), behind(1)),
                pl.BlockSpec((3, 4, width), behind(2)),
                pl.BlockSpec((4, width), behind(1)),
                pl.BlockSpec((4, width), behind(1)),
                fixed((1, samples)),
                fixed((2 * ROWS, 4 * LANES)),
                fixed((256, 2 * ROWS)),
                fixed((3 * ROWS, 96)),
                fixed((ROWS, 1024)),
            ],
            out_specs=[
                pl.BlockSpec((NODES, 4, width), behind(2)),
                pl.BlockSpec((NODES, 4, width), behind(2)),
                fixed((144, samples)),
            ],
            scratch_shapes=[
                pltpu.VMEM((slot_faces, LANES), f32),
                pltpu.VMEM((width // LANES, ROWS, LANES), f32),
                pltpu.VMEM((128, width), f32),
                pltpu.VMEM((48, width), f32),
                pltpu.VMEM((ROWS, width), f32),
                pltpu.VMEM((64, width), f32),
                pltpu.VMEM((64, width), f32),
                pltpu.VMEM((48, width), f32),
                pltpu.VMEM((width // 256, 2 * ROWS, 256), bf16),
                pltpu.VMEM((width // 256, 96, 256), bf16),
                pltpu.VMEM((width // 256, 256, 256), f32),
                pltpu.VMEM((width // 256, 1024, 256), bf16),
                pltpu.SMEM((4 * width,), jnp.int32),
                pltpu.SMEM((4 * width,), jnp.int32),
                pltpu.SemaphoreType.DMA((2,)),
                *[pltpu.VMEM((LANES, LANES), f32)] * 4,
            ],
        ),
        out_shape=[
            shape(fields.shape, f32),
            shape(residue.shape, f32),
            shape((144, samples), f32),
        ],
        compiler_params=pltpu.CompilerParams(vmem_limit_bytes=48 << 20),
        name="section",
    )(
        live_counts,
        in_hbm(faces.reshape(-1)),
        normals,
        fields,
        fields,
        residue,
        geometry,
        normals,
        face_scale,
        neighbours,
        elems,
        const["table_select"],
        const["twice_select"],
        const["from_p"],
        const["lift"],
    )

    below, above, partial = lax.optimization_barrier((below, above, partial))
    to_left, to_right = pl.pallas_call(
        relay_kernel,
        out_shape=[pltpu.VMEM(piece, f32), pltpu.VMEM(piece, f32)],
        name="relay",
    )(in_vmem(left), in_vmem(right), in_vmem(below), in_vmem(above))
    forward, backward = steps_along("py")
    from_right = lax.ppermute(to_left, "py", backward)
    from_left = lax.ppermute(to_right, "py", forward)

    def head(rank):
        return lambda t: (0,) * rank

    fields_next, residue_next, spread = pl.pallas_call(
        functools.partial(boundary_kernel, slot_faces, const["powers"], samples),
        grid=(1,),
        in_specs=[
            pl.BlockSpec((NODES, 4, reach), head(3)),
            pl.BlockSpec((NODES, 4, reach), head(3)),
            pl.BlockSpec((3, 4, reach), head(3)),
            pl.BlockSpec((4, reach), head(2)),
            pl.BlockSpec((4, reach), head(2)),
            fixed(piece),
            fixed(piece),
            fixed(piece),
            fixed(piece),
            fixed((1, samples)),
            fixed((1, samples)),
            fixed((3, samples)),
            fixed((144, samples)),
            fixed((ROWS, 1024)),
            fixed((PAD, PAD)),
        ],
        out_specs=[
            pl.BlockSpec((NODES, 4, reach), head(3)),
            pl.BlockSpec((NODES, 4, reach), head(3)),
            fixed((devices, 1, samples)),
        ],
        out_shape=[
            shape(fields.shape, f32),
            shape(residue.shape, f32),
            shape((devices, 1, samples), f32),
        ],
        scratch_shapes=[
            pltpu.VMEM((64, reach), f32),
            pltpu.VMEM((768, reach), bf16),
            pltpu.VMEM((ROWS, reach), f32),
            pltpu.VMEM((48, reach), f32),
            pltpu.VMEM((PAD, samples), f32),
        ],
        input_output_aliases={0: 0, 1: 1},
        compiler_params=pltpu.CompilerParams(vmem_limit_bytes=24 << 20),
        name="boundary",
    )(
        in_hbm(fields_next),
        in_hbm(residue_next),
        normals,
        face_scale,
        neighbours,
        from_right,
        from_left,
        below,
        above,
        elems,
        in_hbm(sample_ids.reshape(1, samples)),
        sample_coords,
        partial,
        const["lift"],
        const["inverse"],
    )
    received = lax.all_to_all(spread, ("px", "py"), 0, 0, tiled=True)

    receivers = samples // QPTS
    harmonic = np.tile(harmonic_table(), (1, receivers)).astype(np.float32)
    groups = (np.arange(samples)[None] // QPTS == np.arange(receivers)[:, None]).astype(np.float32)
    coefficients = pl.pallas_call(
        harmonic_kernel,
        out_shape=shape((receivers, harmonic.shape[0]), f32),
        name="harmonic",
    )(in_vmem(received), in_vmem(jnp.asarray(harmonic)), in_vmem(jnp.asarray(groups)))
    return (
        jnp.transpose(fields_next, (1, 0, 2)),
        jnp.transpose(residue_next, (1, 0, 2)),
        coefficients.T,
    )


def solution(mesh):
    placed = (
        P(None, None, ("px", "py")),
        P(None, None, ("px", "py")),
        P(None, ("px", "py")),
        P(None, None, ("px", "py")),
        P(None, ("px", "py")),
        P(None, ("px", "py")),
        P(None, ("px", "py")),
        P(("px", "py")),
        P(("px", "py")),
        P(("px", "py")),
        P(None, ("px", "py")),
    )
    return jax.shard_map(
        local,
        mesh=mesh,
        in_specs=placed,
        out_specs=(P(None, None, ("px", "py")), P(None, None, ("px", "py")), P(None, ("px", "py"))),
        check_vma=False,
    )
```
